32 devices in a mesh: band: 32 (over z, y, x, core).
Axes of the slice: x: 2, y: 2, z: 4, core: 2. Of those that a mesh axis runs over, the one named last changes fastest.
Arguments:
- tokens_in: bfloat16 [16384, 1024], P('band'), may hold values from -6 to 6
- prompt_states: bfloat16 [32, 128, 1024], P('band'), may hold values from -6 to 6
- image_ids: int32 [512], replicated, may hold values from 0 to 31, as said below
- text_lengths: int32 [32], replicated, may hold values from 8 to 128, as said below
- attn_gain: bfloat16 [1024], P('band'), may hold values from 0.5 to 1.5
- attn_shift: bfloat16 [1024], P('band'), may hold values from -1.75 to 1.75
- self_query: bfloat16 [1024, 1024], P('band'), may hold values from -0.1875 to 0.1875
- self_key: bfloat16 [1024, 1024], P('band'), may hold values from -0.1875 to 0.1875
- self_value: bfloat16 [1024, 1024], P('band'), may hold values from -0.1875 to 0.1875
- self_out: bfloat16 [1024, 1024], P('band'), may hold values from -0.75 to 0.75
- cross_gain: bfloat16 [1024], P('band'), may hold values from 0.5 to 1.5
- cross_shift: bfloat16 [1024], P('band'), may hold values from -1.75 to 1.75
- cross_query: bfloat16 [1024, 1024], P('band'), may hold values from -0.1875 to 0.1875
- cross_key: bfloat16 [1024, 1024], P('band'), may hold values from -0.1875 to 0.1875
- cross_value: bfloat16 [1024, 1024], P('band'), may hold values from -0.1875 to 0.1875
- cross_out: bfloat16 [1024, 1024], P('band'), may hold values from -0.5 to 0.5
- dense_gain: bfloat16 [1024], P('band'), may hold values from 0.5 to 1.5
- dense_shift: bfloat16 [1024], P('band'), may hold values from -1.75 to 1.75
- dense_in: bfloat16 [1024, 4096], P('band'), may hold values from -0.1875 to 0.1875
- dense_out: bfloat16 [4096, 1024], P('band'), may hold values from -0.09375 to 0.09375
- out_grad: bfloat16 [16384, 1024], P('band'), may hold values from -6 to 6
Outputs:
- block_out: bfloat16 [16384, 1024], P('band')
- grad_tokens: float32 [16384, 1024], P('band')
- grad_prompt: float32 [32, 128, 1024], P('band')
- grad_attn_gain: float32 [1024], P('band')
- grad_attn_shift: float32 [1024], P('band')
- grad_self_query: float32 [1024, 1024], P('band')
- grad_self_key: float32 [1024, 1024], P('band')
- grad_self_value: float32 [1024, 1024], P('band')
- grad_self_out: float32 [1024, 1024], P('band')
- grad_cross_gain: float32 [1024], P('band')
- grad_cross_shift: float32 [1024], P('band')
- grad_cross_query: float32 [1024, 1024], P('band')
- grad_cross_key: float32 [1024, 1024], P('band')
- grad_cross_value: float32 [1024, 1024], P('band')
- grad_cross_out: float32 [1024, 1024], P('band')
- grad_dense_gain: float32 [1024], P('band')
- grad_dense_shift: float32 [1024], P('band')
- grad_dense_in: float32 [1024, 4096], P('band')
- grad_dense_out: float32 [4096, 1024], P('band')
The draws below stay inside these ranges and needn't reach their ends.
Inputs may be any that keep to these rules, and one draw needn't show every extreme that they name: `image_ids`: image numbers never fall along the rows and each image is one run of rows; image 0 begins at row 0, and image i for i >= 1 begins at row 16 * i - 8 + e with 1 <= e < 8, e drawn for each image. `text_lengths`: image 0's prompt fills all 128 slots.
All inputs are finite; a program needn't handle non-finite values.
Results may differ from the reference program's by a relative error of at most 0.018.
Values may be sent and summed in bfloat16 or wider, within the bound.
A program may use at most 192 MiB of HBM per device.

```python
import jax
import jax.numpy as jnp
from jax import lax

D = 1024
HEADS = 16
HEAD = 64
FF = 4096
TEXT = 128
ROW_TOK = 32
ROWS_DEV = 16
IMAGES = 32
ROWS = 512
TOKENS = 16384


def draw_image_ids(key, part):
    half = ROWS_DEV // 2
    jitter = jax.random.randint(key, (IMAGES,), 1, half).astype(jnp.int32)
    starts = ROWS_DEV * jnp.arange(IMAGES, dtype=jnp.int32) - half + jitter
    place = jnp.arange(ROWS, dtype=jnp.int32)
    ids = jnp.sum((place[:, None] >= starts[None, 1:]).astype(jnp.int32), axis=1)
    return ids.astype(jnp.int32)


def draw_text_lengths(key, part):
    drawn = jax.random.randint(key, (IMAGES,), 8, TEXT + 1)
    return drawn.at[0].set(TEXT).astype(jnp.int32)


def steps_of(stream_key, shape, cuts, least, top_value):
    level, own = 1.0, jax.random.fold_in(stream_key, 6)
    for dim, blocks in cuts:
        steps = jnp.exp(jax.random.uniform(jax.random.fold_in(own, dim), (blocks,), jnp.float32, least / len(cuts), top_value / len(cuts)))
        level = level * jnp.repeat(steps, shape[dim] // blocks).reshape([-1 if axis == dim else 1 for axis in range(len(shape))])
    return level


def bell_draw(own_key, dims, scale, most, split=(), held_as=jnp.bfloat16):
    factor_of = steps_of(own_key, dims, split, -0.22, 0.18) if split else 1.0
    values = jax.random.normal(own_key, dims, jnp.float32) * scale * factor_of
    return jnp.minimum(jnp.maximum(values, -most), most).astype(held_as)


def setup_inputs(seed: int = 0) -> dict:
    key_of = jax.random.split(jax.random.key(seed), 22)
    tokens_in = bell_draw(key_of[0], (TOKENS, D), 1.0, 6.0, ((0, 32),))
    prompt_states = bell_draw(key_of[1], (IMAGES, TEXT, D), 1.0, 6.0, ((0, 32),))
    image_ids = draw_image_ids(jax.random.fold_in(key_of[21], 71), 0)
    text_lengths = draw_text_lengths(jax.random.fold_in(key_of[21], 71), 0)
    attn_gain = jnp.clip(1.0 + 0.1 * jax.random.normal(key_of[4], (D,), jnp.float32), 0.5, 1.5).astype(jnp.bfloat16)
    attn_shift = bell_draw(key_of[5], (D,), 0.3, 1.75, ((0, 32),))
    self_query = bell_draw(key_of[6], (D, D), D ** -0.5, 0.1875, ((0, 32),))
    self_key = bell_draw(key_of[7], (D, D), D ** -0.5, 0.1875, ((0, 32),))
    self_value = bell_draw(key_of[8], (D, D), D ** -0.5, 0.1875, ((0, 32),))
    self_out = bell_draw(key_of[9], (D, D), (D // 16) ** -0.5, 0.75, ((0, 32),))
    cross_gain = jnp.clip(1.0 + 0.1 * jax.random.normal(key_of[10], (D,), jnp.float32), 0.5, 1.5).astype(jnp.bfloat16)
    cross_shift = bell_draw(key_of[11], (D,), 0.3, 1.75, ((0, 32),))
    cross_query = bell_draw(key_of[12], (D, D), D ** -0.5, 0.1875, ((0, 32),))
    cross_key = bell_draw(key_of[13], (D, D), D ** -0.5, 0.1875, ((0, 32),))
    cross_value = bell_draw(key_of[14], (D, D), D ** -0.5, 0.1875, ((0, 32),))
    cross_out = bell_draw(key_of[15], (D, D), (D // 8) ** -0.5, 0.5, ((0, 32),))
    dense_gain = jnp.clip(1.0 + 0.1 * jax.random.normal(key_of[16], (D,), jnp.float32), 0.5, 1.5).astype(jnp.bfloat16)
    dense_shift = bell_draw(key_of[17], (D,), 0.3, 1.75, ((0, 32),))
    dense_in = bell_draw(key_of[18], (D, FF), D ** -0.5, 0.1875, ((0, 32),))
    dense_out = bell_draw(key_of[19], (FF, D), FF ** -0.5, 0.09375, ((0, 32),))
    out_grad = bell_draw(key_of[20], (TOKENS, D), 1.0, 6.0, ((0, 32),))
    return dict(tokens_in=tokens_in, prompt_states=prompt_states, image_ids=image_ids, text_lengths=text_lengths, attn_gain=attn_gain, attn_shift=attn_shift, self_query=self_query, self_key=self_key, self_value=self_value, self_out=self_out, cross_gain=cross_gain, cross_shift=cross_shift, cross_query=cross_query, cross_key=cross_key, cross_value=cross_value, cross_out=cross_out, dense_gain=dense_gain, dense_shift=dense_shift, dense_in=dense_in, dense_out=dense_out, out_grad=out_grad)


@jax.custom_vjp
def low(v):
    return lax.optimization_barrier(v.astype(jnp.bfloat16)).astype(jnp.float32)

@jax.custom_vjp
def low_back(v):
    return v

def low_keep(v):
    return (low(v), None)

def low_pass(kept, grad):
    return (grad,)

def back_keep(v):
    return (v, None)

def back_low(kept, grad):
    return (low(grad),)
low.defvjp(low_keep, low_pass)
low_back.defvjp(back_keep, back_low)

def matmul(left, right):
    return jnp.dot(left, right, precision=lax.Precision.HIGHEST, preferred_element_type=jnp.float32)

def layer_norm(value, gain, shift):
    center = value - lax.optimization_barrier(jnp.mean(value, axis=-1, keepdims=True))
    spread = lax.optimization_barrier(jnp.mean(center * center, axis=-1, keepdims=True))
    return center * lax.rsqrt(spread + 1e-06) * gain + shift

def attention(block_q, block_k, block_v, allowed):
    scores = jnp.einsum('qhe,khe->hqk', block_q, block_k, precision=lax.Precision.HIGHEST) * 0.125
    scores = low_back(scores)
    scores = jnp.where(allowed[None], scores, -1e+30)
    peak = lax.optimization_barrier(jnp.max(scores, axis=-1, keepdims=True))
    expo = jnp.exp(scores - peak)
    probs = low(expo / lax.optimization_barrier(jnp.sum(expo, axis=-1, keepdims=True)))
    return jnp.einsum('hqk,khe->qhe', probs, block_v, precision=lax.Precision.HIGHEST)

def reference(tokens_in, prompt_states, image_ids, text_lengths, attn_gain, attn_shift, self_query, self_key, self_value, self_out, cross_gain, cross_shift, cross_query, cross_key, cross_value, cross_out, dense_gain, dense_shift, dense_in, dense_out, out_grad):
    bands = image_ids.shape[0] // ROWS_DEV
    tok_dev = ROWS_DEV * ROW_TOK
    text = prompt_states.shape[1]
    token_ids = jnp.repeat(image_ids, ROW_TOK).reshape(bands, tok_dev).astype(jnp.int32)
    prev_ids = jnp.concatenate([jnp.full((1, tok_dev), -1, jnp.int32), token_ids[:-1]], 0)
    key_ids = jnp.concatenate([prev_ids, token_ids], 1).astype(jnp.int32)
    band_index = jnp.arange(bands, dtype=jnp.int32)
    padded_lens = jnp.concatenate([text_lengths, jnp.zeros((1,), jnp.int32)]).astype(jnp.int32)
    pair_lens = jnp.stack([text_lengths, padded_lens[1:]], 1).astype(jnp.int32)
    pair_owner = jnp.stack([band_index, band_index + 1], 1).astype(jnp.int32)

    def self_block(parts):
        block_q, block_k, block_v, query_ids, block_key_ids = parts
        key_place = jnp.arange(2 * tok_dev, dtype=jnp.int32)
        query_place = tok_dev + jnp.arange(tok_dev, dtype=jnp.int32)
        allowed = (block_key_ids[None, :] == query_ids[:, None]) & (key_place[None, :] <= query_place[:, None])
        return attention(block_q, block_k, block_v, allowed)

    def cross_block(parts):
        block_q, block_k, block_v, query_ids, owners, lens = parts
        slot_owner = jnp.repeat(owners, text)
        slot_len = jnp.repeat(lens, text)
        slot_place = jnp.tile(jnp.arange(text, dtype=jnp.int32), 2)
        allowed = (query_ids[:, None] == slot_owner[None, :]) & (slot_place < slot_len)[None, :]
        return attention(block_q, block_k, block_v, allowed)

    def heads(tensor, count):
        return tensor.reshape(bands, count, HEADS, HEAD)

    def with_before(tensor):
        return jnp.concatenate([jnp.concatenate([jnp.zeros_like(tensor[:1]), tensor[:-1]], 0), tensor], 1)

    def with_after(tensor):
        return jnp.concatenate([tensor, jnp.concatenate([tensor[1:], jnp.zeros_like(tensor[:1])], 0)], 1)

    def forward(tokens, prompt, gain_attn, bias_attn, full_query, full_key, full_value, full_out, gain_cross, bias_cross, full_cross_query, full_cross_key, full_cross_value, full_cross_out, gain_dense, bias_dense, full_dense_in, full_dense_out):
        attn_in = low(layer_norm(tokens, gain_attn, bias_attn))
        query = low_back(low(matmul(attn_in, full_query)))
        key = low_back(low(matmul(attn_in, full_key)))
        value = low_back(low(matmul(attn_in, full_value)))
        self_mix = lax.map(jax.checkpoint(self_block), (heads(query, tok_dev), with_before(heads(key, tok_dev)), with_before(heads(value, tok_dev)), token_ids, key_ids))
        self_mix = low_back(low(self_mix.reshape(-1, HEADS * HEAD)))
        resid_one = tokens + low_back(matmul(self_mix, full_out))
        cross_in = low(layer_norm(resid_one, gain_cross, bias_cross))
        cross_q = low_back(low(matmul(cross_in, full_cross_query)))
        flat_prompt = prompt.reshape(-1, prompt.shape[2])
        prompt_key = low_back(low(matmul(flat_prompt, full_cross_key)))
        prompt_value = low_back(low(matmul(flat_prompt, full_cross_value)))
        cross_mix = lax.map(jax.checkpoint(cross_block), (heads(cross_q, tok_dev), with_after(heads(prompt_key, text)), with_after(heads(prompt_value, text)), token_ids, pair_owner, pair_lens))
        cross_mix = low_back(low(cross_mix.reshape(-1, HEADS * HEAD)))
        resid_two = resid_one + low_back(matmul(cross_mix, full_cross_out))
        dense_x = low(layer_norm(resid_two, gain_dense, bias_dense))
        hidden = low_back(matmul(dense_x, full_dense_in))
        act = low(jax.nn.gelu(hidden, approximate=False))
        return resid_two + low_back(matmul(act, full_dense_out))
    weights = (attn_gain, attn_shift, self_query, self_key, self_value, self_out, cross_gain, cross_shift, cross_query, cross_key, cross_value, cross_out, dense_gain, dense_shift, dense_in, dense_out)
    prims = (tokens_in.astype(jnp.float32), prompt_states.astype(jnp.float32)) + tuple((w.astype(jnp.float32) for w in weights))
    result, pullback = jax.vjp(forward, *prims)
    grads = pullback(out_grad.astype(jnp.float32))
    return (result.astype(jnp.bfloat16), grads[0], grads[1], grads[2], grads[3], grads[4], grads[5], grads[6], grads[7], grads[8], grads[9], grads[10], grads[11], grads[12], grads[13], grads[14], grads[15], grads[16], grads[17])
```

```python
import functools

import jax
import jax.numpy as jnp
from jax import lax
from jax.experimental import pallas as pl
from jax.experimental.pallas import tpu as pltpu
from jax.sharding import PartitionSpec as P

HEADS = 16
HEAD = 64
ROW_TOK = 32
MESH = pl.DeviceIdType.MESH


def dims_of(count):
    side = 1
    while 2 * (2 * side) ** 2 * 2 <= count:
        side *= 2
    return (count // (2 * side * side), side, side, 2)

class Place:
    def __init__(self, count):
        self.Z, self.P, self.Q, self.C = dims_of(count)
        me = lax.axis_index("band")
        self.c = me % 2
        self.q = (me // 2) % self.Q
        self.p = (me // (2 * self.Q)) % self.P
        self.z = me // (2 * self.Q * self.P)
    def dev(self, dz=0, dp=0, dq=0, dc=0):
        z = (self.z + dz) % self.Z
        p = (self.p + dp) % self.P
        q = (self.q + dq) % self.Q
        c = (self.c + dc) % 2
        return ((z * self.P + p) * self.Q + q) * 2 + c
    def partners(self):
        return ([self.dev(dz=o) for o in range(1, self.Z)] + [self.dev(dp=o) for o in range(1, self.P)]
                + [self.dev(dq=o) for o in range(1, self.Q)] + [self.dev(dc=1)])

def barrier(place):
    sem = pltpu.get_barrier_semaphore()
    who = place.partners()
    for d in who:
        pl.semaphore_signal(sem, inc=1, device_id=(d,), device_id_type=MESH)
    pl.semaphore_wait(sem, len(who))

class Gather:
    def __init__(self, pc, own, out, send, recv, loc, k):
        self.pc, self.own, self.out, self.send, self.recv, self.loc, self.k = pc, own, out, send, recv, loc, k
        Z, Pn, Qn = pc.Z, pc.P, pc.Q
        n = 0
        self.slots = {}
        for o in range(1, Z): self.slots["z", o] = n; n += 1
        for h in range(2):
            for o in range(1, Pn): self.slots["p", h, o] = n; n += 1
            for o in range(1, Qn): self.slots["q", h, o] = n; n += 1
        for o in range(1, Pn):
            for r in range(1, Qn):
                self.slots["pq", o, r] = n; n += 1
                self.slots["qp", o, r] = n; n += 1
        for a in range(Pn):
            for b in range(Qn):
                self.slots["c", a, b] = n; n += 1
        self.count = n
    @staticmethod
    def nslots(Z, Pn, Qn):
        return (Z - 1) + 2 * (Pn - 1 + Qn - 1) + 2 * (Pn - 1) * (Qn - 1) + Pn * Qn
    def copy(self, key, src, dst, dev):
        s = self.slots[key]
        return pltpu.make_async_remote_copy(src_ref=src, dst_ref=dst, send_sem=self.send.at[self.k, s], recv_sem=self.recv.at[self.k, s],
                                            device_id=(dev,), device_id_type=MESH)
    def half(self, h):
        return pl.ds(h * (self.pc.Z // 2), self.pc.Z // 2)
    def s0(self):
        pc = self.pc
        self.local = pltpu.make_async_copy(self.own, self.out(pc.z, pc.p, pc.q, pc.c), self.loc.at[self.k])
        self.local.start()
        self.zs = [self.copy(("z", o), self.own, self.out(pc.z, pc.p, pc.q, pc.c), pc.dev(dz=o)) for o in range(1, pc.Z)]
        for d in self.zs: d.start()
    def s1(self):
        pc = self.pc
        self.local.wait()
        for d in self.zs: d.wait_recv()
        self.ps = {}
        for h in range(2):
            v = self.out(self.half(h), pc.p, pc.q, pc.c)
            for o in range(1, pc.P): self.ps["p", h, o] = self.copy(("p", h, o), v, v, pc.dev(dp=o))
            for o in range(1, pc.Q): self.ps["q", h, o] = self.copy(("q", h, o), v, v, pc.dev(dq=o))
        for o in range(1, pc.P): self.ps["p", 0, o].start()
        for o in range(1, pc.Q): self.ps["q", 1, o].start()
        for o in range(1, pc.P): self.ps["p", 1, o].start()
        for o in range(1, pc.Q): self.ps["q", 0, o].start()
        self.cs = []
        v = self.out(slice(None), pc.p, pc.q, pc.c)
        d = self.copy(("c", 0, 0), v, v, pc.dev(dc=1)); d.start(); self.cs.append(d)
    def s2(self):
        pc = self.pc
        self.rs = []
        for o in range(1, pc.P): self.ps["p", 0, o].wait_recv()
        for o in range(1, pc.P):
            v = self.out(self.half(0), (pc.p - o) % pc.P, pc.q, pc.c)
            for r in range(1, pc.Q):
                d = self.copy(("pq", o, r), v, v, pc.dev(dq=r)); d.start(); self.rs.append(d)
        for r in range(1, pc.Q): self.ps["q", 1, r].wait_recv()
        for r in range(1, pc.Q):
            v = self.out(self.half(1), pc.p, (pc.q - r) % pc.Q, pc.c)
            for o in range(1, pc.P):
                d = self.copy(("qp", o, r), v, v, pc.dev(dp=o)); d.start(); self.rs.append(d)
        for o in range(1, pc.P): self.ps["p", 1, o].wait_recv()
        for o in range(1, pc.P):
            v = self.out(slice(None), (pc.p - o) % pc.P, pc.q, pc.c)
            d = self.copy(("c", o, 0), v, v, pc.dev(dc=1)); d.start(); self.cs.append(d)
        for r in range(1, pc.Q): self.ps["q", 0, r].wait_recv()
        for r in range(1, pc.Q):
            v = self.out(slice(None), pc.p, (pc.q - r) % pc.Q, pc.c)
            d = self.copy(("c", 0, r), v, v, pc.dev(dc=1)); d.start(); self.cs.append(d)
    def s3(self):
        pc = self.pc
        for d in self.rs: d.wait_recv()
        for o in range(1, pc.P):
            for r in range(1, pc.Q):
                v = self.out(slice(None), (pc.p - o) % pc.P, (pc.q - r) % pc.Q, pc.c)
                d = self.copy(("c", o, r), v, v, pc.dev(dc=1)); d.start(); self.cs.append(d)
    def s4(self):
        for d in self.cs: d.wait_recv()
    def drain(self):
        for d in self.zs: d.wait_send()
        for d in self.ps.values(): d.wait_send()
        for d in self.rs: d.wait_send()
        for d in self.cs: d.wait_send()

def chunks_of(shapes, n):
    out = []
    for a, (r, c) in enumerate(shapes):
        base_r = min(s[0] for s in shapes if s[1] >= 1024) if c >= 1024 else r
        if c >= 1024:
            for i in range(0, r, base_r):
                for j in range(0, c, 1024):
                    out.append((a, i, base_r, j, 1024))
        else:
            out.append((a, 0, r, 0, c))
    return out

def ag_kernel(count, nW, chunks, *refs):
    ins, outs = refs[:nW], refs[nW:2 * nW]
    send, recv, loc = refs[2 * nW:]
    pc = Place(count)
    barrier(pc)
    gs = []
    for k, (a, r0, rn, c0, cn) in enumerate(chunks):
        own = ins[a].at[pl.ds(r0, rn), pl.ds(c0, cn)]
        def out(z, p, q, c, a=a, r0=r0, rn=rn, c0=c0, cn=cn):
            return outs[a].at[z, p, q, c, pl.ds(r0, rn), pl.ds(c0, cn)]
        gs.append(Gather(pc, own, out, send, recv, loc, k))
    n = len(gs)
    for t in range(n + 4):
        for stage in range(5):
            k = t - stage
            if 0 <= k < n:
                getattr(gs[k], f"s{stage}")()
    for g in gs: g.drain()

def gather_all(shards, count, cid=0):
    dims = dims_of(count)
    nW = len(shards)
    chunks = chunks_of([s.shape for s in shards], count)
    ns = Gather.nslots(*dims[:3])
    outs = pl.pallas_call(
        functools.partial(ag_kernel, count, nW, chunks),
        out_shape=[jax.ShapeDtypeStruct(dims + s.shape, s.dtype) for s in shards],
        in_specs=[pl.BlockSpec(memory_space=pl.ANY)] * nW,
        out_specs=[pl.BlockSpec(memory_space=pl.ANY)] * nW,
        scratch_shapes=[pltpu.SemaphoreType.DMA((len(chunks), ns)), pltpu.SemaphoreType.DMA((len(chunks), ns)), pltpu.SemaphoreType.DMA((len(chunks),))],
        compiler_params=pltpu.CompilerParams(collective_id=cid, has_side_effects=True),
        name="gather",
    )(*shards)
    return [o.reshape((count * s.shape[0],) + s.shape[1:]) for o, s in zip(outs, shards)]


class Scatter:
    def __init__(self, pc, grad, put, bufs, send, recv, loc, k, kb):
        self.pc, self.grad, self.put, self.send, self.recv, self.loc, self.k, self.kb = pc, grad, put, send, recv, loc, k, kb
        self.own, self.r1, self.r2a, self.r2b, self.r3a, self.r3b, self.r4 = [b.at[kb] for b in bufs]
        Z, Pn, Qn = pc.Z, pc.P, pc.Q
        n = 0
        self.slots = {"c": 0}; n = 1
        for o in range(1, Qn): self.slots["2a", o] = n; n += 1
        for o in range(1, Pn): self.slots["2b", o] = n; n += 1
        for o in range(1, Pn): self.slots["3a", o] = n; n += 1
        for o in range(1, Qn): self.slots["3b", o] = n; n += 1
        for o in range(1, Z): self.slots["4", o] = n; n += 1
    @staticmethod
    def nslots(Z, Pn, Qn):
        return 1 + 2 * (Pn - 1 + Qn - 1) + Z - 1
    @staticmethod
    def buffers(n, dims, block, dtype):
        Z, Pn, Qn = dims[:3]; H = Z // 2
        return [(n, Z, Pn, Qn) + block, (n, Z, Pn, Qn) + block, (n, Qn - 1, H, Pn) + block, (n, Pn - 1, H, Qn) + block,
                (n, Pn - 1, H) + block, (n, Qn - 1, H) + block, (n, Z - 1) + block]
    def copy(self, key, src, dst, dev):
        s = self.slots[key]
        return pltpu.make_async_remote_copy(src_ref=src, dst_ref=dst, send_sem=self.send.at[self.k, s], recv_sem=self.recv.at[self.k, s],
                                            device_id=(dev,), device_id_type=MESH)
    def s0(self):
        pc = self.pc
        self.d1 = self.copy("c", self.grad(1 - pc.c), self.r1, pc.dev(dc=1)); self.d1.start()
        self.l = pltpu.make_async_copy(self.grad(pc.c), self.own, self.loc.at[self.k]); self.l.start()
    def s1(self):
        pc = self.pc; Z, Pn, Qn = pc.Z, pc.P, pc.Q; H = Z // 2
        self.l.wait(); self.d1.wait_recv()
        def body(i, _):
            z, p, q = i // (Pn * Qn), (i // Qn) % Pn, i % Qn
            self.r1[z, p, q] = (self.r1[z, p, q].astype(jnp.float32) + self.own[z, p, q].astype(jnp.float32)).astype(self.r1.dtype)
            return 0
        lax.fori_loop(0, Z * Pn * Qn, body, 0)
        self.d2 = []
        for o in range(1, Qn):
            d = self.copy(("2a", o), self.r1.at[pl.ds(0, H), :, (pc.q + o) % Qn], self.r2a.at[o - 1], pc.dev(dq=o)); d.start(); self.d2.append(d)
        for o in range(1, Pn):
            d = self.copy(("2b", o), self.r1.at[pl.ds(H, H), (pc.p + o) % Pn], self.r2b.at[o - 1], pc.dev(dp=o)); d.start(); self.d2.append(d)
    def s2(self):
        pc = self.pc; Z, Pn, Qn = pc.Z, pc.P, pc.Q; H = Z // 2
        for d in self.d2: d.wait_recv()
        def body(i, _):
            h, p = i // Pn, i % Pn
            t = self.r1[h, p, pc.q].astype(jnp.float32)
            for o in range(Qn - 1): t += self.r2a[o, h, p].astype(jnp.float32)
            self.r2a[0, h, p] = t.astype(self.r1.dtype)
            return 0
        lax.fori_loop(0, H * Pn, body, 0)
        def body(i, _):
            h, q = i // Qn, i % Qn
            t = self.r1[H + h, pc.p, q].astype(jnp.float32)
            for o in range(Pn - 1): t += self.r2b[o, h, q].astype(jnp.float32)
            self.r2b[0, h, q] = t.astype(self.r1.dtype)
            return 0
        lax.fori_loop(0, H * Qn, body, 0)
        self.d3 = []
        for o in range(1, Pn):
            d = self.copy(("3a", o), self.r2a.at[0, :, (pc.p + o) % Pn], self.r3a.at[o - 1], pc.dev(dp=o)); d.start(); self.d3.append(d)
        for o in range(1, Qn):
            d = self.copy(("3b", o), self.r2b.at[0, :, (pc.q + o) % Qn], self.r3b.at[o - 1], pc.dev(dq=o)); d.start(); self.d3.append(d)
    def s3(self):
        pc = self.pc; Z, Pn, Qn = pc.Z, pc.P, pc.Q; H = Z // 2
        for d in self.d3: d.wait_recv()
        def body(h, _):
            t = self.r2a[0, h, pc.p].astype(jnp.float32)
            for o in range(Pn - 1): t += self.r3a[o, h].astype(jnp.float32)
            self.r3a[0, h] = t.astype(self.r1.dtype)
            t = self.r2b[0, h, pc.q].astype(jnp.float32)
            for o in range(Qn - 1): t += self.r3b[o, h].astype(jnp.float32)
            self.r3b[0, h] = t.astype(self.r1.dtype)
            return 0
        lax.fori_loop(0, H, body, 0)
        self.d4 = []
        for o in range(1, Z):
            zt = (pc.z + o) % Z
            @pl.when(zt < H)
            def _():
                self.copy(("4", o), self.r3a.at[0, zt], self.r4.at[o - 1], pc.dev(dz=o)).start()
            @pl.when(zt >= H)
            def _():
                self.copy(("4", o), self.r3b.at[0, zt - H], self.r4.at[o - 1], pc.dev(dz=o)).start()
            self.d4.append(self.copy(("4", o), self.r3a.at[0, 0], self.r4.at[o - 1], pc.dev(dz=o)))
    def s4(self):
        pc = self.pc; Z, Pn, Qn = pc.Z, pc.P, pc.Q; H = Z // 2
        for d in self.d4: d.wait_recv()
        def fin(first):
            t = first.astype(jnp.float32)
            for o in range(Z - 1): t += self.r4[o].astype(jnp.float32)
            self.put(t)
        @pl.when(pc.z < H)
        def _(): fin(self.r3a[0, pc.z])
        @pl.when(pc.z >= H)
        def _(): fin(self.r3b[0, pc.z - H])
    def drain(self):
        self.d1.wait_send()
        for d in self.d2 + self.d3 + self.d4: d.wait_send()

def rs_kernel(count, nW, chunks, *refs):
    ins, outs = refs[:nW], refs[nW : 2 * nW]
    big, small = refs[2 * nW : 2 * nW + 7], refs[2 * nW + 7 : 2 * nW + 14]
    send, recv, loc = refs[2 * nW + 14 :]
    pc = Place(count)
    barrier(pc)
    ss = []
    wide = chunks[0][4]
    for k, (a, r0, rn, c0, cn) in enumerate(chunks):
        def grad(c, a=a, r0=r0, rn=rn, c0=c0, cn=cn):
            return ins[a].at[:, :, :, c, pl.ds(r0, rn), pl.ds(c0, cn)]
        def put(t, a=a, r0=r0, rn=rn, c0=c0, cn=cn):
            outs[a][pl.ds(r0, rn), pl.ds(c0, cn)] = t
        if cn == wide:
            ss.append(Scatter(pc, grad, put, big, send, recv, loc, k, k))
        else:
            ss.append(Scatter(pc, grad, put, small, send, recv, loc, k, 0))
    n = len(ss)
    for t in range(n + 4):
        for stage in range(5):
            k = t - stage
            if 0 <= k < n:
                getattr(ss[k], f"s{stage}")()
    for s in ss: s.drain()

def scatter_all(grads, shard_shapes, count, cid=1):
    dims = dims_of(count)
    nW = len(grads)
    chunks = chunks_of(shard_shapes, count)
    ns = Scatter.nslots(*dims[:3])
    block = chunks[0][2], chunks[0][4]
    bufs = [pltpu.VMEM(s, jnp.bfloat16) for s in Scatter.buffers(len(chunks) - 1, dims, block, None)]
    bufs += [pltpu.VMEM(s, jnp.float32) for s in Scatter.buffers(1, dims, shard_shapes[-1], None)]
    sems = [pltpu.SemaphoreType.DMA((len(chunks), ns)), pltpu.SemaphoreType.DMA((len(chunks), ns)), pltpu.SemaphoreType.DMA((len(chunks),))]
    return pl.pallas_call(
        functools.partial(rs_kernel, count, nW, chunks),
        out_shape=[jax.ShapeDtypeStruct(s, jnp.float32) for s in shard_shapes],
        in_specs=[pl.BlockSpec(memory_space=pl.ANY)] * nW,
        out_specs=[pl.BlockSpec(memory_space=pltpu.VMEM)] * nW,
        scratch_shapes=bufs + sems,
        compiler_params=pltpu.CompilerParams(collective_id=cid, has_side_effects=True, vmem_limit_bytes=60 << 20),
        name="scatter",
    )(*[g.reshape(dims + tuple(s)) for g, s in zip(grads, shard_shapes)])


def from_behind(block, axis, distance):
    devices = range(lax.axis_size(axis))
    route = [(i - distance, i) for i in devices if i - distance in devices]
    return lax.ppermute(block, axis, route)


def as_sent(shard):
    return jax.tree.map(lambda a: a.astype(jnp.bfloat16) if a.dtype == jnp.float32 else a, shard)


def layer_norm(value, gain, shift):
    center = value - jnp.mean(value, axis=-1, keepdims=True)
    spread = jnp.mean(center * center, axis=-1, keepdims=True)
    return center * lax.rsqrt(spread + 1e-06) * gain + shift


def norm_back(value, gain, shift, incoming):
    _, pullback = jax.vjp(layer_norm, value, gain, shift)
    return pullback(incoming)


def gelu_exact(value):
    return jax.nn.gelu(value, approximate=False)


def matmul(left, right):
    return jnp.dot(left, right, preferred_element_type=jnp.float32)


def matmul_nt(left, right):
    return lax.dot_general(
        left, right, (((1,), (1,)), ((), ())), preferred_element_type=jnp.float32
    )


def matmul_tn(left, right):
    return lax.dot_general(
        left, right, (((0,), (0,)), ((), ())), preferred_element_type=jnp.float32
    )


def by_groups(tensor):
    return tensor.reshape(tensor.shape[0], HEADS // 4, 4, HEAD).transpose(1, 0, 2, 3)


def from_groups(tensor):
    return tensor.transpose(1, 0, 2, 3).reshape(tensor.shape[1], HEADS * HEAD)


def masked_scores(block_q, block_k, allowed):
    scores = (
        jnp.einsum("qhe,khe->hqk", block_q, block_k, preferred_element_type=jnp.float32) * 0.125
    )
    return jnp.where(allowed[None], scores, -1e30)


def attend_fwd(query, keys, values, allowed):

    def one_group(parts):
        block_q, block_k, block_v = parts
        scores = masked_scores(block_q, block_k, allowed)
        peak = jnp.max(scores, axis=-1, keepdims=True)
        expo = jnp.exp(scores - peak)
        total = jnp.sum(expo, axis=-1, keepdims=True)
        probs = (expo / total).astype(jnp.bfloat16)
        mixed = jnp.einsum(
            "hqk,khe->qhe", probs, block_v, preferred_element_type=jnp.float32
        ).astype(jnp.bfloat16)
        return (mixed, peak[..., 0] + jnp.log(total[..., 0]))

    mixed, lse = lax.map(one_group, (by_groups(query), by_groups(keys), by_groups(values)))
    return (from_groups(mixed), lse)


def attend_back(query, keys, values, allowed, lse, grad_mix):

    def one_group(parts):
        block_q, block_k, block_v, block_d, block_l = parts
        scores = masked_scores(block_q, block_k, allowed)
        probs = jnp.exp(scores - block_l[..., None])
        grad_prob = jnp.einsum("qhe,khe->hqk", block_d, block_v, preferred_element_type=jnp.float32)
        inner = jnp.sum(probs * grad_prob, axis=-1, keepdims=True)
        grad_scores = (probs * (grad_prob - inner)).astype(jnp.bfloat16)
        grad_q = (
            jnp.einsum("hqk,khe->qhe", grad_scores, block_k, preferred_element_type=jnp.float32)
            * 0.125
        )
        grad_k = (
            jnp.einsum("hqk,qhe->khe", grad_scores, block_q, preferred_element_type=jnp.float32)
            * 0.125
        )
        grad_v = jnp.einsum(
            "hqk,qhe->khe", probs.astype(jnp.bfloat16), block_d, preferred_element_type=jnp.float32
        )
        return (grad_q, grad_k, grad_v)

    grad_q, grad_k, grad_v = lax.map(
        one_group, (by_groups(query), by_groups(keys), by_groups(values), by_groups(grad_mix), lse)
    )
    return (from_groups(grad_q), from_groups(grad_k), from_groups(grad_v))


def on_device(
    tokens_in,
    prompt_states,
    image_ids,
    text_lengths,
    attn_gain,
    attn_shift,
    self_query,
    self_key,
    self_value,
    self_out,
    cross_gain,
    cross_shift,
    cross_query,
    cross_key,
    cross_value,
    cross_out,
    dense_gain,
    dense_shift,
    dense_in,
    dense_out,
    out_grad,
):
    shards = (
        attn_gain,
        attn_shift,
        self_query,
        self_key,
        self_value,
        self_out,
        cross_gain,
        cross_shift,
        cross_query,
        cross_key,
        cross_value,
        cross_out,
        dense_gain,
        dense_shift,
        dense_in,
        dense_out,
    )
    count = lax.axis_size("band")
    gains = (shards[0], shards[1], shards[6], shards[7], shards[12], shards[13])
    packed = jnp.pad(jnp.stack(gains), ((0, 2), (0, 128 - shards[0].shape[0])))
    mats = tuple(shards[i] for i in (2, 3, 4, 5, 8, 9, 10, 11, 14, 15))
    *full, many = gather_all(list(mats) + [packed], count)
    many = many.reshape(count, 8, 128)[:, :6, : shards[0].shape[0]].transpose(1, 0, 2).reshape(6, -1)
    whole = (many[0], many[1], *full[:4], many[2], many[3], *full[4:8], many[4], many[5], *full[8:])
    (
        gain_attn,
        bias_attn,
        full_query,
        full_key,
        full_value,
        full_out,
        gain_cross,
        bias_cross,
        full_cross_query,
        full_cross_key,
        full_cross_value,
        full_cross_out,
        gain_dense,
        bias_dense,
        full_dense_in,
        full_dense_out,
    ) = whole
    device = lax.axis_index("band")
    tok_dev = tokens_in.shape[0]
    rows_dev = tok_dev // ROW_TOK
    text = prompt_states.shape[1]
    padded_ids = jnp.concatenate([jnp.full((rows_dev,), -1, jnp.int32), image_ids])
    window_ids = lax.dynamic_slice_in_dim(padded_ids, device * rows_dev, 2 * rows_dev)
    key_ids = jnp.repeat(window_ids, ROW_TOK, total_repeat_length=2 * tok_dev)
    query_ids = key_ids[tok_dev:]
    key_place = jnp.arange(2 * tok_dev, dtype=jnp.int32)
    query_place = tok_dev + jnp.arange(tok_dev, dtype=jnp.int32)
    self_allowed = (key_ids[None, :] == query_ids[:, None]) & (
        key_place[None, :] <= query_place[:, None]
    )
    padded_len = jnp.concatenate([text_lengths, jnp.zeros((1,), jnp.int32)])
    near_len = lax.dynamic_slice_in_dim(padded_len, device, 2)
    slot_owner = device + jnp.arange(2, dtype=jnp.int32)
    owner_key = jnp.repeat(slot_owner, text, total_repeat_length=2 * text)
    length_key = jnp.repeat(near_len, text, total_repeat_length=2 * text)
    place_key = jnp.tile(jnp.arange(text, dtype=jnp.int32), 2)
    live_owner = owner_key < count
    cross_allowed = (
        (query_ids[:, None] == owner_key[None, :])
        & (place_key < length_key)[None, :]
        & live_owner[None, :]
    )
    tokens = tokens_in.astype(jnp.float32)
    attn_in = layer_norm(
        tokens, gain_attn.astype(jnp.float32), bias_attn.astype(jnp.float32)
    ).astype(jnp.bfloat16)
    query = matmul(attn_in, full_query).astype(jnp.bfloat16)
    key = matmul(attn_in, full_key).astype(jnp.bfloat16)
    value = matmul(attn_in, full_value).astype(jnp.bfloat16)
    before = from_behind((key, value), "band", 1)
    keys_all = jnp.concatenate([before[0], key], 0)
    values_all = jnp.concatenate([before[1], value], 0)
    self_mix, self_lse = attend_fwd(query, keys_all, values_all, self_allowed)
    resid_one = tokens + matmul(self_mix, full_out)
    cross_in = layer_norm(
        resid_one, gain_cross.astype(jnp.float32), bias_cross.astype(jnp.float32)
    ).astype(jnp.bfloat16)
    cross_q = matmul(cross_in, full_cross_query).astype(jnp.bfloat16)
    own_states = prompt_states[0]
    own_pair = (
        matmul(own_states, full_cross_key).astype(jnp.bfloat16),
        matmul(own_states, full_cross_value).astype(jnp.bfloat16),
    )
    next_pair = from_behind((own_pair[0], own_pair[1]), "band", -1)
    prompt_key = jnp.concatenate([own_pair[0], next_pair[0]], 0)
    prompt_value = jnp.concatenate([own_pair[1], next_pair[1]], 0)
    cross_mix, cross_lse = attend_fwd(cross_q, prompt_key, prompt_value, cross_allowed)
    resid_two = resid_one + matmul(cross_mix, full_cross_out)
    dense_x = layer_norm(
        resid_two, gain_dense.astype(jnp.float32), bias_dense.astype(jnp.float32)
    ).astype(jnp.bfloat16)
    hidden = matmul(dense_x, full_dense_in)
    act = gelu_exact(hidden).astype(jnp.bfloat16)
    block_out = (resid_two + matmul(act, full_dense_out)).astype(jnp.bfloat16)
    grad_out = out_grad.astype(jnp.float32)
    grad_dense_out = matmul_tn(act, out_grad)
    grad_act = matmul_nt(out_grad, full_dense_out)
    _, gelu_pull = jax.vjp(gelu_exact, hidden)
    grad_hidden = gelu_pull(grad_act)[0].astype(jnp.bfloat16)
    grad_dense_in = matmul_tn(dense_x, grad_hidden)
    grad_dense_x = matmul_nt(grad_hidden, full_dense_in)
    grad_resid, grad_dense_gain, grad_dense_shift = norm_back(
        resid_two, gain_dense.astype(jnp.float32), bias_dense.astype(jnp.float32), grad_dense_x
    )
    grad_resid_two = grad_out + grad_resid
    dense_local = (grad_dense_gain, grad_dense_shift, grad_dense_in, grad_dense_out)
    branch_two = grad_resid_two.astype(jnp.bfloat16)
    grad_cross_out = matmul_tn(cross_mix, branch_two)
    grad_cross_mix = matmul_nt(branch_two, full_cross_out).astype(jnp.bfloat16)
    grad_cq, grad_pk, grad_pv = attend_back(
        cross_q, prompt_key, prompt_value, cross_allowed, cross_lse, grad_cross_mix
    )
    back_pair = from_behind((as_sent(grad_pk[text:]), as_sent(grad_pv[text:])), "band", 1)
    grad_pk_low = (grad_pk[:text] + back_pair[0]).astype(jnp.bfloat16)
    grad_pv_low = (grad_pv[:text] + back_pair[1]).astype(jnp.bfloat16)
    grad_cross_key = matmul_tn(own_states, grad_pk_low)
    grad_cross_value = matmul_tn(own_states, grad_pv_low)
    grad_prompt = (
        matmul_nt(grad_pk_low, full_cross_key) + matmul_nt(grad_pv_low, full_cross_value)
    )[None]
    grad_cq_low = grad_cq.astype(jnp.bfloat16)
    grad_cross_query = matmul_tn(cross_in, grad_cq_low)
    grad_cross_in = matmul_nt(grad_cq_low, full_cross_query)
    grad_resid, grad_cross_gain, grad_cross_shift = norm_back(
        resid_one, gain_cross.astype(jnp.float32), bias_cross.astype(jnp.float32), grad_cross_in
    )
    grad_resid_one = grad_resid_two + grad_resid
    cross_local = (
        grad_cross_gain,
        grad_cross_shift,
        grad_cross_query,
        grad_cross_key,
        grad_cross_value,
        grad_cross_out,
    )
    branch_one = grad_resid_one.astype(jnp.bfloat16)
    grad_self_out = matmul_tn(self_mix, branch_one)
    grad_self_mix = matmul_nt(branch_one, full_out).astype(jnp.bfloat16)
    grad_q, grad_keys_all, grad_values_all = attend_back(
        query, keys_all, values_all, self_allowed, self_lse, grad_self_mix
    )
    back_kv = from_behind(
        (as_sent(grad_keys_all[:tok_dev]), as_sent(grad_values_all[:tok_dev])), "band", -1
    )
    grad_k = grad_keys_all[tok_dev:] + back_kv[0]
    grad_v = grad_values_all[tok_dev:] + back_kv[1]
    grad_q_low = grad_q.astype(jnp.bfloat16)
    grad_k_low = grad_k.astype(jnp.bfloat16)
    grad_v_low = grad_v.astype(jnp.bfloat16)
    grad_self_query = matmul_tn(attn_in, grad_q_low)
    grad_self_key = matmul_tn(attn_in, grad_k_low)
    grad_self_value = matmul_tn(attn_in, grad_v_low)
    grad_attn_in = (
        matmul_nt(grad_q_low, full_query)
        + matmul_nt(grad_k_low, full_key)
        + matmul_nt(grad_v_low, full_value)
    )
    grad_resid, grad_attn_gain, grad_attn_shift = norm_back(
        tokens, gain_attn.astype(jnp.float32), bias_attn.astype(jnp.float32), grad_attn_in
    )
    grad_tokens = grad_resid_one + grad_resid
    self_local = (
        grad_attn_gain,
        grad_attn_shift,
        grad_self_query,
        grad_self_key,
        grad_self_value,
        grad_self_out,
    )
    locals_ = self_local + cross_local + dense_local
    vecs = jnp.stack([locals_[i] for i in (0, 1, 6, 7, 12, 13)])
    width = vecs.shape[1] // count
    vecs = vecs.reshape(6, count, width).transpose(1, 0, 2)
    vecs = jnp.pad(vecs, ((0, 0), (0, 2), (0, 128 - width))).reshape(count * 8, 128)
    order = (2, 3, 4, 5, 8, 9, 10, 11, 14, 15)
    mats = [locals_[i].astype(jnp.bfloat16) for i in order]
    *sums, small = scatter_all(mats + [vecs], [(m.shape[0] // count, m.shape[1]) for m in mats] + [(8, 128)], count)
    summed = [None] * 16
    for i, s in zip(order, sums):
        summed[i] = s
    for j, i in enumerate((0, 1, 6, 7, 12, 13)):
        summed[i] = small[j, :width]
    summed = tuple(summed)
    return (block_out, grad_tokens, grad_prompt) + summed


def solution(mesh):
    return jax.shard_map(
        on_device,
        mesh=mesh,
        in_specs=(
            P("band", None),
            P("band", None, None),
            P(),
            P(),
            P("band"),
            P("band"),
            P("band", None),
            P("band", None),
            P("band", None),
            P("band", None),
            P("band"),
            P("band"),
            P("band", None),
            P("band", None),
            P("band", None),
            P("band", None),
            P("band"),
            P("band"),
            P("band", None),
            P("band", None),
            P("band", None),
        ),
        out_specs=(
            P("band", None),
            P("band", None),
            P("band", None, None),
            P("band"),
            P("band"),
            P("band", None),
            P("band", None),
            P("band", None),
            P("band", None),
            P("band"),
            P("band"),
            P("band", None),
            P("band", None),
            P("band", None),
            P("band", None),
            P("band"),
            P("band"),
            P("band", None),
            P("band", None),
        ),
        check_vma=False,
    )
```

```python
import functools
import types

import jax
import jax.numpy as jnp
from jax import lax
from jax.experimental import pallas as pl
from jax.experimental.pallas import tpu as pltpu
from jax.sharding import PartitionSpec as P

HEADS = 16
HEAD = 64
ROW_TOK = 32
MESH = pl.DeviceIdType.MESH


def dims_of(count):
    side = 1
    while 2 * (2 * side) ** 2 * 2 <= count:
        side *= 2
    return (count // (2 * side * side), side, side, 2)

class Place:
    def __init__(self, count):
        self.Z, self.P, self.Q, self.C = dims_of(count)
        me = lax.axis_index("band")
        self.c = me % 2
        self.q = (me // 2) % self.Q
        self.p = (me // (2 * self.Q)) % self.P
        self.z = me // (2 * self.Q * self.P)
    def dev(self, dz=0, dp=0, dq=0, dc=0):
        z = (self.z + dz) % self.Z
        p = (self.p + dp) % self.P
        q = (self.q + dq) % self.Q
        c = (self.c + dc) % 2
        return ((z * self.P + p) * self.Q + q) * 2 + c
    def partners(self):
        return ([self.dev(dz=o) for o in range(1, self.Z)] + [self.dev(dp=o) for o in range(1, self.P)]
                + [self.dev(dq=o) for o in range(1, self.Q)] + [self.dev(dc=1)])

def barrier(place):
    sem = pltpu.get_barrier_semaphore()
    who = place.partners()
    for d in who:
        pl.semaphore_signal(sem, inc=1, device_id=(d,), device_id_type=MESH)
    pl.semaphore_wait(sem, len(who))

class Gather:
    def __init__(self, pc, own, out, send, recv, loc, k):
        self.pc, self.own, self.out, self.send, self.recv, self.loc, self.k = pc, own, out, send, recv, loc, k
        Z, Pn, Qn = pc.Z, pc.P, pc.Q
        n = 0
        self.slots = {}
        for o in range(1, Z): self.slots["z", o] = n; n += 1
        for h in range(2):
            for o in range(1, Pn): self.slots["p", h, o] = n; n += 1
            for o in range(1, Qn): self.slots["q", h, o] = n; n += 1
        for o in range(1, Pn):
            for r in range(1, Qn):
                self.slots["pq", o, r] = n; n += 1
                self.slots["qp", o, r] = n; n += 1
        for a in range(Pn):
            for b in range(Qn):
                self.slots["c", a, b] = n; n += 1
        self.count = n
    @staticmethod
    def nslots(Z, Pn, Qn):
        return (Z - 1) + 2 * (Pn - 1 + Qn - 1) + 2 * (Pn - 1) * (Qn - 1) + Pn * Qn
    def copy(self, key, src, dst, dev):
        s = self.slots[key]
        return pltpu.make_async_remote_copy(src_ref=src, dst_ref=dst, send_sem=self.send.at[self.k, s], recv_sem=self.recv.at[self.k, s],
                                            device_id=(dev,), device_id_type=MESH)
    def half(self, h):
        return pl.ds(h * (self.pc.Z // 2), self.pc.Z // 2)
    def s0(self):
        pc = self.pc
        self.local = pltpu.make_async_copy(self.own, self.out(pc.z, pc.p, pc.q, pc.c), self.loc.at[self.k])
        self.local.start()
        self.zs = [self.copy(("z", o), self.own, self.out(pc.z, pc.p, pc.q, pc.c), pc.dev(dz=o)) for o in range(1, pc.Z)]
        for d in self.zs: d.start()
    def s1(self):
        pc = self.pc
        self.local.wait()
        for d in self.zs: d.wait_recv()
        self.ps = {}
        for h in range(2):
            v = self.out(self.half(h), pc.p, pc.q, pc.c)
            for o in range(1, pc.P): self.ps["p", h, o] = self.copy(("p", h, o), v, v, pc.dev(dp=o))
            for o in range(1, pc.Q): self.ps["q", h, o] = self.copy(("q", h, o), v, v, pc.dev(dq=o))
        for o in range(1, pc.P): self.ps["p", 0, o].start()
        for o in range(1, pc.Q): self.ps["q", 1, o].start()
        for o in range(1, pc.P): self.ps["p", 1, o].start()
        for o in range(1, pc.Q): self.ps["q", 0, o].start()
        self.cs = []
        v = self.out(slice(None), pc.p, pc.q, pc.c)
        d = self.copy(("c", 0, 0), v, v, pc.dev(dc=1)); d.start(); self.cs.append(d)
    def s2(self):
        pc = self.pc
        self.rs = []
        for o in range(1, pc.P): self.ps["p", 0, o].wait_recv()
        for o in range(1, pc.P):
            v = self.out(self.half(0), (pc.p - o) % pc.P, pc.q, pc.c)
            for r in range(1, pc.Q):
                d = self.copy(("pq", o, r), v, v, pc.dev(dq=r)); d.start(); self.rs.append(d)
        for r in range(1, pc.Q): self.ps["q", 1, r].wait_recv()
        for r in range(1, pc.Q):
            v = self.out(self.half(1), pc.p, (pc.q - r) % pc.Q, pc.c)
            for o in range(1, pc.P):
                d = self.copy(("qp", o, r), v, v, pc.dev(dp=o)); d.start(); self.rs.append(d)
        for o in range(1, pc.P): self.ps["p", 1, o].wait_recv()
        for o in range(1, pc.P):
            v = self.out(slice(None), (pc.p - o) % pc.P, pc.q, pc.c)
            d = self.copy(("c", o, 0), v, v, pc.dev(dc=1)); d.start(); self.cs.append(d)
        for r in range(1, pc.Q): self.ps["q", 0, r].wait_recv()
        for r in range(1, pc.Q):
            v = self.out(slice(None), pc.p, (pc.q - r) % pc.Q, pc.c)
            d = self.copy(("c", 0, r), v, v, pc.dev(dc=1)); d.start(); self.cs.append(d)
    def s3(self):
        pc = self.pc
        for d in self.rs: d.wait_recv()
        for o in range(1, pc.P):
            for r in range(1, pc.Q):
                v = self.out(slice(None), (pc.p - o) % pc.P, (pc.q - r) % pc.Q, pc.c)
                d = self.copy(("c", o, r), v, v, pc.dev(dc=1)); d.start(); self.cs.append(d)
    def s4(self):
        for d in self.cs: d.wait_recv()
    def drain(self):
        for d in self.zs: d.wait_send()
        for d in self.ps.values(): d.wait_send()
        for d in self.rs: d.wait_send()
        for d in self.cs: d.wait_send()

def chunks_of(shapes, n):
    out = []
    for a, (r, c) in enumerate(shapes):
        base_r = min(s[0] for s in shapes if s[1] >= 1024) if c >= 1024 else r
        if c >= 1024:
            for i in range(0, r, base_r):
                for j in range(0, c, 1024):
                    out.append((a, i, base_r, j, 1024))
        else:
            out.append((a, 0, r, 0, c))
    return out

def ag_kernel(count, nW, chunks, *refs):
    ins, outs = refs[:nW], refs[nW:2 * nW]
    send, recv, loc = refs[2 * nW:]
    pc = Place(count)
    barrier(pc)
    gs = []
    for k, (a, r0, rn, c0, cn) in enumerate(chunks):
        own = ins[a].at[pl.ds(r0, rn), pl.ds(c0, cn)]
        def out(z, p, q, c, a=a, r0=r0, rn=rn, c0=c0, cn=cn):
            return outs[a].at[z, p, q, c, pl.ds(r0, rn), pl.ds(c0, cn)]
        gs.append(Gather(pc, own, out, send, recv, loc, k))
    n = len(gs)
    for t in range(n + 4):
        for stage in range(5):
            k = t - stage
            if 0 <= k < n:
                getattr(gs[k], f"s{stage}")()
    for g in gs: g.drain()

def gather_all(shards, count, cid=0):
    dims = dims_of(count)
    nW = len(shards)
    chunks = chunks_of([s.shape for s in shards], count)
    ns = Gather.nslots(*dims[:3])
    outs = pl.pallas_call(
        functools.partial(ag_kernel, count, nW, chunks),
        out_shape=[jax.ShapeDtypeStruct(dims + s.shape, s.dtype) for s in shards],
        in_specs=[pl.BlockSpec(memory_space=pl.ANY)] * nW,
        out_specs=[pl.BlockSpec(memory_space=pl.ANY)] * nW,
        scratch_shapes=[pltpu.SemaphoreType.DMA((len(chunks), ns)), pltpu.SemaphoreType.DMA((len(chunks), ns)), pltpu.SemaphoreType.DMA((len(chunks),))],
        compiler_params=pltpu.CompilerParams(collective_id=cid, has_side_effects=True),
        name="gather",
    )(*shards)
    return [o.reshape((count * s.shape[0],) + s.shape[1:]) for o, s in zip(outs, shards)]


class Scatter:
    def __init__(self, pc, grad, put, bufs, send, recv, loc, k, kb):
        self.pc, self.grad, self.put, self.send, self.recv, self.loc, self.k, self.kb = pc, grad, put, send, recv, loc, k, kb
        self.own = bufs[0] if bufs[0] is None else bufs[0].at[kb]
        self.r1, self.r2a, self.r2b, self.r3a, self.r3b, self.r4 = [b.at[kb] for b in bufs[1:]]
        Z, Pn, Qn = pc.Z, pc.P, pc.Q
        n = 0
        self.slots = {"c": 0}; n = 1
        for o in range(1, Qn): self.slots["2a", o] = n; n += 1
        for o in range(1, Pn): self.slots["2b", o] = n; n += 1
        for o in range(1, Pn): self.slots["3a", o] = n; n += 1
        for o in range(1, Qn): self.slots["3b", o] = n; n += 1
        for o in range(1, Z): self.slots["4", o] = n; n += 1
    @staticmethod
    def nslots(Z, Pn, Qn):
        return 1 + 2 * (Pn - 1 + Qn - 1) + Z - 1
    @staticmethod
    def buffers(n, dims, block, dtype):
        Z, Pn, Qn = dims[:3]; H = Z // 2
        return [(n, Z, Pn, Qn) + block, (n, Z, Pn, Qn) + block, (n, Qn - 1, H, Pn) + block, (n, Pn - 1, H, Qn) + block,
                (n, Pn - 1, H) + block, (n, Qn - 1, H) + block, (n, Z - 1) + block]
    def copy(self, key, src, dst, dev):
        s = self.slots[key]
        return pltpu.make_async_remote_copy(src_ref=src, dst_ref=dst, send_sem=self.send.at[self.k, s], recv_sem=self.recv.at[self.k, s],
                                            device_id=(dev,), device_id_type=MESH)
    def s0(self):
        pc = self.pc
        self.d1 = self.copy("c", self.grad(1 - pc.c), self.r1, pc.dev(dc=1)); self.d1.start()
        self.l = pltpu.make_async_copy(self.grad(pc.c), self.own, self.loc.at[self.k]); self.l.start()
    def arrive(self):
        self.l.wait(); self.d1.wait_recv()
    def s1(self):
        pc = self.pc; Z, Pn, Qn = pc.Z, pc.P, pc.Q; H = Z // 2
        self.arrive()
        def body(i, _):
            z, p, q = i // (Pn * Qn), (i // Qn) % Pn, i % Qn
            self.r1[z, p, q] = (self.r1[z, p, q].astype(jnp.float32) + self.own[z, p, q].astype(jnp.float32)).astype(self.r1.dtype)
            return 0
        lax.fori_loop(0, Z * Pn * Qn, body, 0)
        self.d2 = []
        for o in range(1, Qn):
            d = self.copy(("2a", o), self.r1.at[pl.ds(0, H), :, (pc.q + o) % Qn], self.r2a.at[o - 1], pc.dev(dq=o)); d.start(); self.d2.append(d)
        for o in range(1, Pn):
            d = self.copy(("2b", o), self.r1.at[pl.ds(H, H), (pc.p + o) % Pn], self.r2b.at[o - 1], pc.dev(dp=o)); d.start(); self.d2.append(d)
    def s2(self):
        pc = self.pc; Z, Pn, Qn = pc.Z, pc.P, pc.Q; H = Z // 2
        for d in self.d2: d.wait_recv()
        def body(i, _):
            h, p = i // Pn, i % Pn
            t = self.r1[h, p, pc.q].astype(jnp.float32)
            for o in range(Qn - 1): t += self.r2a[o, h, p].astype(jnp.float32)
            self.r2a[0, h, p] = t.astype(self.r1.dtype)
            return 0
        lax.fori_loop(0, H * Pn, body, 0)
        def body(i, _):
            h, q = i // Qn, i % Qn
            t = self.r1[H + h, pc.p, q].astype(jnp.float32)
            for o in range(Pn - 1): t += self.r2b[o, h, q].astype(jnp.float32)
            self.r2b[0, h, q] = t.astype(self.r1.dtype)
            return 0
        lax.fori_loop(0, H * Qn, body, 0)
        self.d3 = []
        for o in range(1, Pn):
            d = self.copy(("3a", o), self.r2a.at[0, :, (pc.p + o) % Pn], self.r3a.at[o - 1], pc.dev(dp=o)); d.start(); self.d3.append(d)
        for o in range(1, Qn):
            d = self.copy(("3b", o), self.r2b.at[0, :, (pc.q + o) % Qn], self.r3b.at[o - 1], pc.dev(dq=o)); d.start(); self.d3.append(d)
    def s3(self):
        pc = self.pc; Z, Pn, Qn = pc.Z, pc.P, pc.Q; H = Z // 2
        for d in self.d3: d.wait_recv()
        def body(h, _):
            t = self.r2a[0, h, pc.p].astype(jnp.float32)
            for o in range(Pn - 1): t += self.r3a[o, h].astype(jnp.float32)
            self.r3a[0, h] = t.astype(self.r1.dtype)
            t = self.r2b[0, h, pc.q].astype(jnp.float32)
            for o in range(Qn - 1): t += self.r3b[o, h].astype(jnp.float32)
            self.r3b[0, h] = t.astype(self.r1.dtype)
            return 0
        lax.fori_loop(0, H, body, 0)
        self.d4 = []
        for o in range(1, Z):
            zt = (pc.z + o) % Z
            @pl.when(zt < H)
            def _():
                self.copy(("4", o), self.r3a.at[0, zt], self.r4.at[o - 1], pc.dev(dz=o)).start()
            @pl.when(zt >= H)
            def _():
                self.copy(("4", o), self.r3b.at[0, zt - H], self.r4.at[o - 1], pc.dev(dz=o)).start()
            self.d4.append(self.copy(("4", o), self.r3a.at[0, 0], self.r4.at[o - 1], pc.dev(dz=o)))
    def s4(self):
        pc = self.pc; Z, Pn, Qn = pc.Z, pc.P, pc.Q; H = Z // 2
        for d in self.d4: d.wait_recv()
        def fin(first):
            t = first.astype(jnp.float32)
            for o in range(Z - 1): t += self.r4[o].astype(jnp.float32)
            self.put(t)
        @pl.when(pc.z < H)
        def _(): fin(self.r3a[0, pc.z])
        @pl.when(pc.z >= H)
        def _(): fin(self.r3b[0, pc.z - H])
    def drain(self):
        self.d1.wait_send()
        for d in self.d2 + self.d3 + self.d4: d.wait_send()

def rs_kernel(count, nW, chunks, *refs):
    ins, outs = refs[:nW], refs[nW : 2 * nW]
    big, small = refs[2 * nW : 2 * nW + 7], refs[2 * nW + 7 : 2 * nW + 14]
    send, recv, loc = refs[2 * nW + 14 :]
    pc = Place(count)
    barrier(pc)
    ss = []
    wide = chunks[0][4]
    for k, (a, r0, rn, c0, cn) in enumerate(chunks):
        def grad(c, a=a, r0=r0, rn=rn, c0=c0, cn=cn):
            return ins[a].at[:, :, :, c, pl.ds(r0, rn), pl.ds(c0, cn)]
        def put(t, a=a, r0=r0, rn=rn, c0=c0, cn=cn):
            outs[a][pl.ds(r0, rn), pl.ds(c0, cn)] = t
        if cn == wide:
            ss.append(Scatter(pc, grad, put, big, send, recv, loc, k, k))
        else:
            ss.append(Scatter(pc, grad, put, small, send, recv, loc, k, 0))
    n = len(ss)
    for t in range(n + 4):
        for stage in range(5):
            k = t - stage
            if 0 <= k < n:
                getattr(ss[k], f"s{stage}")()
    for s in ss: s.drain()

def scatter_all(grads, shard_shapes, count, cid=1):
    dims = dims_of(count)
    nW = len(grads)
    chunks = chunks_of(shard_shapes, count)
    ns = Scatter.nslots(*dims[:3])
    block = chunks[0][2], chunks[0][4]
    bufs = [pltpu.VMEM(s, jnp.bfloat16) for s in Scatter.buffers(len(chunks) - 1, dims, block, None)]
    bufs += [pltpu.VMEM(s, jnp.float32) for s in Scatter.buffers(1, dims, shard_shapes[-1], None)]
    sems = [pltpu.SemaphoreType.DMA((len(chunks), ns)), pltpu.SemaphoreType.DMA((len(chunks), ns)), pltpu.SemaphoreType.DMA((len(chunks),))]
    return pl.pallas_call(
        functools.partial(rs_kernel, count, nW, chunks),
        out_shape=[jax.ShapeDtypeStruct(s, jnp.float32) for s in shard_shapes],
        in_specs=[pl.BlockSpec(memory_space=pl.ANY)] * nW,
        out_specs=[pl.BlockSpec(memory_space=pltpu.VMEM)] * nW,
        scratch_shapes=bufs + sems,
        compiler_params=pltpu.CompilerParams(collective_id=cid, has_side_effects=True, vmem_limit_bytes=60 << 20),
        name="scatter",
    )(*[g.reshape(dims + tuple(s)) for g, s in zip(grads, shard_shapes)])


def from_behind(block, axis, distance):
    devices = range(lax.axis_size(axis))
    route = [(i - distance, i) for i in devices if i - distance in devices]
    return lax.ppermute(block, axis, route)


def as_sent(shard):
    return jax.tree.map(lambda a: a.astype(jnp.bfloat16) if a.dtype == jnp.float32 else a, shard)


def layer_norm(value, gain, shift):
    center = value - jnp.mean(value, axis=-1, keepdims=True)
    spread = jnp.mean(center * center, axis=-1, keepdims=True)
    return center * lax.rsqrt(spread + 1e-06) * gain + shift


def norm_back(value, gain, shift, incoming):
    _, pullback = jax.vjp(layer_norm, value, gain, shift)
    return pullback(incoming)


def gelu_exact(value):
    return jax.nn.gelu(value, approximate=False)


def matmul(left, right):
    return jnp.dot(left, right, preferred_element_type=jnp.float32)


def matmul_nt(left, right):
    return lax.dot_general(
        left, right, (((1,), (1,)), ((), ())), preferred_element_type=jnp.float32
    )


def matmul_tn(left, right):
    return lax.dot_general(
        left, right, (((0,), (0,)), ((), ())), preferred_element_type=jnp.float32
    )


def by_groups(tensor):
    return tensor.reshape(tensor.shape[0], HEADS // 4, 4, HEAD).transpose(1, 0, 2, 3)


def from_groups(tensor):
    return tensor.transpose(1, 0, 2, 3).reshape(tensor.shape[1], HEADS * HEAD)


def masked_scores(block_q, block_k, allowed):
    scores = (
        jnp.einsum("qhe,khe->hqk", block_q, block_k, preferred_element_type=jnp.float32) * 0.125
    )
    return jnp.where(allowed[None], scores, -1e30)


def attend_fwd(query, keys, values, allowed):

    def one_group(parts):
        block_q, block_k, block_v = parts
        scores = masked_scores(block_q, block_k, allowed)
        peak = jnp.max(scores, axis=-1, keepdims=True)
        expo = jnp.exp(scores - peak)
        total = jnp.sum(expo, axis=-1, keepdims=True)
        probs = (expo / total).astype(jnp.bfloat16)
        mixed = jnp.einsum(
            "hqk,khe->qhe", probs, block_v, preferred_element_type=jnp.float32
        ).astype(jnp.bfloat16)
        return (mixed, peak[..., 0] + jnp.log(total[..., 0]))

    mixed, lse = lax.map(one_group, (by_groups(query), by_groups(keys), by_groups(values)))
    return (from_groups(mixed), lse)


def attend_back(query, keys, values, allowed, lse, grad_mix):

    def one_group(parts):
        block_q, block_k, block_v, block_d, block_l = parts
        scores = masked_scores(block_q, block_k, allowed)
        probs = jnp.exp(scores - block_l[..., None])
        grad_prob = jnp.einsum("qhe,khe->hqk", block_d, block_v, preferred_element_type=jnp.float32)
        inner = jnp.sum(probs * grad_prob, axis=-1, keepdims=True)
        grad_scores = (probs * (grad_prob - inner)).astype(jnp.bfloat16)
        grad_q = (
            jnp.einsum("hqk,khe->qhe", grad_scores, block_k, preferred_element_type=jnp.float32)
            * 0.125
        )
        grad_k = (
            jnp.einsum("hqk,qhe->khe", grad_scores, block_q, preferred_element_type=jnp.float32)
            * 0.125
        )
        grad_v = jnp.einsum(
            "hqk,qhe->khe", probs.astype(jnp.bfloat16), block_d, preferred_element_type=jnp.float32
        )
        return (grad_q, grad_k, grad_v)

    grad_q, grad_k, grad_v = lax.map(
        one_group, (by_groups(query), by_groups(keys), by_groups(values), by_groups(grad_mix), lse)
    )
    return (from_groups(grad_q), from_groups(grad_k), from_groups(grad_v))


def on_device_wide(
    tokens_in,
    prompt_states,
    image_ids,
    text_lengths,
    attn_gain,
    attn_shift,
    self_query,
    self_key,
    self_value,
    self_out,
    cross_gain,
    cross_shift,
    cross_query,
    cross_key,
    cross_value,
    cross_out,
    dense_gain,
    dense_shift,
    dense_in,
    dense_out,
    out_grad,
):
    shards = (
        attn_gain,
        attn_shift,
        self_query,
        self_key,
        self_value,
        self_out,
        cross_gain,
        cross_shift,
        cross_query,
        cross_key,
        cross_value,
        cross_out,
        dense_gain,
        dense_shift,
        dense_in,
        dense_out,
    )
    count = lax.axis_size("band")
    gains = (shards[0], shards[1], shards[6], shards[7], shards[12], shards[13])
    packed = jnp.pad(jnp.stack(gains), ((0, 2), (0, 128 - shards[0].shape[0])))
    mats = tuple(shards[i] for i in (2, 3, 4, 5, 8, 9, 10, 11, 14, 15))
    *full, many = gather_all(list(mats) + [packed], count)
    many = many.reshape(count, 8, 128)[:, :6, : shards[0].shape[0]].transpose(1, 0, 2).reshape(6, -1)
    whole = (many[0], many[1], *full[:4], many[2], many[3], *full[4:8], many[4], many[5], *full[8:])
    (
        gain_attn,
        bias_attn,
        full_query,
        full_key,
        full_value,
        full_out,
        gain_cross,
        bias_cross,
        full_cross_query,
        full_cross_key,
        full_cross_value,
        full_cross_out,
        gain_dense,
        bias_dense,
        full_dense_in,
        full_dense_out,
    ) = whole
    device = lax.axis_index("band")
    tok_dev = tokens_in.shape[0]
    rows_dev = tok_dev // ROW_TOK
    text = prompt_states.shape[1]
    padded_ids = jnp.concatenate([jnp.full((rows_dev,), -1, jnp.int32), image_ids])
    window_ids = lax.dynamic_slice_in_dim(padded_ids, device * rows_dev, 2 * rows_dev)
    key_ids = jnp.repeat(window_ids, ROW_TOK, total_repeat_length=2 * tok_dev)
    query_ids = key_ids[tok_dev:]
    key_place = jnp.arange(2 * tok_dev, dtype=jnp.int32)
    query_place = tok_dev + jnp.arange(tok_dev, dtype=jnp.int32)
    self_allowed = (key_ids[None, :] == query_ids[:, None]) & (
        key_place[None, :] <= query_place[:, None]
    )
    padded_len = jnp.concatenate([text_lengths, jnp.zeros((1,), jnp.int32)])
    near_len = lax.dynamic_slice_in_dim(padded_len, device, 2)
    slot_owner = device + jnp.arange(2, dtype=jnp.int32)
    owner_key = jnp.repeat(slot_owner, text, total_repeat_length=2 * text)
    length_key = jnp.repeat(near_len, text, total_repeat_length=2 * text)
    place_key = jnp.tile(jnp.arange(text, dtype=jnp.int32), 2)
    live_owner = owner_key < count
    cross_allowed = (
        (query_ids[:, None] == owner_key[None, :])
        & (place_key < length_key)[None, :]
        & live_owner[None, :]
    )
    tokens = tokens_in.astype(jnp.float32)
    attn_in = layer_norm(
        tokens, gain_attn.astype(jnp.float32), bias_attn.astype(jnp.float32)
    ).astype(jnp.bfloat16)
    query = matmul(attn_in, full_query).astype(jnp.bfloat16)
    key = matmul(attn_in, full_key).astype(jnp.bfloat16)
    value = matmul(attn_in, full_value).astype(jnp.bfloat16)
    before = from_behind((key, value), "band", 1)
    keys_all = jnp.concatenate([before[0], key], 0)
    values_all = jnp.concatenate([before[1], value], 0)
    self_mix, self_lse = attend_fwd(query, keys_all, values_all, self_allowed)
    resid_one = tokens + matmul(self_mix, full_out)
    cross_in = layer_norm(
        resid_one, gain_cross.astype(jnp.float32), bias_cross.astype(jnp.float32)
    ).astype(jnp.bfloat16)
    cross_q = matmul(cross_in, full_cross_query).astype(jnp.bfloat16)
    own_states = prompt_states[0]
    own_pair = (
        matmul(own_states, full_cross_key).astype(jnp.bfloat16),
        matmul(own_states, full_cross_value).astype(jnp.bfloat16),
    )
    next_pair = from_behind((own_pair[0], own_pair[1]), "band", -1)
    prompt_key = jnp.concatenate([own_pair[0], next_pair[0]], 0)
    prompt_value = jnp.concatenate([own_pair[1], next_pair[1]], 0)
    cross_mix, cross_lse = attend_fwd(cross_q, prompt_key, prompt_value, cross_allowed)
    resid_two = resid_one + matmul(cross_mix, full_cross_out)
    dense_x = layer_norm(
        resid_two, gain_dense.astype(jnp.float32), bias_dense.astype(jnp.float32)
    ).astype(jnp.bfloat16)
    hidden = matmul(dense_x, full_dense_in)
    act = gelu_exact(hidden).astype(jnp.bfloat16)
    block_out = (resid_two + matmul(act, full_dense_out)).astype(jnp.bfloat16)
    grad_out = out_grad.astype(jnp.float32)
    grad_dense_out = matmul_tn(act, out_grad)
    grad_act = matmul_nt(out_grad, full_dense_out)
    _, gelu_pull = jax.vjp(gelu_exact, hidden)
    grad_hidden = gelu_pull(grad_act)[0].astype(jnp.bfloat16)
    grad_dense_in = matmul_tn(dense_x, grad_hidden)
    grad_dense_x = matmul_nt(grad_hidden, full_dense_in)
    grad_resid, grad_dense_gain, grad_dense_shift = norm_back(
        resid_two, gain_dense.astype(jnp.float32), bias_dense.astype(jnp.float32), grad_dense_x
    )
    grad_resid_two = grad_out + grad_resid
    dense_local = (grad_dense_gain, grad_dense_shift, grad_dense_in, grad_dense_out)
    branch_two = grad_resid_two.astype(jnp.bfloat16)
    grad_cross_out = matmul_tn(cross_mix, branch_two)
    grad_cross_mix = matmul_nt(branch_two, full_cross_out).astype(jnp.bfloat16)
    grad_cq, grad_pk, grad_pv = attend_back(
        cross_q, prompt_key, prompt_value, cross_allowed, cross_lse, grad_cross_mix
    )
    back_pair = from_behind((as_sent(grad_pk[text:]), as_sent(grad_pv[text:])), "band", 1)
    grad_pk_low = (grad_pk[:text] + back_pair[0]).astype(jnp.bfloat16)
    grad_pv_low = (grad_pv[:text] + back_pair[1]).astype(jnp.bfloat16)
    grad_cross_key = matmul_tn(own_states, grad_pk_low)
    grad_cross_value = matmul_tn(own_states, grad_pv_low)
    grad_prompt = (
        matmul_nt(grad_pk_low, full_cross_key) + matmul_nt(grad_pv_low, full_cross_value)
    )[None]
    grad_cq_low = grad_cq.astype(jnp.bfloat16)
    grad_cross_query = matmul_tn(cross_in, grad_cq_low)
    grad_cross_in = matmul_nt(grad_cq_low, full_cross_query)
    grad_resid, grad_cross_gain, grad_cross_shift = norm_back(
        resid_one, gain_cross.astype(jnp.float32), bias_cross.astype(jnp.float32), grad_cross_in
    )
    grad_resid_one = grad_resid_two + grad_resid
    cross_local = (
        grad_cross_gain,
        grad_cross_shift,
        grad_cross_query,
        grad_cross_key,
        grad_cross_value,
        grad_cross_out,
    )
    branch_one = grad_resid_one.astype(jnp.bfloat16)
    grad_self_out = matmul_tn(self_mix, branch_one)
    grad_self_mix = matmul_nt(branch_one, full_out).astype(jnp.bfloat16)
    grad_q, grad_keys_all, grad_values_all = attend_back(
        query, keys_all, values_all, self_allowed, self_lse, grad_self_mix
    )
    back_kv = from_behind(
        (as_sent(grad_keys_all[:tok_dev]), as_sent(grad_values_all[:tok_dev])), "band", -1
    )
    grad_k = grad_keys_all[tok_dev:] + back_kv[0]
    grad_v = grad_values_all[tok_dev:] + back_kv[1]
    grad_q_low = grad_q.astype(jnp.bfloat16)
    grad_k_low = grad_k.astype(jnp.bfloat16)
    grad_v_low = grad_v.astype(jnp.bfloat16)
    grad_self_query = matmul_tn(attn_in, grad_q_low)
    grad_self_key = matmul_tn(attn_in, grad_k_low)
    grad_self_value = matmul_tn(attn_in, grad_v_low)
    grad_attn_in = (
        matmul_nt(grad_q_low, full_query)
        + matmul_nt(grad_k_low, full_key)
        + matmul_nt(grad_v_low, full_value)
    )
    grad_resid, grad_attn_gain, grad_attn_shift = norm_back(
        tokens, gain_attn.astype(jnp.float32), bias_attn.astype(jnp.float32), grad_attn_in
    )
    grad_tokens = grad_resid_one + grad_resid
    self_local = (
        grad_attn_gain,
        grad_attn_shift,
        grad_self_query,
        grad_self_key,
        grad_self_value,
        grad_self_out,
    )
    locals_ = self_local + cross_local + dense_local
    vecs = jnp.stack([locals_[i] for i in (0, 1, 6, 7, 12, 13)])
    width = vecs.shape[1] // count
    vecs = vecs.reshape(6, count, width).transpose(1, 0, 2)
    vecs = jnp.pad(vecs, ((0, 0), (0, 2), (0, 128 - width))).reshape(count * 8, 128)
    order = (2, 3, 4, 5, 8, 9, 10, 11, 14, 15)
    mats = [locals_[i].astype(jnp.bfloat16) for i in order]
    *sums, small = scatter_all(mats + [vecs], [(m.shape[0] // count, m.shape[1]) for m in mats] + [(8, 128)], count)
    summed = [None] * 16
    for i, s in zip(order, sums):
        summed[i] = s
    for j, i in enumerate((0, 1, 6, 7, 12, 13)):
        summed[i] = small[j, :width]
    summed = tuple(summed)
    return (block_out, grad_tokens, grad_prompt) + summed


class Moves:
    def __init__(self, pc, send, recv, k):
        self.pc, self.send, self.recv, self.k, self.n, self.sent = pc, send, recv, k, 0, []

    def slot(self):
        self.n += 1
        return self.n - 1

    def make(self, src, dst, dev, s, r):
        return pltpu.make_async_remote_copy(
            src_ref=src, dst_ref=dst, send_sem=self.send.at[self.k, s], recv_sem=self.recv.at[self.k, r],
            device_id=(dev,), device_id_type=MESH)

    def go(self, src, dst, dev):
        s = self.slot()
        d = self.make(src, dst, dev, s, s)
        d.start()
        self.sent.append((d, None))
        return d

    def go_if(self, cond, src, dst, dev, s, r):
        d = self.make(src, dst, dev, s, r)

        @pl.when(cond)
        def _():
            d.start()

        self.sent.append((d, cond))
        return d

    def drain(self):
        for d, cond in self.sent:
            if cond is None:
                d.wait_send()
            else:

                @pl.when(cond)
                def _(d=d):
                    d.wait_send()


class Line:
    def __init__(self, moves, view):
        self.m, self.view = moves, view
        self.slots = {o: moves.slot() for o in (1, 2, 3)}
        self.far = moves.slot()

    def start(self, src=None):
        m, pc, slots = self.m, self.m.pc, self.slots
        here = self.view(pc.z)
        src = here if src is None else src
        self.got = {
            1: m.go_if(pc.z != 3, src, here, pc.dev(dz=1), slots[1], slots[1]),
            2: m.make(src, here, pc.dev(dz=2), slots[2], slots[2]),
            3: m.go_if(pc.z != 0, src, here, pc.dev(dz=3), slots[3], slots[3]),
        }
        self.got[2].start()
        m.sent.append((self.got[2], None))

    def relay(self):
        m, pc = self.m, self.m.pc
        low, high = self.view(0), self.view(3)
        self.got[2].wait_recv()
        m.go_if(pc.z == 2, low, low, pc.dev(dz=1), self.far, self.slots[3])
        m.go_if(pc.z == 1, high, high, pc.dev(dz=3), self.far, self.slots[1])

    def finish(self):
        self.got[1].wait_recv()
        self.got[3].wait_recv()


class GatherZ(Moves):
    def __init__(self, pc, own, out, send, recv, loc, k):
        super().__init__(pc, send, recv, k)
        self.own, self.out, self.loc = own, out, loc

    def keep(self):
        pc = self.pc
        here = self.out(pc.z, pc.p, pc.q, pc.c)
        self.local = pltpu.make_async_copy(self.own, here, self.loc.at[self.k])
        self.local.start()
        return here

    def s0(self):
        pc = self.pc
        self.keep()
        self.line = Line(self, lambda z: self.out(z, pc.p, pc.q, pc.c))
        self.line.start(self.own)

    def s1(self):
        self.line.relay()

    def s2(self):
        pc = self.pc
        self.local.wait()
        self.line.finish()
        v = self.out(slice(None), pc.p, pc.q, pc.c)
        self.ps, self.qs = self.go(v, v, pc.dev(dp=1)), self.go(v, v, pc.dev(dq=1))

    def s3(self):
        pc = self.pc
        self.ps.wait_recv()
        v = self.out(pl.ds(0, 2), 1 - pc.p, pc.q, pc.c)
        self.rs = [self.go(v, v, pc.dev(dq=1))]
        self.qs.wait_recv()
        v = self.out(pl.ds(2, 2), pc.p, 1 - pc.q, pc.c)
        self.rs += [self.go(v, v, pc.dev(dp=1))]

    def s4(self):
        for d in self.rs:
            d.wait_recv()
        v = self.out(slice(None), slice(None), slice(None), self.pc.c)
        self.cs = self.go(v, v, self.pc.dev(dc=1))

    def s5(self):
        self.cs.wait_recv()


class GatherP(GatherZ):
    def s0(self):
        pc = self.pc
        here = self.keep()
        h = self.own.shape[0] // 2
        self.a, self.b = pl.ds(0, h), pl.ds(h, h)
        self.xs = [self.go(self.own.at[self.a], here.at[self.a], pc.dev(dp=1)), self.go(self.own.at[self.b], here.at[self.b], pc.dev(dq=1))]

    def s1(self):
        pc = self.pc
        self.local.wait()
        for d in self.xs:
            d.wait_recv()
        self.lines = [
            Line(self, lambda z: self.out(z, slice(None), pc.q, pc.c).at[:, self.a]),
            Line(self, lambda z: self.out(z, pc.p, slice(None), pc.c).at[:, self.b]),
        ]
        for line in self.lines:
            line.start()

    def s2(self):
        for line in self.lines:
            line.relay()

    def s3(self):
        pc = self.pc
        for line in self.lines:
            line.finish()
        va = self.out(slice(None), slice(None), pc.q, pc.c).at[:, :, self.a]
        vb = self.out(slice(None), pc.p, slice(None), pc.c).at[:, :, self.b]
        self.rs = [self.go(va, va, pc.dev(dq=1)), self.go(vb, vb, pc.dev(dp=1))]


def add_to(ref, *others):
    total = ref[...].astype(jnp.float32)
    for other in others:
        total += other[...].astype(jnp.float32)
    ref[...] = total.astype(ref.dtype)


class LineSum:
    def __init__(self, moves, block, came, joined):
        self.m, self.block, self.came, self.joined = moves, block, came, joined
        self.slots = {o: moves.slot() for o in (1, 2, 3)}
        self.far = moves.slot()
        self.outer = (moves.pc.z == 0) | (moves.pc.z == 3)

    def start(self):
        m, pc, slots = self.m, self.m.pc, self.slots
        first, last = pc.z == 0, pc.z == 3
        m.go_if(first, self.block(3), self.joined, pc.dev(dz=1), self.far, self.far)
        m.go_if(last, self.block(0), self.joined, pc.dev(dz=3), self.far, self.far)
        self.two = self.block((pc.z + 2) % 4)
        self.got = {
            1: m.go_if(pc.z != 3, self.block((pc.z + 1) % 4), self.came.at[0], pc.dev(dz=1), slots[1], slots[1]),
            2: m.go_if(self.outer, self.two, self.came.at[1], pc.dev(dz=2), slots[2], slots[2]),
            3: m.go_if(pc.z != 0, self.block((pc.z + 3) % 4), self.came.at[2], pc.dev(dz=3), slots[3], slots[3]),
        }

    def relay(self):
        m, pc = self.m, self.m.pc
        inner = (pc.z == 1) | (pc.z == 2)
        d = m.make(self.two, self.joined, pc.dev(dz=1), self.far, self.far)

        @pl.when(inner)
        def _():
            d.wait_recv()
            add_to(self.two, self.joined)

        m.go_if(inner, self.two, self.came.at[1], pc.dev(dz=2), self.slots[2], self.slots[2])

    def finish(self, use):
        pc = self.m.pc
        own = self.block(pc.z)
        self.got[2].wait_recv()

        @pl.when(pc.z == 0)
        def _():
            self.got[3].wait_recv()
            use(own, self.came.at[1], self.came.at[2])

        @pl.when(pc.z == 3)
        def _():
            self.got[1].wait_recv()
            use(own, self.came.at[0], self.came.at[1])

        @pl.when((pc.z == 1) | (pc.z == 2))
        def _():
            self.got[1].wait_recv()
            self.got[3].wait_recv()
            use(own, self.came.at[0], self.came.at[1], self.came.at[2])


class Sum(Moves):
    def __init__(self, pc, grad, put, r1, bufs, send, recv, k, credit=None, waits=False, gives=False):
        super().__init__(pc, send, recv, k)
        self.grad, self.put, self.r1, self.bufs = grad, put, r1, bufs
        self.credit, self.waits, self.gives = credit, waits, gives

    def others(self):
        pc = self.pc
        out = [(0, 0, pc.dev(dc=1)), (1, 1, pc.dev(dq=1)), (2, 2, pc.dev(dp=1))]
        return out + [(2 + 4 - o, 2 + o, pc.dev(dz=o)) for o in (1, 2, 3)]

    def s0(self):
        pc = self.pc
        if self.waits:
            for _, mine, _ in self.others():
                pl.semaphore_wait(self.credit.at[mine], 1)
        s = self.slot()
        self.d1 = self.make(self.grad(1 - pc.c), self.r1, pc.dev(dc=1), s, s)
        self.d1.start()

    def with_sibling(self):
        self.d1.wait()
        own = self.grad(self.pc.c)

        def body(i, _):
            at = i // 4, (i // 2) % 2, i % 2
            add_to(self.r1.at[at], own.at[at])
            return 0

        lax.fori_loop(0, 16, body, 0)

    def s6(self):
        self.drain()
        if self.gives:
            for theirs, _, dev in self.others():
                pl.semaphore_signal(self.credit.at[theirs], inc=1, device_id=(dev,), device_id_type=MESH)


class SumZ(Sum):
    @staticmethod
    def buffers(n, block):
        return [(n, 2, 2) + block, (n, 2, 2) + block, (n, 4) + block, (n, 3) + block, (n,) + block]

    def s1(self):
        pc = self.pc
        self.with_sibling()
        self.a, self.b, self.r3, self.r4, self.rx = self.bufs
        self.d2 = [
            self.go(self.r1.at[pl.ds(0, 2), :, 1 - pc.q], self.a, pc.dev(dq=1)),
            self.go(self.r1.at[pl.ds(2, 2), 1 - pc.p], self.b, pc.dev(dp=1)),
        ]

    def s2(self):
        pc = self.pc
        for d in self.d2:
            d.wait_recv()

        def body(i, _):
            h, e = i // 2, i % 2
            add_to(self.a.at[h, e], self.r1.at[h, e, pc.q])
            add_to(self.b.at[h, e], self.r1.at[2 + h, pc.p, e])
            return 0

        lax.fori_loop(0, 4, body, 0)
        self.d3 = [
            self.go(self.a.at[:, 1 - pc.p], self.r3.at[pl.ds(0, 2)], pc.dev(dp=1)),
            self.go(self.b.at[:, 1 - pc.q], self.r3.at[pl.ds(2, 2)], pc.dev(dq=1)),
        ]

    def s3(self):
        pc = self.pc
        for d in self.d3:
            d.wait_recv()

        def body(h, _):
            add_to(self.r3.at[h], self.a.at[h, pc.p])
            add_to(self.r3.at[2 + h], self.b.at[h, pc.q])
            return 0

        lax.fori_loop(0, 2, body, 0)
        self.line = LineSum(self, lambda z: self.r3.at[z], self.r4, self.rx)
        self.line.start()

    def s4(self):
        self.line.relay()

    def s5(self):
        def use(own, *came):
            total = own[...].astype(jnp.float32)
            for c in came:
                total += c[...].astype(jnp.float32)
            self.put(slice(None), total)

        self.line.finish(use)


class SumP(Sum):
    @staticmethod
    def buffers(n, block):
        half = (block[0] // 2, block[1])
        pair = [(n, 4, 2) + half, (n, 3, 2) + half, (n, 2) + half, (n,) + half]
        return pair + pair

    def s1(self):
        pc = self.pc
        self.with_sibling()
        h = self.r1.shape[3] // 2
        self.half = pl.ds(0, h), pl.ds(h, h)
        self.sides = self.bufs[:4], self.bufs[4:]
        self.d2 = [
            self.go(self.r1.at[:, :, 1 - pc.q, self.half[0]], self.sides[0][0], pc.dev(dq=1)),
            self.go(self.r1.at[:, 1 - pc.p, :, self.half[1]], self.sides[1][0], pc.dev(dp=1)),
        ]

    def s2(self):
        pc = self.pc
        for d in self.d2:
            d.wait_recv()
        a, b = self.sides[0][0], self.sides[1][0]

        def body(i, _):
            z, e = i // 2, i % 2
            add_to(a.at[z, e], self.r1.at[z, e, pc.q, self.half[0]])
            add_to(b.at[z, e], self.r1.at[z, pc.p, e, self.half[1]])
            return 0

        lax.fori_loop(0, 8, body, 0)
        self.lines = [LineSum(self, lambda z, s=s: s[0].at[z], s[1], s[2]) for s in self.sides]
        for line in self.lines:
            line.start()

    def s3(self):
        for line in self.lines:
            line.relay()

    def s4(self):
        pc = self.pc
        for line in self.lines:
            line.finish(add_to)
        a, b = self.sides[0][0], self.sides[1][0]
        self.d3 = [
            self.go(a.at[pc.z, 1 - pc.p], self.sides[0][3], pc.dev(dp=1)),
            self.go(b.at[pc.z, 1 - pc.q], self.sides[1][3], pc.dev(dq=1)),
        ]

    def s5(self):
        pc = self.pc
        for d in self.d3:
            d.wait_recv()
        for s, mine, at in zip(self.sides, (pc.p, pc.q), self.half):
            self.put(at, s[0][pc.z, mine].astype(jnp.float32) + s[3][...].astype(jnp.float32))


BF = jnp.bfloat16
F32 = jnp.float32
NN = (((1,), (0,)), ((), ()))
NT = (((1,), (1,)), ((), ()))
TN = (((0,), (0,)), ((), ()))
SCALE = 0.125 * 1.4426950408889634
FWD_NAMES = ("q", "k", "v", "o", "cq", "ck", "cv", "co", "di", "do")


def named(r, prefix):
    return [getattr(r, prefix + m) for m in FWD_NAMES]


def dot(left, right, form):
    return lax.dot_general(left, right, form, preferred_element_type=F32)


def tiles(total, step, body):
    if total == step:
        body(0)
    else:
        def one(i, _):
            body(pl.multiple_of(i * step, step))
            return 0

        lax.fori_loop(0, total // step, one, 0)


def product(left, right, form, put, step=512):
    wide = right.shape[0] if form is NT else right.shape[1]

    def one(off):
        part = right[pl.ds(off, step), :] if form is NT else right[:, pl.ds(off, step)]
        put(off, dot(left(), part, form))

    tiles(wide, step, one)


def store(ref):
    def put(off, value):
        ref[:, pl.ds(off, value.shape[1])] = value.astype(ref.dtype)

    return put


def norm_rows(src, dst, gains, i, step=64):
    def one(r):
        rows = pl.ds(r, step)
        value = src[rows, :].astype(F32)
        center = value - jnp.mean(value, axis=-1, keepdims=True)
        spread = jnp.mean(center * center, axis=-1, keepdims=True)
        unit = center * lax.rsqrt(spread + 1e-06)
        dst[rows, :] = (unit * gains[i : i + 1, :] + gains[i + 1 : i + 2, :]).astype(dst.dtype)

    tiles(src.shape[0], step, one)


def norm_back_rows(src, grad, base, dst, low, gains, i, sums, step=64):
    def one(r):
        rows = pl.ds(r, step)
        value = src[rows, :].astype(F32)
        center = value - jnp.mean(value, axis=-1, keepdims=True)
        spread = jnp.mean(center * center, axis=-1, keepdims=True)
        inverse = lax.rsqrt(spread + 1e-06)
        unit = center * inverse
        came = grad[rows, :]
        inner = came * gains[i : i + 1, :]
        back = (
            inner
            - jnp.mean(inner, axis=-1, keepdims=True)
            - unit * jnp.mean(inner * unit, axis=-1, keepdims=True)
        ) * inverse
        total = base[rows, :].astype(F32) + back
        dst[rows, :] = total
        if low is not None:
            low[rows, :] = total.astype(BF)
        sums[i] += jnp.sum((came * unit).reshape(step // 8, 8, -1), axis=0)
        sums[i + 1] += jnp.sum(came.reshape(step // 8, 8, -1), axis=0)

    tiles(src.shape[0], step, one)


def image_edges(ids, lens, rows_dev):
    me = lax.axis_index("band")
    first = rows_dev * me - rows_dev // 2

    def start_of(i):
        before = jnp.sum(jnp.where(ids[...] < i, 1.0, 0.0), axis=1, keepdims=True)
        return (before - first.astype(F32)) * float(ROW_TOK)

    def length_of(i):
        here = lax.broadcasted_iota(jnp.int32, lens.shape, 1) == i
        return jnp.sum(jnp.where(here, lens[...].astype(F32), 0.0), axis=1, keepdims=True)

    return start_of(me), start_of(me + 1), length_of(me), length_of(me + 1)


def make_masks(ids, lens, bias, cross_bias, rows_dev, text):
    low, high, own_len, next_len = image_edges(ids, lens, rows_dev)
    queries = bias.shape[1]
    halo = bias.shape[0] - queries
    step = 128

    def position(shape, axis, start):
        return (lax.broadcasted_iota(jnp.int32, shape, axis) + start).astype(F32)

    def one(r):
        shape = (step, queries)
        key, query = position(shape, 0, r), position(shape, 1, halo)
        least = jnp.where(query >= high, high, low)
        bias[pl.ds(r, step), :] = jnp.where((key <= query) & (key >= least), 0.0, -1e30)

    tiles(bias.shape[0], step, one)

    def two(r):
        shape = (step, queries)
        key, query = position(shape, 0, r), position(shape, 1, halo)
        later = query >= high
        least = jnp.where(later, float(text), 0.0)
        most = jnp.where(later, text + next_len, own_len)
        cross_bias[pl.ds(r, step), :] = jnp.where((key >= least) & (key < most), 0.0, -1e30)

    tiles(cross_bias.shape[0], step, two)


def mine_of(h, shape, axis):
    place = lax.broadcasted_iota(jnp.int32, shape, axis)
    return place < HEAD if h == 0 else place >= HEAD


def attend_pairs(q, k, v, bias, mix, lse, first, last, spans):
    def one(i, _):
        off = pl.multiple_of(i * 128, 128)
        lanes = pl.ds(off, 128)
        for q0, qn, kw in spans:
            qp, kp, vp = q[q0 : q0 + qn, lanes], k[:kw, lanes], v[:kw, lanes]
            for h in range(2):
                qm = jnp.where(mine_of(h, qp.shape, 1), qp, jnp.zeros_like(qp))
                vm = jnp.where(mine_of(h, vp.shape, 1), vp, jnp.ones_like(vp))
                s = dot(kp, qm, NT) * SCALE + bias[:kw, q0 : q0 + qn]
                peak = jnp.max(s, axis=0, keepdims=True)
                p = jnp.exp2(s - peak).astype(BF)
                got = dot(vm, p, TN)
                total = got[HEAD * (1 - h) : HEAD * (1 - h) + 1]
                own = got[HEAD * h : HEAD * (h + 1)] * (1.0 / total)
                rows = pl.ds(pl.multiple_of(off + HEAD * h, HEAD), HEAD)
                mix[rows, q0 : q0 + qn] = own.astype(BF)
                lse[i, h : h + 1, q0 : q0 + qn] = peak + jnp.log2(total)
        return 0

    lax.fori_loop(first, last, one, 0)


def attend_back_pairs(q, k, v, bias, mix, grad_mix, lse, dq, acc, put, first, last, spans):
    dk, dv = acc.at[0], acc.at[1]

    def one(i, _):
        off = pl.multiple_of(i * 128, 128)
        lanes = pl.ds(off, 128)
        acc[...] = jnp.zeros_like(acc)
        for q0, qn, kw in spans:
            cols = slice(q0, q0 + qn)
            qp, kp, vp = q[cols, lanes], k[:kw, lanes], v[:kw, lanes]
            go, mi = grad_mix[lanes, cols], mix[lanes, cols]
            dqt = jnp.zeros((128, qn), F32)
            for h in range(2):
                qm = jnp.where(mine_of(h, qp.shape, 1), qp, jnp.zeros_like(qp))
                km = jnp.where(mine_of(h, kp.shape, 1), kp, jnp.zeros_like(kp))
                gm = jnp.where(mine_of(h, go.shape, 0), go, jnp.zeros_like(go))
                inner = jnp.sum(gm.astype(F32) * mi.astype(F32), axis=0, keepdims=True)
                s = dot(kp, qm, NT) * SCALE + bias[:kw, cols]
                p = jnp.exp2(s - lse[i, h : h + 1, cols])
                ds = (p * (dot(vp, gm, NN) - inner)).astype(BF)
                dv[:kw, :] += dot(p.astype(BF), gm, NT)
                dk[:kw, :] += dot(ds, qm, NN)
                dqt += dot(km, ds, TN)
            dq[cols, lanes] = jnp.transpose(dqt * 0.125).astype(BF)
        put(lanes, dk, dv)
        return 0

    lax.fori_loop(first, last, one, 0)


class Copies:
    def __init__(self, sem):
        self.sem, self.used = sem, 0

    def start(self, src, dst):
        d = pltpu.make_async_copy(src, dst, self.sem.at[self.used])
        self.used += 1
        assert self.used <= self.sem.shape[0]
        d.start()
        return d


class Weights:
    def __init__(self, copies, slots, entries):
        self.copies, self.slots, self.entries = copies, slots, entries
        self.begun, self.used, self.live = 0, 0, {}

    def pump(self, done):
        while (
            self.begun < len(self.entries)
            and self.begun < self.used + self.slots.shape[0]
            and self.entries[self.begun][1] <= done
        ):
            src = self.entries[self.begun][0]
            self.live[self.begun] = self.copies.start(src, self.slots.at[self.begun % self.slots.shape[0]])
            self.begun += 1

    def take(self):
        e = self.used
        assert e < self.begun
        self.live[e].wait()
        return self.slots.at[e % self.slots.shape[0]]

    def free(self):
        self.used += 1


def ring_neighbors(count):
    me = lax.axis_index("band")
    return (me + 1) % count, (me + count - 1) % count


def enter(pc, count):
    sem = pltpu.get_barrier_semaphore()
    who = pc.partners() + list(ring_neighbors(count))
    for d in who:
        pl.semaphore_signal(sem, inc=1, device_id=(d,), device_id_type=MESH)
    pl.semaphore_wait(sem, len(who))


def forward_kernel(count, names, tick_us, *refs):
    r = types.SimpleNamespace(**dict(zip(names, refs)))
    pc = Place(count)
    Z, Pn, Qn = pc.Z, pc.P, pc.Q
    tok = r.tokens.shape[0]
    halo = tok // 2
    text = r.prompt.shape[0]
    copies = Copies(r.lsem)
    enter(pc, count)

    def remote(src, dst, i, dev):
        d = pltpu.make_async_remote_copy(
            src_ref=src, dst_ref=dst, send_sem=r.xsend.at[i], recv_sem=r.xrecv.at[i],
            device_id=(dev,), device_id_type=MESH)
        d.start()
        return d

    after, before = ring_neighbors(count)
    edge = [
        remote(r.tokens.at[pl.ds(tok - halo, halo)], r.tok.at[pl.ds(0, halo)], 0, after),
        remote(r.prompt, r.pr.at[pl.ds(text, text)], 1, before),
    ]
    loads = types.SimpleNamespace(
        tok=copies.start(r.tokens, r.tok.at[pl.ds(halo, tok)]),
        pr=copies.start(r.prompt, r.pr.at[pl.ds(0, text)]),
        gout=copies.start(r.gout, r.go),
    )

    shards = named(r, "s_") + [r.s_gains]
    wholes = named(r, "w_") + [r.gg]
    rows = shards[0].shape[0]
    order = [(10, 0, shards[10].shape[0], 0, 128)] + [(a, 0, rows, 0, 1024) for a in range(8)]
    order += [(9, rows * i, rows, 0, 1024) for i in range(shards[9].shape[0] // rows)]
    order += [(8, 0, rows, 1024 * j, 1024) for j in range(shards[8].shape[1] // 1024)]
    parts = shards[9].shape[0] // rows
    at = {n: 1 + a for a, n in enumerate(FWD_NAMES[:8])}
    at["do"], at["di"] = 8 + parts, 9 + parts
    gs = []
    for g, (a, r0, rn, c0, cn) in enumerate(order):
        own = shards[a].at[pl.ds(r0, rn), pl.ds(c0, cn)]
        view = wholes[a] if a == 10 else wholes[a].reshape((Z, Pn, Qn, 2) + shards[a].shape)

        def out(z, p, q, c, view=view, r0=r0, rn=rn, c0=c0, cn=cn):
            return view.at[z, p, q, c, pl.ds(r0, rn), pl.ds(c0, cn)]

        gs.append((GatherP if g % 2 else GatherZ)(pc, own, out, r.send, r.recv, r.loc, g))
    n = len(gs)

    def tick(t):
        for stage in range(6):
            g = t - stage
            if 0 <= g < n:
                getattr(gs[g], f"s{stage}")()

    ff = [(r.w_do.at[pl.ds(1024 * j, 1024)], at["do"]) for j in range(parts)]
    entries = [(w, 1 + a) for a, w in enumerate(wholes[:8])] + ff
    entries += [(r.w_di.at[:, pl.ds(1024 * j, 1024)], at["di"] + j) for j in range(parts)]
    weights = Weights(copies, r.ring, entries)
    saves = []

    def save(dst, src):
        saves.append(copies.start(src, dst))

    spans = [(0, tok // 2, tok), (tok // 2, tok // 2, tok + halo)]
    cross_spans = [(0, tok, 2 * text)]

    def t_masks():
        make_masks(r.ids, r.lens, r.bias, r.cbias, tok // ROW_TOK, text)

    def t_norm():
        width = 1024 // count
        per = 128 // width
        for g in range(8):
            total = jnp.zeros((8, 128), F32)
            for d in range(g * per, (g + 1) * per):
                c, qq, pp, zz = d % 2, (d // 2) % Qn, (d // (2 * Qn)) % Pn, d // (2 * Qn * Pn)
                total += r.gg[zz, pp, qq, c].astype(F32)
            r.gf[:, 128 * g : 128 * (g + 1)] = total
        save(r.o_gf, r.gf)
        loads.tok.wait()
        edge[0].wait_recv()
        norm_rows(r.tok, r.ain, r.gf, 0)
        save(r.o_ain, r.ain.at[pl.ds(halo, tok)])

    def t_project(dst, src, lo, out):
        def go():
            w = weights.take()
            product(lambda: src[lo:, :], w, NN, store(dst))
            weights.free()
            save(out, dst)
        return go

    def t_self(a, b):
        def go():
            attend_pairs(r.q, r.k, r.v, r.bias, r.mix, r.lse, a, b, spans)
            if b == HEADS // 2:
                save(r.o_mix, r.mix)
                save(r.o_lse, r.lse)
        return go

    def t_out():
        w = weights.take()

        def put(off, value):
            cols = pl.ds(off, value.shape[1])
            r.res1[:, cols] = r.tok[halo:, cols].astype(F32) + value

        product(lambda: r.mix[...], w, TN, put)
        weights.free()
        save(r.o_res1, r.res1)
        norm_rows(r.res1, r.cin, r.gf, 2)
        save(r.o_cin, r.cin)

    def t_prompt():
        loads.pr.wait()
        edge[1].wait_recv()

    def t_cross(a, b):
        def go():
            attend_pairs(r.cq, r.pk, r.pv, r.cbias, r.cmix, r.clse, a, b, cross_spans)
            if b == HEADS // 2:
                save(r.o_cmix, r.cmix)
                save(r.o_clse, r.clse)
        return go

    def t_cross_out():
        w = weights.take()

        def put(off, value):
            cols = pl.ds(off, value.shape[1])
            r.res2[:, cols] = r.res1[:, cols] + value

        product(lambda: r.cmix[...], w, TN, put)
        weights.free()
        save(r.o_res2, r.res2)
        norm_rows(r.res2, r.dx, r.gf, 4)
        save(r.o_dx, r.dx)

    def t_grad_act(j):
        def go():
            if j == 0:
                loads.gout.wait()
            w = weights.take()
            product(lambda: r.go[...], w, NT, store(r.ga.at[pl.ds(j * tok, tok)]))
            weights.free()
        return go

    def t_hidden(j):
        def go():
            w = weights.take()
            product(lambda: r.dx[...], w, NN, store(r.hid))

            def one(a):
                here, there = pl.ds(a, 16), pl.ds(j * tok + a, 16)
                value = r.hid[here, :]
                share = 0.5 + 0.5 * lax.erf(value * 0.7071067811865476)
                slope = share + value * (jnp.exp(value * value * -0.5) * 0.3989422804014327)
                r.act[there, :] = (value * share).astype(BF)
                r.gh[there, :] = (r.ga[there, :] * slope).astype(BF)

            tiles(tok, 16, one)
            mine = pl.ds(j * tok, tok)
            weights.free()
            save(r.o_act.at[mine], r.act.at[mine])
            save(r.o_gh.at[mine], r.gh.at[mine])
        return go

    half = HEADS // 2
    tasks = [(-1, 2, t_masks), (0, 6, t_norm), (at["q"], 2.5, t_project(r.q, r.ain, halo, r.o_q)),
             (at["k"], 4, t_project(r.k, r.ain, 0, r.o_k)), (at["v"], 4, t_project(r.v, r.ain, 0, r.o_v))]
    tasks += [(at["v"], 3.5, t_self(a, a + 2)) for a in range(0, half, 2)]
    tasks += [(at["o"], 3, t_out), (at["cq"], 1.5, t_project(r.cq, r.cin, 0, r.o_cq)), (-1, 0, t_prompt),
              (at["ck"], 1, t_project(r.pk, r.pr, 0, r.o_pk)), (at["cv"], 1, t_project(r.pv, r.pr, 0, r.o_pv)),
              (at["cv"], 4, t_cross(0, 4)), (at["cv"], 4, t_cross(4, 8)), (at["co"], 4, t_cross_out)]
    tasks += [(at["do"], 1.5, t_grad_act(j)) for j in range(parts)]
    tasks += [(at["di"] + j, 3.5, t_hidden(j)) for j in range(parts)]
    for t in range(n + 5):
        tick(t)
        weights.pump(t - 5)
        spent = 0
        while tasks and (tasks[0][0] <= t - 5 or tasks[0][0] < 0) and spent < tick_us:
            _, cost, go = tasks.pop(0)
            go()
            spent += cost
            weights.pump(t - 5)
    for _, _, go in tasks:
        go()
        weights.pump(n)
    for g in gs:
        g.drain()
    for d in edge:
        d.wait_send()
    for d in saves:
        d.wait()


def forward(args, gains, ids, lens, count):
    tokens, prompt, gout, mats = args
    tok, text = tokens.shape[0], prompt.shape[0]
    halo = tok // 2
    dims = dims_of(count)
    parts = mats[9].shape[0] // mats[0].shape[0]
    chunks = 9 + 2 * parts
    small = dict(s_gains=gains, tokens=tokens, prompt=prompt, gout=gout, ids=ids, lens=lens)
    names = ["s_" + m for m in FWD_NAMES] + list(small)
    outs = {"w_" + m: (w.shape[0] * count, w.shape[1], BF) for m, w in zip(FWD_NAMES, mats)}
    outs |= dict(
        o_gf=(8, 1024, F32), o_ain=(tok, 1024, BF), o_q=(tok, 1024, BF), o_k=(tok + halo, 1024, BF),
        o_v=(tok + halo, 1024, BF), o_mix=(1024, tok, BF), o_lse=(HEADS // 2, 2, tok, F32), o_res1=(tok, 1024, F32),
        o_cin=(tok, 1024, BF), o_cq=(tok, 1024, BF), o_pk=(2 * text, 1024, BF), o_pv=(2 * text, 1024, BF),
        o_cmix=(1024, tok, BF), o_clse=(HEADS // 2, 2, tok, F32), o_res2=(tok, 1024, F32), o_dx=(tok, 1024, BF),
        o_act=(parts * tok, 1024, BF), o_gh=(parts * tok, 1024, BF),
    )
    scratch = dict(
        tok=(tok + halo, 1024, BF), ain=(tok + halo, 1024, BF), q=(tok, 1024, BF), k=(tok + halo, 1024, BF),
        v=(tok + halo, 1024, BF), bias=(tok + halo, tok, F32), mix=(1024, tok, BF), lse=(HEADS // 2, 2, tok, F32),
        res1=(tok, 1024, F32), cin=(tok, 1024, BF), cq=(tok, 1024, BF), pr=(2 * text, 1024, BF),
        pk=(2 * text, 1024, BF), pv=(2 * text, 1024, BF), cbias=(2 * text, tok, F32), cmix=(1024, tok, BF),
        clse=(HEADS // 2, 2, tok, F32), res2=(tok, 1024, F32), dx=(tok, 1024, BF),
        ga=(parts * tok, 1024, F32), act=(parts * tok, 1024, BF), gh=(parts * tok, 1024, BF), hid=(tok, 1024, F32),
        go=(tok, 1024, BF), ring=(4, 1024, 1024, BF),
        gf=(8, 1024, F32), gg=dims + (8, 128, BF),
    )
    ns = 16
    sems = dict(send=(chunks, ns), recv=(chunks, ns), loc=(chunks,), xsend=(2,), xrecv=(2,), lsem=(64,))
    every = names + list(outs) + list(scratch) + list(sems)
    got = pl.pallas_call(
        functools.partial(forward_kernel, count, every, 4),
        out_shape=[jax.ShapeDtypeStruct(s[:-1], s[-1]) for s in outs.values()],
        in_specs=[pl.BlockSpec(memory_space=pl.ANY)] * 14 + [pl.BlockSpec(memory_space=pltpu.VMEM)] * 2,
        out_specs=[pl.BlockSpec(memory_space=pl.ANY)] * len(outs),
        scratch_shapes=[pltpu.VMEM(s[:-1], s[-1]) for s in scratch.values()]
        + [pltpu.SemaphoreType.DMA(s) for s in sems.values()],
        compiler_params=pltpu.CompilerParams(collective_id=0, has_side_effects=True, vmem_limit_bytes=62 << 20),
        name="layer_forward",
    )(*mats, *small.values())
    return dict(zip(outs, got))


def backward_kernel(count, names, slots, tick_us, *refs):
    r = types.SimpleNamespace(**dict(zip(names, refs)))
    pc = Place(count)
    Z, Pn, Qn = pc.Z, pc.P, pc.Q
    tok = r.tokens.shape[0]
    halo = tok // 2
    text = r.prompt.shape[0]
    parts = r.o_act.shape[0] // tok
    half = HEADS // 2
    copies = Copies(r.lsem)
    load = copies.start
    a2, g2 = r.act, r.gh
    L = types.SimpleNamespace(
        dx=load(r.o_dx, r.dx), gh=load(r.o_gh, g2), act=load(r.o_act, a2),
        go=load(r.gout, r.go), gf=load(r.o_gf, r.gf), res2=load(r.o_res2, r.xin),
        cmix=load(r.o_cmix, r.mix), pr=load(r.prompt, r.pr), lse=load(r.o_lse, r.lse), clse=load(r.o_clse, r.clse))
    enter(pc, count)
    after, before = ring_neighbors(count)

    def remote(src, dst, i, dev):
        d = pltpu.make_async_remote_copy(
            src_ref=src, dst_ref=dst, send_sem=r.xsend.at[i], recv_sem=r.xrecv.at[i],
            device_id=(dev,), device_id_type=MESH)
        d.start()
        return d

    blk = r.r1.shape[4]
    chunks = []
    nring = 9 + 2 * parts
    zbufs = [getattr(r, "z%d" % i) for i in range(5)]
    pbufs = [getattr(r, "p%d" % i) for i in range(8)]
    sum_slots = r.grads

    def chunk(grad, put, wide=1024):
        g = len(chunks)
        slot = g % slots

        def part(ref, s):
            return ref.at[(s,) + (slice(None),) * (len(ref.shape) - 2) + (pl.ds(0, wide),)]

        kind, bufs = (SumP, pbufs) if g % 2 else (SumZ, zbufs)
        r1 = part(r.r1, slot)
        chunks.append(
            kind(pc, grad, put, r1, [part(x, slot // 2) for x in bufs], r.send, r.recv, g, r.credit, g >= slots, g + slots < nring))
        return g

    def block_view(ref, rows):
        return ref.reshape(Z, Pn, Qn, 2, rows, 1024)

    def putter(first, c0=0):
        def put(at, t):
            base = first if at == slice(None) else first + at.start
            r.g_all[base : base + t.shape[0], c0 : c0 + t.shape[1]] = t

        return put

    ready, active, summed = [], [], set()
    holder = [[] for _ in range(sum_slots.shape[0])]
    turn = [0]

    def tick():
        for item in sorted(active, key=lambda x: x[0] % 6):
            stage, g = item
            getattr(chunks[g], f"s{stage}")()
            if stage == 1:
                summed.add(g)
            item[0] += 1
        active[:] = [x for x in active if x[0] <= 6]
        if ready:
            g = ready.pop(0)
            chunks[g].s0()
            active.append([1, g])

    def until(gs):
        while not all(g in summed for g in gs):
            tick()

    def grad_chunk(first, form, left, right, cut=1):
        s = turn[0] % len(holder)
        turn[0] += 1
        until(holder[s])
        ref = sum_slots.at[s]
        view = block_view(ref, blk)
        wide = 1024 // cut
        holder[s] = []
        for i in range(cut):
            cols = pl.ds(wide * i, wide)
            product(left, right.at[:, cols], form, store(ref.at[:, cols]))
            g = chunk(lambda c, cols=cols: view.at[:, :, :, c, :, cols], putter(first, wide * i), wide)
            holder[s].append(g)
            ready.append(g)

    entries = [(r.w_di.at[:, pl.ds(1024 * j, 1024)], 0) for j in range(parts)] + [(r.w_do.at[pl.ds(1024 * j, 1024)], 0) for j in range(parts)]
    entries += [(r.w_co, 0), (r.w_cq, 0), (r.w_o, 0), (r.w_ck, 0), (r.w_cv, 0), (r.w_q, 0), (r.w_k, 0), (r.w_v, 0)]
    weights = Weights(copies, r.ring, entries)
    weights.pump(0)
    spans = [(0, tok // 2, tok), (tok // 2, tok // 2, tok + halo)]
    cross_spans = [(0, tok, 2 * text)]
    saves, X = [], {}
    for ref in (r.sums,):
        ref[...] = jnp.zeros_like(ref)

    def t_din(j):
        def go():
            if j == 0:
                L.dx.wait()
                L.gh.wait()
            grad_chunk(blk * (8 + j), TN, lambda: r.dx[...], g2.at[pl.ds(j * tok, tok)])
        return go

    dense = []

    def t_dout(j):
        def go():
            if j == 0:
                L.act.wait()
                L.go.wait()
            here = r.gdo.at[pl.ds(1024 * j, 1024)]
            product(lambda: a2[pl.ds(j * tok, tok), :], r.go, TN, store(here))
            if j == parts - 1:
                view = block_view(r.gdo, blk * parts)
                for i in range(parts):
                    rows = pl.ds(blk * i, blk)
                    g = chunk(lambda c, rows=rows: view.at[:, :, :, c, rows], putter(blk * (8 + parts + i)))
                    dense.append(g)
                    ready.append(g)
        return go

    def area(first, n):
        whole = a2 if first < parts * tok else g2
        return whole.at[pl.ds(first % (parts * tok), n)]

    top = parts * tok
    cq, pk, pv, dq = area(0, tok), area(tok, 2 * text), area(tok + 2 * text, 2 * text), area(2 * tok, tok)
    cin, b2 = area(3 * tok, tok), area(top, tok)
    q, k, v, sq = area(0, tok), area(top + tok, tok + halo), area(top + 2 * tok + halo, tok + halo), area(tok, tok)
    b1, ain = area(2 * tok, tok), area(3 * tok, tok)
    klow, vlow = area(2 * tok, tok), area(top, tok)

    def t_masks():
        make_masks(r.ids, r.lens, r.bias, r.cbias, tok // ROW_TOK, text)

    def t_gdx(j):
        def go():
            w = weights.take()
            mine = pl.ds(j * tok, tok)

            def put(off, value):
                cols = pl.ds(off, value.shape[1])
                if j == 0:
                    r.tmp[:, cols] = value
                else:
                    r.tmp[:, cols] += value

            product(lambda: g2[mine, :], w, NT, put)
            weights.free()
            weights.pump(0)
        return go

    def t_out(j):
        def go():
            if j == 0:
                L.res2.wait()
            w = weights.take()
            mine = pl.ds(j * tok, tok)

            def put(off, value):
                cols = pl.ds(off, value.shape[1])
                total = (r.xin if j == 0 else r.gx)[:, cols] + value
                if j < parts - 1:
                    r.gx[:, cols] = total
                else:
                    r.dx[:, cols] = total.astype(BF)

            product(lambda: a2[mine, :], w, NN, put)
            weights.free()
            weights.pump(0)
            if j == parts - 1:
                X["o"] = copies.start(r.dx, r.o_out)
        return go

    def t_norm2():
        L.cq = load(r.o_cq, cq)
        L.pk = load(r.o_pk, pk)
        L.pv = load(r.o_pv, pv)
        L.cin = load(r.o_cin, cin)
        L.gf.wait()
        norm_back_rows(r.xin, r.tmp, r.go, r.gx, b2, r.gf, 4, r.sums)
        L.res1 = load(r.o_res1, r.xin)

    def t_gco():
        L.cmix.wait()
        grad_chunk(blk * 7, NN, lambda: r.mix[...], b2)

    def t_gcm():
        w = weights.take()
        product(lambda: w[...], b2, NT, store(r.gmt), tok // 2)
        weights.free()
        weights.pump(0)

    def cross_put(lanes, dk, dv):
        for i, (d, s) in enumerate(((dk, 0.125), (dv, 1.0))):
            r.pkv[i, :, lanes] = d[:text, :] * s
            r.psend[i, :, lanes] = (d[text:, :] * s).astype(BF)

    def t_cross(a, b):
        def go():
            if a == 0:
                for d in (L.cq, L.pk, L.pv, L.clse):
                    d.wait()
            attend_back_pairs(cq, pk, pv, r.cbias, r.mix, r.gmt, r.clse, dq, r.kv.at[:, pl.ds(0, 2 * text)], cross_put, a, b, cross_spans)
            if b == half:
                X["p"] = remote(r.psend, r.precv, 0, after)
                L.mix = load(r.o_mix, r.mix)
        return go

    def t_gcq():
        L.cin.wait()
        grad_chunk(blk * 4, TN, lambda: cin[...], dq)

    def t_norm1():
        w = weights.take()
        product(lambda: dq[...], w, NT, store(r.tmp))
        weights.free()
        weights.pump(0)
        L.res1.wait()
        norm_back_rows(r.xin, r.tmp, r.gx, r.gx, b1, r.gf, 2, r.sums)
        L.q, L.k, L.v = load(r.o_q, q), load(r.o_k, k), load(r.o_v, v)

    def t_go():
        L.mix.wait()
        grad_chunk(blk * 3, NN, lambda: r.mix[...], b1)

    def t_gm():
        w = weights.take()
        product(lambda: w[...], b1, NT, store(r.gmt), tok // 2)
        weights.free()
        weights.pump(0)

    hsend = r.gdo.at[pl.ds(0, 2 * halo)].reshape(2, halo, 1024)

    def self_put(lanes, dk, dv):
        for i, (d, s) in enumerate(((dk, 0.125), (dv, 1.0))):
            hsend[i, :, lanes] = (d[:halo, :] * s).astype(BF)
            r.dkv[i, :, lanes] = d[halo:, :] * s

    def t_self(a, b):
        def go():
            if a == 0:
                until(dense)
                for d in (L.q, L.k, L.v, L.lse):
                    d.wait()
            attend_back_pairs(q, k, v, r.bias, r.mix, r.gmt, r.lse, sq, r.kv, self_put, a, b, spans)
            if b == half:
                X["h"] = remote(hsend, r.hrecv, 1, before)
                L.ain = load(r.o_ain, ain)
                X.pop("o").wait()
                L.tokens = load(r.tokens, r.dx)
        return go

    gp = r.xin.at[pl.ds(0, text)]

    def t_prompt():
        X["p"].wait_recv()
        L.pr.wait()
        for i in range(2):
            r.plow[i] = (r.pkv[i] + r.precv[i].astype(F32)).astype(BF)

    def t_gp(i):
        def go():
            if i == 0:
                t_prompt()
            low = r.plow.at[i]
            grad_chunk(blk * (5 + i), TN, lambda: r.pr[...], low)
            w = weights.take()

            def put(off, value):
                cols = pl.ds(off, value.shape[1])
                if i == 0:
                    gp[:, cols] = value
                else:
                    gp[:, cols] += value

            product(lambda: low[...], w, NT, put)
            weights.free()
            weights.pump(0)
            if i == 1:
                saves.append(copies.start(gp, r.o_all.at[pl.ds(tok, text)]))
        return go

    def t_gq():
        L.ain.wait()
        grad_chunk(blk * 0, TN, lambda: ain[...], sq)

    def t_gkv(i):
        def go():
            if i == 0:
                X["h"].wait_recv()
            low = (klow, vlow)[i]
            low[pl.ds(0, halo), :] = r.dkv[i, :halo, :].astype(BF)
            low[pl.ds(halo, halo), :] = (r.dkv[i, halo:, :] + r.hrecv[i].astype(F32)).astype(BF)
            grad_chunk(blk * (1 + i), TN, lambda: ain[...], low, 1 + i)
        return go

    def t_gain(i):
        def go():
            w = weights.take()

            def put(off, value):
                cols = pl.ds(off, value.shape[1])
                if i == 0:
                    r.tmp[:, cols] = value
                else:
                    r.tmp[:, cols] += value

            product(lambda: (sq, klow, vlow)[i][...], w, NT, put)
            weights.free()
            weights.pump(0)
        return go

    def t_norm0():
        L.tokens.wait()
        norm_back_rows(r.dx, r.tmp, r.gx, r.gx, None, r.gf, 0, r.sums)
        saves.append(copies.start(r.gx, r.o_all.at[pl.ds(0, tok)]))

    def t_vecs():
        width = 1024 // count
        per = 128 // width
        for g in range(8):
            lanes = slice(128 * g, 128 * (g + 1))
            tile = jnp.concatenate(
                [jnp.sum(r.sums[i, :, lanes], axis=0, keepdims=True) for i in range(6)] + [jnp.zeros((2, 128), F32)], axis=0)
            for d in range(g * per, (g + 1) * per):
                c, qq, pp, zz = d % 2, (d // 2) % Qn, (d // (2 * Qn)) % Pn, d // (2 * Qn * Pn)
                r.vg[zz, pp, qq, c] = tile

        def put(at, t):
            r.g_vec[...] = t

        bufs = [getattr(r, "v%d" % i) for i in range(6)]
        chunks.append(SumZ(pc, lambda c: r.vg.at[:, :, :, c], put, bufs[0], bufs[1:], r.send, r.recv, len(chunks)))
        ready.append(len(chunks) - 1)

    tasks = [(1.5, t_din(j)) for j in range(parts)] + [(1.5, t_dout(j)) for j in range(parts)]
    tasks += [(1.5, t_gdx(j)) for j in range(parts)] + [(1.5, t_out(j)) for j in range(parts)]
    tasks += [(3, t_norm2), (1.5, t_gco), (1.5, t_gcm), (2, t_masks)] + [(4, t_cross(0, 4)), (4, t_cross(4, 8))]
    tasks += [(1.5, t_gcq), (4, t_norm1), (1.5, t_go), (1.5, t_gm)]
    tasks += [(5, t_self(a, a + 2)) for a in range(0, half, 2)]
    tasks += [(1, t_gp(0)), (1, t_gp(1)), (1.5, t_gq), (2, t_gkv(0)), (2, t_gkv(1))]
    tasks += [(1.5, t_gain(i)) for i in range(3)] + [(3, t_norm0), (0.3, t_vecs)]
    spent = 0
    for cost, go in tasks:
        go()
        spent += cost
        if spent >= tick_us and (ready or active):
            tick()
            spent = 0
    while ready or active:
        tick()
    saves.append(copies.start(r.g_all, r.o_all.at[pl.ds(tok + text, r.g_all.shape[0])]))
    for d in X.values():
        d.wait_send()
    for d in saves:
        d.wait()


def backward(args, held, ids, lens, count):
    tokens, prompt, gout, mats = args
    tok, text = tokens.shape[0], prompt.shape[0]
    halo = tok // 2
    dims = dims_of(count)
    blk = mats[0].shape[0]
    parts = mats[9].shape[0] // blk
    slots = 6
    chunks = 10 + 2 * parts
    weights = (8 + 2 * parts) * blk
    given = dict(tokens=tokens, prompt=prompt, gout=gout) | held | dict(ids=ids, lens=lens)
    outs = dict(o_out=(tok, 1024, BF), o_all=(tok + text + weights, 1024, F32))
    vouts = dict(g_vec=(8, 128, F32))
    block = (blk, 1024)
    scratch = {"z%d" % i: s + (BF,) for i, s in enumerate(SumZ.buffers(slots // 2, block))}
    scratch |= {"p%d" % i: s + (BF,) for i, s in enumerate(SumP.buffers(slots // 2, block))}
    scratch |= {"v%d" % i: s + (F32,) for i, s in enumerate([dims[:3] + (8, 128)] + [s[1:] for s in SumZ.buffers(1, (8, 128))])}
    scratch |= dict(
        r1=(slots,) + dims[:3] + block + (BF,), g_all=(weights, 1024, F32),
        grads=(3, 1024, 1024, BF), gdo=(1024 * parts, 1024, BF), act=(parts * tok, 1024, BF), gh=(parts * tok, 1024, BF),
        ring=(2, 1024, 1024, BF), gx=(tok, 1024, F32), tmp=(tok, 1024, F32), xin=(tok, 1024, F32), dkv=(2, tok, 1024, F32),
        kv=(2, tok + halo, 128, F32), mix=(1024, tok, BF), gmt=(1024, tok, BF), bias=(tok + halo, tok, F32), cbias=(2 * text, tok, F32),
        dx=(tok, 1024, BF), go=(tok, 1024, BF), gf=(8, 1024, F32), pr=(text, 1024, BF), lse=(HEADS // 2, 2, tok, F32),
        clse=(HEADS // 2, 2, tok, F32), hrecv=(2, halo, 1024, BF), psend=(2, text, 1024, BF),
        precv=(2, text, 1024, BF), pkv=(2, text, 1024, F32), plow=(2, text, 1024, BF), sums=(6, 8, 1024, F32), vg=dims + (8, 128, F32))
    sems = dict(send=(chunks, 16), recv=(chunks, 16), xsend=(2,), xrecv=(2,), lsem=(48,))
    every = list(given) + list(outs) + list(vouts) + list(scratch) + list(sems) + ["credit"]
    got = pl.pallas_call(
        functools.partial(backward_kernel, count, every, slots, 6),
        out_shape=[jax.ShapeDtypeStruct(s[:-1], s[-1]) for s in (outs | vouts).values()],
        in_specs=[pl.BlockSpec(memory_space=pl.ANY)] * (len(given) - 2) + [pl.BlockSpec(memory_space=pltpu.VMEM)] * 2,
        out_specs=[pl.BlockSpec(memory_space=pl.ANY)] * len(outs) + [pl.BlockSpec(memory_space=pltpu.VMEM)] * len(vouts),
        scratch_shapes=[pltpu.VMEM(s[:-1], s[-1]) for s in scratch.values()]
        + [pltpu.SemaphoreType.DMA(s) for s in sems.values()] + [pltpu.SemaphoreType.REGULAR((6,))],
        compiler_params=pltpu.CompilerParams(collective_id=1, has_side_effects=True, vmem_limit_bytes=63 << 20),
        name="layer_backward",
    )(*given.values())
    return got


def on_device(
    tokens_in,
    prompt_states,
    image_ids,
    text_lengths,
    attn_gain,
    attn_shift,
    self_query,
    self_key,
    self_value,
    self_out,
    cross_gain,
    cross_shift,
    cross_query,
    cross_key,
    cross_value,
    cross_out,
    dense_gain,
    dense_shift,
    dense_in,
    dense_out,
    out_grad,
):
    mats = (self_query, self_key, self_value, self_out, cross_query, cross_key, cross_value, cross_out, dense_in, dense_out)
    count = lax.axis_size("band")
    blk = mats[0].shape[0]
    if dims_of(count) != (4, 2, 2, 2) or blk % 32:
        return on_device_wide(
            tokens_in,
            prompt_states,
            image_ids,
            text_lengths,
            attn_gain,
            attn_shift,
            self_query,
            self_key,
            self_value,
            self_out,
            cross_gain,
            cross_shift,
            cross_query,
            cross_key,
            cross_value,
            cross_out,
            dense_gain,
            dense_shift,
            dense_in,
            dense_out,
            out_grad,
        )
    width = attn_gain.shape[0]
    per = 128 // width
    place = lax.axis_index("band") % per
    packed = jnp.stack((attn_gain, attn_shift, cross_gain, cross_shift, dense_gain, dense_shift))
    packed = jnp.pad(jnp.tile(packed, (1, per)), ((0, 2), (0, 0)))
    packed = jnp.where(jnp.arange(128, dtype=jnp.int32)[None] // width == place, packed, jnp.zeros_like(packed))
    ids, lens = image_ids[None], text_lengths[None]
    data = (tokens_in, prompt_states[0], out_grad, mats)
    held = forward(data, packed, ids, lens, count)
    block_out, every, vecs = backward(data, held, ids, lens, count)
    vecs = lax.dynamic_slice(vecs, (0, place * width), (8, width))
    tok, text = tokens_in.shape[0], prompt_states.shape[1]
    parts = mats[9].shape[0] // blk
    own = every[tok + text :]
    g = [own[blk * i : blk * (i + 1)] for i in range(8)]
    wide = own[8 * blk : (8 + parts) * blk].reshape(parts, blk, -1).transpose(1, 0, 2).reshape(blk, -1)
    return (
        block_out, every[:tok], every[None, tok : tok + text],
        vecs[0], vecs[1], *g[:4],
        vecs[2], vecs[3], *g[4:],
        vecs[4], vecs[5], wide, own[(8 + parts) * blk :],
    )


def solution(mesh):
    return jax.shard_map(
        on_device,
        mesh=mesh,
        in_specs=(
            P("band", None),
            P("band", None, None),
            P(),
            P(),
            P("band"),
            P("band"),
            P("band", None),
            P("band", None),
            P("band", None),
            P("band", None),
            P("band"),
            P("band"),
            P("band", None),
            P("band", None),
            P("band", None),
            P("band", None),
            P("band"),
            P("band"),
            P("band", None),
            P("band", None),
            P("band", None),
        ),
        out_specs=(
            P("band", None),
            P("band", None),
            P("band", None, None),
            P("band"),
            P("band"),
            P("band", None),
            P("band", None),
            P("band", None),
            P("band", None),
            P("band"),
            P("band"),
            P("band", None),
            P("band", None),
            P("band", None),
            P("band", None),
            P("band"),
            P("band"),
            P("band", None),
            P("band", None),
        ),
        check_vma=False,
    )
```

```python
import functools
import types

import jax
import jax.numpy as jnp
from jax import lax
from jax.experimental import pallas as pl
from jax.experimental.pallas import tpu as pltpu
from jax.sharding import PartitionSpec as P

HEADS = 16
HEAD = 64
ROW_TOK = 32
MESH = pl.DeviceIdType.MESH


def dims_of(count):
    side = 1
    while 2 * (2 * side) ** 2 * 2 <= count:
        side *= 2
    return (count // (2 * side * side), side, side, 2)

class Place:
    def __init__(self, count):
        self.Z, self.P, self.Q, self.C = dims_of(count)
        me = lax.axis_index("band")
        self.c = me % 2
        self.q = (me // 2) % self.Q
        self.p = (me // (2 * self.Q)) % self.P
        self.z = me // (2 * self.Q * self.P)
    def dev(self, dz=0, dp=0, dq=0, dc=0):
        z = (self.z + dz) % self.Z
        p = (self.p + dp) % self.P
        q = (self.q + dq) % self.Q
        c = (self.c + dc) % 2
        return ((z * self.P + p) * self.Q + q) * 2 + c
    def partners(self):
        return ([self.dev(dz=o) for o in range(1, self.Z)] + [self.dev(dp=o) for o in range(1, self.P)]
                + [self.dev(dq=o) for o in range(1, self.Q)] + [self.dev(dc=1)])

def barrier(place):
    sem = pltpu.get_barrier_semaphore()
    who = place.partners()
    for d in who:
        pl.semaphore_signal(sem, inc=1, device_id=(d,), device_id_type=MESH)
    pl.semaphore_wait(sem, len(who))

class Gather:
    def __init__(self, pc, own, out, send, recv, loc, k):
        self.pc, self.own, self.out, self.send, self.recv, self.loc, self.k = pc, own, out, send, recv, loc, k
        Z, Pn, Qn = pc.Z, pc.P, pc.Q
        n = 0
        self.slots = {}
        for o in range(1, Z): self.slots["z", o] = n; n += 1
        for h in range(2):
            for o in range(1, Pn): self.slots["p", h, o] = n; n += 1
            for o in range(1, Qn): self.slots["q", h, o] = n; n += 1
        for o in range(1, Pn):
            for r in range(1, Qn):
                self.slots["pq", o, r] = n; n += 1
                self.slots["qp", o, r] = n; n += 1
        for a in range(Pn):
            for b in range(Qn):
                self.slots["c", a, b] = n; n += 1
        self.count = n
    @staticmethod
    def nslots(Z, Pn, Qn):
        return (Z - 1) + 2 * (Pn - 1 + Qn - 1) + 2 * (Pn - 1) * (Qn - 1) + Pn * Qn
    def copy(self, key, src, dst, dev):
        s = self.slots[key]
        return pltpu.make_async_remote_copy(src_ref=src, dst_ref=dst, send_sem=self.send.at[self.k, s], recv_sem=self.recv.at[self.k, s],
                                            device_id=(dev,), device_id_type=MESH)
    def half(self, h):
        return pl.ds(h * (self.pc.Z // 2), self.pc.Z // 2)
    def s0(self):
        pc = self.pc
        self.local = pltpu.make_async_copy(self.own, self.out(pc.z, pc.p, pc.q, pc.c), self.loc.at[self.k])
        self.local.start()
        self.zs = [self.copy(("z", o), self.own, self.out(pc.z, pc.p, pc.q, pc.c), pc.dev(dz=o)) for o in range(1, pc.Z)]
        for d in self.zs: d.start()
    def s1(self):
        pc = self.pc
        self.local.wait()
        for d in self.zs: d.wait_recv()
        self.ps = {}
        for h in range(2):
            v = self.out(self.half(h), pc.p, pc.q, pc.c)
            for o in range(1, pc.P): self.ps["p", h, o] = self.copy(("p", h, o), v, v, pc.dev(dp=o))
            for o in range(1, pc.Q): self.ps["q", h, o] = self.copy(("q", h, o), v, v, pc.dev(dq=o))
        for o in range(1, pc.P): self.ps["p", 0, o].start()
        for o in range(1, pc.Q): self.ps["q", 1, o].start()
        for o in range(1, pc.P): self.ps["p", 1, o].start()
        for o in range(1, pc.Q): self.ps["q", 0, o].start()
        self.cs = []
        v = self.out(slice(None), pc.p, pc.q, pc.c)
        d = self.copy(("c", 0, 0), v, v, pc.dev(dc=1)); d.start(); self.cs.append(d)
    def s2(self):
        pc = self.pc
        self.rs = []
        for o in range(1, pc.P): self.ps["p", 0, o].wait_recv()
        for o in range(1, pc.P):
            v = self.out(self.half(0), (pc.p - o) % pc.P, pc.q, pc.c)
            for r in range(1, pc.Q):
                d = self.copy(("pq", o, r), v, v, pc.dev(dq=r)); d.start(); self.rs.append(d)
        for r in range(1, pc.Q): self.ps["q", 1, r].wait_recv()
        for r in range(1, pc.Q):
            v = self.out(self.half(1), pc.p, (pc.q - r) % pc.Q, pc.c)
            for o in range(1, pc.P):
                d = self.copy(("qp", o, r), v, v, pc.dev(dp=o)); d.start(); self.rs.append(d)
        for o in range(1, pc.P): self.ps["p", 1, o].wait_recv()
        for o in range(1, pc.P):
            v = self.out(slice(None), (pc.p - o) % pc.P, pc.q, pc.c)
            d = self.copy(("c", o, 0), v, v, pc.dev(dc=1)); d.start(); self.cs.append(d)
        for r in range(1, pc.Q): self.ps["q", 0, r].wait_recv()
        for r in range(1, pc.Q):
            v = self.out(slice(None), pc.p, (pc.q - r) % pc.Q, pc.c)
            d = self.copy(("c", 0, r), v, v, pc.dev(dc=1)); d.start(); self.cs.append(d)
    def s3(self):
        pc = self.pc
        for d in self.rs: d.wait_recv()
        for o in range(1, pc.P):
            for r in range(1, pc.Q):
                v = self.out(slice(None), (pc.p - o) % pc.P, (pc.q - r) % pc.Q, pc.c)
                d = self.copy(("c", o, r), v, v, pc.dev(dc=1)); d.start(); self.cs.append(d)
    def s4(self):
        for d in self.cs: d.wait_recv()
    def drain(self):
        for d in self.zs: d.wait_send()
        for d in self.ps.values(): d.wait_send()
        for d in self.rs: d.wait_send()
        for d in self.cs: d.wait_send()

def chunks_of(shapes, n):
    out = []
    for a, (r, c) in enumerate(shapes):
        base_r = min(s[0] for s in shapes if s[1] >= 1024) if c >= 1024 else r
        if c >= 1024:
            for i in range(0, r, base_r):
                for j in range(0, c, 1024):
                    out.append((a, i, base_r, j, 1024))
        else:
            out.append((a, 0, r, 0, c))
    return out

def ag_kernel(count, nW, chunks, *refs):
    ins, outs = refs[:nW], refs[nW:2 * nW]
    send, recv, loc = refs[2 * nW:]
    pc = Place(count)
    barrier(pc)
    gs = []
    for k, (a, r0, rn, c0, cn) in enumerate(chunks):
        own = ins[a].at[pl.ds(r0, rn), pl.ds(c0, cn)]
        def out(z, p, q, c, a=a, r0=r0, rn=rn, c0=c0, cn=cn):
            return outs[a].at[z, p, q, c, pl.ds(r0, rn), pl.ds(c0, cn)]
        gs.append(Gather(pc, own, out, send, recv, loc, k))
    n = len(gs)
    for t in range(n + 4):
        for stage in range(5):
            k = t - stage
            if 0 <= k < n:
                getattr(gs[k], f"s{stage}")()
    for g in gs: g.drain()

def gather_all(shards, count, cid=0):
    dims = dims_of(count)
    nW = len(shards)
    chunks = chunks_of([s.shape for s in shards], count)
    ns = Gather.nslots(*dims[:3])
    outs = pl.pallas_call(
        functools.partial(ag_kernel, count, nW, chunks),
        out_shape=[jax.ShapeDtypeStruct(dims + s.shape, s.dtype) for s in shards],
        in_specs=[pl.BlockSpec(memory_space=pl.ANY)] * nW,
        out_specs=[pl.BlockSpec(memory_space=pl.ANY)] * nW,
        scratch_shapes=[pltpu.SemaphoreType.DMA((len(chunks), ns)), pltpu.SemaphoreType.DMA((len(chunks), ns)), pltpu.SemaphoreType.DMA((len(chunks),))],
        compiler_params=pltpu.CompilerParams(collective_id=cid, has_side_effects=True),
        name="gather",
    )(*shards)
    return [o.reshape((count * s.shape[0],) + s.shape[1:]) for o, s in zip(outs, shards)]


class Scatter:
    def __init__(self, pc, grad, put, bufs, send, recv, loc, k, kb):
        self.pc, self.grad, self.put, self.send, self.recv, self.loc, self.k, self.kb = pc, grad, put, send, recv, loc, k, kb
        self.own = bufs[0] if bufs[0] is None else bufs[0].at[kb]
        self.r1, self.r2a, self.r2b, self.r3a, self.r3b, self.r4 = [b.at[kb] for b in bufs[1:]]
        Z, Pn, Qn = pc.Z, pc.P, pc.Q
        n = 0
        self.slots = {"c": 0}; n = 1
        for o in range(1, Qn): self.slots["2a", o] = n; n += 1
        for o in range(1, Pn): self.slots["2b", o] = n; n += 1
        for o in range(1, Pn): self.slots["3a", o] = n; n += 1
        for o in range(1, Qn): self.slots["3b", o] = n; n += 1
        for o in range(1, Z): self.slots["4", o] = n; n += 1
    @staticmethod
    def nslots(Z, Pn, Qn):
        return 1 + 2 * (Pn - 1 + Qn - 1) + Z - 1
    @staticmethod
    def buffers(n, dims, block, dtype):
        Z, Pn, Qn = dims[:3]; H = Z // 2
        return [(n, Z, Pn, Qn) + block, (n, Z, Pn, Qn) + block, (n, Qn - 1, H, Pn) + block, (n, Pn - 1, H, Qn) + block,
                (n, Pn - 1, H) + block, (n, Qn - 1, H) + block, (n, Z - 1) + block]
    def copy(self, key, src, dst, dev):
        s = self.slots[key]
        return pltpu.make_async_remote_copy(src_ref=src, dst_ref=dst, send_sem=self.send.at[self.k, s], recv_sem=self.recv.at[self.k, s],
                                            device_id=(dev,), device_id_type=MESH)
    def s0(self):
        pc = self.pc
        self.d1 = self.copy("c", self.grad(1 - pc.c), self.r1, pc.dev(dc=1)); self.d1.start()
        self.l = pltpu.make_async_copy(self.grad(pc.c), self.own, self.loc.at[self.k]); self.l.start()
    def arrive(self):
        self.l.wait(); self.d1.wait_recv()
    def s1(self):
        pc = self.pc; Z, Pn, Qn = pc.Z, pc.P, pc.Q; H = Z // 2
        self.arrive()
        def body(i, _):
            z, p, q = i // (Pn * Qn), (i // Qn) % Pn, i % Qn
            self.r1[z, p, q] = (self.r1[z, p, q].astype(jnp.float32) + self.own[z, p, q].astype(jnp.float32)).astype(self.r1.dtype)
            return 0
        lax.fori_loop(0, Z * Pn * Qn, body, 0)
        self.d2 = []
        for o in range(1, Qn):
            d = self.copy(("2a", o), self.r1.at[pl.ds(0, H), :, (pc.q + o) % Qn], self.r2a.at[o - 1], pc.dev(dq=o)); d.start(); self.d2.append(d)
        for o in range(1, Pn):
            d = self.copy(("2b", o), self.r1.at[pl.ds(H, H), (pc.p + o) % Pn], self.r2b.at[o - 1], pc.dev(dp=o)); d.start(); self.d2.append(d)
    def s2(self):
        pc = self.pc; Z, Pn, Qn = pc.Z, pc.P, pc.Q; H = Z // 2
        for d in self.d2: d.wait_recv()
        def body(i, _):
            h, p = i // Pn, i % Pn
            t = self.r1[h, p, pc.q].astype(jnp.float32)
            for o in range(Qn - 1): t += self.r2a[o, h, p].astype(jnp.float32)
            self.r2a[0, h, p] = t.astype(self.r1.dtype)
            return 0
        lax.fori_loop(0, H * Pn, body, 0)
        def body(i, _):
            h, q = i // Qn, i % Qn
            t = self.r1[H + h, pc.p, q].astype(jnp.float32)
            for o in range(Pn - 1): t += self.r2b[o, h, q].astype(jnp.float32)
            self.r2b[0, h, q] = t.astype(self.r1.dtype)
            return 0
        lax.fori_loop(0, H * Qn, body, 0)
        self.d3 = []
        for o in range(1, Pn):
            d = self.copy(("3a", o), self.r2a.at[0, :, (pc.p + o) % Pn], self.r3a.at[o - 1], pc.dev(dp=o)); d.start(); self.d3.append(d)
        for o in range(1, Qn):
            d = self.copy(("3b", o), self.r2b.at[0, :, (pc.q + o) % Qn], self.r3b.at[o - 1], pc.dev(dq=o)); d.start(); self.d3.append(d)
    def s3(self):
        pc = self.pc; Z, Pn, Qn = pc.Z, pc.P, pc.Q; H = Z // 2
        for d in self.d3: d.wait_recv()
        def body(h, _):
            t = self.r2a[0, h, pc.p].astype(jnp.float32)
            for o in range(Pn - 1): t += self.r3a[o, h].astype(jnp.float32)
            self.r3a[0, h] = t.astype(self.r1.dtype)
            t = self.r2b[0, h, pc.q].astype(jnp.float32)
            for o in range(Qn - 1): t += self.r3b[o, h].astype(jnp.float32)
            self.r3b[0, h] = t.astype(self.r1.dtype)
            return 0
        lax.fori_loop(0, H, body, 0)
        self.d4 = []
        for o in range(1, Z):
            zt = (pc.z + o) % Z
            @pl.when(zt < H)
            def _():
                self.copy(("4", o), self.r3a.at[0, zt], self.r4.at[o - 1], pc.dev(dz=o)).start()
            @pl.when(zt >= H)
            def _():
                self.copy(("4", o), self.r3b.at[0, zt - H], self.r4.at[o - 1], pc.dev(dz=o)).start()
            self.d4.append(self.copy(("4", o), self.r3a.at[0, 0], self.r4.at[o - 1], pc.dev(dz=o)))
    def s4(self):
        pc = self.pc; Z, Pn, Qn = pc.Z, pc.P, pc.Q; H = Z // 2
        for d in self.d4: d.wait_recv()
        def fin(first):
            t = first.astype(jnp.float32)
            for o in range(Z - 1): t += self.r4[o].astype(jnp.float32)
            self.put(t)
        @pl.when(pc.z < H)
        def _(): fin(self.r3a[0, pc.z])
        @pl.when(pc.z >= H)
        def _(): fin(self.r3b[0, pc.z - H])
    def drain(self):
        self.d1.wait_send()
        for d in self.d2 + self.d3 + self.d4: d.wait_send()

def rs_kernel(count, nW, chunks, *refs):
    ins, outs = refs[:nW], refs[nW : 2 * nW]
    big, small = refs[2 * nW : 2 * nW + 7], refs[2 * nW + 7 : 2 * nW + 14]
    send, recv, loc = refs[2 * nW + 14 :]
    pc = Place(count)
    barrier(pc)
    ss = []
    wide = chunks[0][4]
    for k, (a, r0, rn, c0, cn) in enumerate(chunks):
        def grad(c, a=a, r0=r0, rn=rn, c0=c0, cn=cn):
            return ins[a].at[:, :, :, c, pl.ds(r0, rn), pl.ds(c0, cn)]
        def put(t, a=a, r0=r0, rn=rn, c0=c0, cn=cn):
            outs[a][pl.ds(r0, rn), pl.ds(c0, cn)] = t
        if cn == wide:
            ss.append(Scatter(pc, grad, put, big, send, recv, loc, k, k))
        else:
            ss.append(Scatter(pc, grad, put, small, send, recv, loc, k, 0))
    n = len(ss)
    for t in range(n + 4):
        for stage in range(5):
            k = t - stage
            if 0 <= k < n:
                getattr(ss[k], f"s{stage}")()
    for s in ss: s.drain()

def scatter_all(grads, shard_shapes, count, cid=1):
    dims = dims_of(count)
    nW = len(grads)
    chunks = chunks_of(shard_shapes, count)
    ns = Scatter.nslots(*dims[:3])
    block = chunks[0][2], chunks[0][4]
    bufs = [pltpu.VMEM(s, jnp.bfloat16) for s in Scatter.buffers(len(chunks) - 1, dims, block, None)]
    bufs += [pltpu.VMEM(s, jnp.float32) for s in Scatter.buffers(1, dims, shard_shapes[-1], None)]
    sems = [pltpu.SemaphoreType.DMA((len(chunks), ns)), pltpu.SemaphoreType.DMA((len(chunks), ns)), pltpu.SemaphoreType.DMA((len(chunks),))]
    return pl.pallas_call(
        functools.partial(rs_kernel, count, nW, chunks),
        out_shape=[jax.ShapeDtypeStruct(s, jnp.float32) for s in shard_shapes],
        in_specs=[pl.BlockSpec(memory_space=pl.ANY)] * nW,
        out_specs=[pl.BlockSpec(memory_space=pltpu.VMEM)] * nW,
        scratch_shapes=bufs + sems,
        compiler_params=pltpu.CompilerParams(collective_id=cid, has_side_effects=True, vmem_limit_bytes=60 << 20),
        name="scatter",
    )(*[g.reshape(dims + tuple(s)) for g, s in zip(grads, shard_shapes)])


def from_behind(block, axis, distance):
    devices = range(lax.axis_size(axis))
    route = [(i - distance, i) for i in devices if i - distance in devices]
    return lax.ppermute(block, axis, route)


def as_sent(shard):
    return jax.tree.map(lambda a: a.astype(jnp.bfloat16) if a.dtype == jnp.float32 else a, shard)


def layer_norm(value, gain, shift):
    center = value - jnp.mean(value, axis=-1, keepdims=True)
    spread = jnp.mean(center * center, axis=-1, keepdims=True)
    return center * lax.rsqrt(spread + 1e-06) * gain + shift


def norm_back(value, gain, shift, incoming):
    _, pullback = jax.vjp(layer_norm, value, gain, shift)
    return pullback(incoming)


def gelu_exact(value):
    return jax.nn.gelu(value, approximate=False)


def matmul(left, right):
    return jnp.dot(left, right, preferred_element_type=jnp.float32)


def matmul_nt(left, right):
    return lax.dot_general(
        left, right, (((1,), (1,)), ((), ())), preferred_element_type=jnp.float32
    )


def matmul_tn(left, right):
    return lax.dot_general(
        left, right, (((0,), (0,)), ((), ())), preferred_element_type=jnp.float32
    )


def by_groups(tensor):
    return tensor.reshape(tensor.shape[0], HEADS // 4, 4, HEAD).transpose(1, 0, 2, 3)


def from_groups(tensor):
    return tensor.transpose(1, 0, 2, 3).reshape(tensor.shape[1], HEADS * HEAD)


def masked_scores(block_q, block_k, allowed):
    scores = (
        jnp.einsum("qhe,khe->hqk", block_q, block_k, preferred_element_type=jnp.float32) * 0.125
    )
    return jnp.where(allowed[None], scores, -1e30)


def attend_fwd(query, keys, values, allowed):

    def one_group(parts):
        block_q, block_k, block_v = parts
        scores = masked_scores(block_q, block_k, allowed)
        peak = jnp.max(scores, axis=-1, keepdims=True)
        expo = jnp.exp(scores - peak)
        total = jnp.sum(expo, axis=-1, keepdims=True)
        probs = (expo / total).astype(jnp.bfloat16)
        mixed = jnp.einsum(
            "hqk,khe->qhe", probs, block_v, preferred_element_type=jnp.float32
        ).astype(jnp.bfloat16)
        return (mixed, peak[..., 0] + jnp.log(total[..., 0]))

    mixed, lse = lax.map(one_group, (by_groups(query), by_groups(keys), by_groups(values)))
    return (from_groups(mixed), lse)


def attend_back(query, keys, values, allowed, lse, grad_mix):

    def one_group(parts):
        block_q, block_k, block_v, block_d, block_l = parts
        scores = masked_scores(block_q, block_k, allowed)
        probs = jnp.exp(scores - block_l[..., None])
        grad_prob = jnp.einsum("qhe,khe->hqk", block_d, block_v, preferred_element_type=jnp.float32)
        inner = jnp.sum(probs * grad_prob, axis=-1, keepdims=True)
        grad_scores = (probs * (grad_prob - inner)).astype(jnp.bfloat16)
        grad_q = (
            jnp.einsum("hqk,khe->qhe", grad_scores, block_k, preferred_element_type=jnp.float32)
            * 0.125
        )
        grad_k = (
            jnp.einsum("hqk,qhe->khe", grad_scores, block_q, preferred_element_type=jnp.float32)
            * 0.125
        )
        grad_v = jnp.einsum(
            "hqk,qhe->khe", probs.astype(jnp.bfloat16), block_d, preferred_element_type=jnp.float32
        )
        return (grad_q, grad_k, grad_v)

    grad_q, grad_k, grad_v = lax.map(
        one_group, (by_groups(query), by_groups(keys), by_groups(values), by_groups(grad_mix), lse)
    )
    return (from_groups(grad_q), from_groups(grad_k), from_groups(grad_v))


def on_device_wide(
    tokens_in,
    prompt_states,
    image_ids,
    text_lengths,
    attn_gain,
    attn_shift,
    self_query,
    self_key,
    self_value,
    self_out,
    cross_gain,
    cross_shift,
    cross_query,
    cross_key,
    cross_value,
    cross_out,
    dense_gain,
    dense_shift,
    dense_in,
    dense_out,
    out_grad,
):
    shards = (
        attn_gain,
        attn_shift,
        self_query,
        self_key,
        self_value,
        self_out,
        cross_gain,
        cross_shift,
        cross_query,
        cross_key,
        cross_value,
        cross_out,
        dense_gain,
        dense_shift,
        dense_in,
        dense_out,
    )
    count = lax.axis_size("band")
    gains = (shards[0], shards[1], shards[6], shards[7], shards[12], shards[13])
    packed = jnp.pad(jnp.stack(gains), ((0, 2), (0, 128 - shards[0].shape[0])))
    mats = tuple(shards[i] for i in (2, 3, 4, 5, 8, 9, 10, 11, 14, 15))
    *full, many = gather_all(list(mats) + [packed], count)
    many = many.reshape(count, 8, 128)[:, :6, : shards[0].shape[0]].transpose(1, 0, 2).reshape(6, -1)
    whole = (many[0], many[1], *full[:4], many[2], many[3], *full[4:8], many[4], many[5], *full[8:])
    (
        gain_attn,
        bias_attn,
        full_query,
        full_key,
        full_value,
        full_out,
        gain_cross,
        bias_cross,
        full_cross_query,
        full_cross_key,
        full_cross_value,
        full_cross_out,
        gain_dense,
        bias_dense,
        full_dense_in,
        full_dense_out,
    ) = whole
    device = lax.axis_index("band")
    tok_dev = tokens_in.shape[0]
    rows_dev = tok_dev // ROW_TOK
    text = prompt_states.shape[1]
    padded_ids = jnp.concatenate([jnp.full((rows_dev,), -1, jnp.int32), image_ids])
    window_ids = lax.dynamic_slice_in_dim(padded_ids, device * rows_dev, 2 * rows_dev)
    key_ids = jnp.repeat(window_ids, ROW_TOK, total_repeat_length=2 * tok_dev)
    query_ids = key_ids[tok_dev:]
    key_place = jnp.arange(2 * tok_dev, dtype=jnp.int32)
    query_place = tok_dev + jnp.arange(tok_dev, dtype=jnp.int32)
    self_allowed = (key_ids[None, :] == query_ids[:, None]) & (
        key_place[None, :] <= query_place[:, None]
    )
    padded_len = jnp.concatenate([text_lengths, jnp.zeros((1,), jnp.int32)])
    near_len = lax.dynamic_slice_in_dim(padded_len, device, 2)
    slot_owner = device + jnp.arange(2, dtype=jnp.int32)
    owner_key = jnp.repeat(slot_owner, text, total_repeat_length=2 * text)
    length_key = jnp.repeat(near_len, text, total_repeat_length=2 * text)
    place_key = jnp.tile(jnp.arange(text, dtype=jnp.int32), 2)
    live_owner = owner_key < count
    cross_allowed = (
        (query_ids[:, None] == owner_key[None, :])
        & (place_key < length_key)[None, :]
        & live_owner[None, :]
    )
    tokens = tokens_in.astype(jnp.float32)
    attn_in = layer_norm(
        tokens, gain_attn.astype(jnp.float32), bias_attn.astype(jnp.float32)
    ).astype(jnp.bfloat16)
    query = matmul(attn_in, full_query).astype(jnp.bfloat16)
    key = matmul(attn_in, full_key).astype(jnp.bfloat16)
    value = matmul(attn_in, full_value).astype(jnp.bfloat16)
    before = from_behind((key, value), "band", 1)
    keys_all = jnp.concatenate([before[0], key], 0)
    values_all = jnp.concatenate([before[1], value], 0)
    self_mix, self_lse = attend_fwd(query, keys_all, values_all, self_allowed)
    resid_one = tokens + matmul(self_mix, full_out)
    cross_in = layer_norm(
        resid_one, gain_cross.astype(jnp.float32), bias_cross.astype(jnp.float32)
    ).astype(jnp.bfloat16)
    cross_q = matmul(cross_in, full_cross_query).astype(jnp.bfloat16)
    own_states = prompt_states[0]
    own_pair = (
        matmul(own_states, full_cross_key).astype(jnp.bfloat16),
        matmul(own_states, full_cross_value).astype(jnp.bfloat16),
    )
    next_pair = from_behind((own_pair[0], own_pair[1]), "band", -1)
    prompt_key = jnp.concatenate([own_pair[0], next_pair[0]], 0)
    prompt_value = jnp.concatenate([own_pair[1], next_pair[1]], 0)
    cross_mix, cross_lse = attend_fwd(cross_q, prompt_key, prompt_value, cross_allowed)
    resid_two = resid_one + matmul(cross_mix, full_cross_out)
    dense_x = layer_norm(
        resid_two, gain_dense.astype(jnp.float32), bias_dense.astype(jnp.float32)
    ).astype(jnp.bfloat16)
    hidden = matmul(dense_x, full_dense_in)
    act = gelu_exact(hidden).astype(jnp.bfloat16)
    block_out = (resid_two + matmul(act, full_dense_out)).astype(jnp.bfloat16)
    grad_out = out_grad.astype(jnp.float32)
    grad_dense_out = matmul_tn(act, out_grad)
    grad_act = matmul_nt(out_grad, full_dense_out)
    _, gelu_pull = jax.vjp(gelu_exact, hidden)
    grad_hidden = gelu_pull(grad_act)[0].astype(jnp.bfloat16)
    grad_dense_in = matmul_tn(dense_x, grad_hidden)
    grad_dense_x = matmul_nt(grad_hidden, full_dense_in)
    grad_resid, grad_dense_gain, grad_dense_shift = norm_back(
        resid_two, gain_dense.astype(jnp.float32), bias_dense.astype(jnp.float32), grad_dense_x
    )
    grad_resid_two = grad_out + grad_resid
    dense_local = (grad_dense_gain, grad_dense_shift, grad_dense_in, grad_dense_out)
    branch_two = grad_resid_two.astype(jnp.bfloat16)
    grad_cross_out = matmul_tn(cross_mix, branch_two)
    grad_cross_mix = matmul_nt(branch_two, full_cross_out).astype(jnp.bfloat16)
    grad_cq, grad_pk, grad_pv = attend_back(
        cross_q, prompt_key, prompt_value, cross_allowed, cross_lse, grad_cross_mix
    )
    back_pair = from_behind((as_sent(grad_pk[text:]), as_sent(grad_pv[text:])), "band", 1)
    grad_pk_low = (grad_pk[:text] + back_pair[0]).astype(jnp.bfloat16)
    grad_pv_low = (grad_pv[:text] + back_pair[1]).astype(jnp.bfloat16)
    grad_cross_key = matmul_tn(own_states, grad_pk_low)
    grad_cross_value = matmul_tn(own_states, grad_pv_low)
    grad_prompt = (
        matmul_nt(grad_pk_low, full_cross_key) + matmul_nt(grad_pv_low, full_cross_value)
    )[None]
    grad_cq_low = grad_cq.astype(jnp.bfloat16)
    grad_cross_query = matmul_tn(cross_in, grad_cq_low)
    grad_cross_in = matmul_nt(grad_cq_low, full_cross_query)
    grad_resid, grad_cross_gain, grad_cross_shift = norm_back(
        resid_one, gain_cross.astype(jnp.float32), bias_cross.astype(jnp.float32), grad_cross_in
    )
    grad_resid_one = grad_resid_two + grad_resid
    cross_local = (
        grad_cross_gain,
        grad_cross_shift,
        grad_cross_query,
        grad_cross_key,
        grad_cross_value,
        grad_cross_out,
    )
    branch_one = grad_resid_one.astype(jnp.bfloat16)
    grad_self_out = matmul_tn(self_mix, branch_one)
    grad_self_mix = matmul_nt(branch_one, full_out).astype(jnp.bfloat16)
    grad_q, grad_keys_all, grad_values_all = attend_back(
        query, keys_all, values_all, self_allowed, self_lse, grad_self_mix
    )
    back_kv = from_behind(
        (as_sent(grad_keys_all[:tok_dev]), as_sent(grad_values_all[:tok_dev])), "band", -1
    )
    grad_k = grad_keys_all[tok_dev:] + back_kv[0]
    grad_v = grad_values_all[tok_dev:] + back_kv[1]
    grad_q_low = grad_q.astype(jnp.bfloat16)
    grad_k_low = grad_k.astype(jnp.bfloat16)
    grad_v_low = grad_v.astype(jnp.bfloat16)
    grad_self_query = matmul_tn(attn_in, grad_q_low)
    grad_self_key = matmul_tn(attn_in, grad_k_low)
    grad_self_value = matmul_tn(attn_in, grad_v_low)
    grad_attn_in = (
        matmul_nt(grad_q_low, full_query)
        + matmul_nt(grad_k_low, full_key)
        + matmul_nt(grad_v_low, full_value)
    )
    grad_resid, grad_attn_gain, grad_attn_shift = norm_back(
        tokens, gain_attn.astype(jnp.float32), bias_attn.astype(jnp.float32), grad_attn_in
    )
    grad_tokens = grad_resid_one + grad_resid
    self_local = (
        grad_attn_gain,
        grad_attn_shift,
        grad_self_query,
        grad_self_key,
        grad_self_value,
        grad_self_out,
    )
    locals_ = self_local + cross_local + dense_local
    vecs = jnp.stack([locals_[i] for i in (0, 1, 6, 7, 12, 13)])
    width = vecs.shape[1] // count
    vecs = vecs.reshape(6, count, width).transpose(1, 0, 2)
    vecs = jnp.pad(vecs, ((0, 0), (0, 2), (0, 128 - width))).reshape(count * 8, 128)
    order = (2, 3, 4, 5, 8, 9, 10, 11, 14, 15)
    mats = [locals_[i].astype(jnp.bfloat16) for i in order]
    *sums, small = scatter_all(mats + [vecs], [(m.shape[0] // count, m.shape[1]) for m in mats] + [(8, 128)], count)
    summed = [None] * 16
    for i, s in zip(order, sums):
        summed[i] = s
    for j, i in enumerate((0, 1, 6, 7, 12, 13)):
        summed[i] = small[j, :width]
    summed = tuple(summed)
    return (block_out, grad_tokens, grad_prompt) + summed


class Moves:
    def __init__(self, pc, send, recv, k):
        self.pc, self.send, self.recv, self.k, self.n, self.sent = pc, send, recv, k, 0, []

    def slot(self):
        self.n += 1
        return self.n - 1

    def make(self, src, dst, dev, s, r):
        return pltpu.make_async_remote_copy(
            src_ref=src, dst_ref=dst, send_sem=self.send.at[self.k, s], recv_sem=self.recv.at[self.k, r],
            device_id=(dev,), device_id_type=MESH)

    def go(self, src, dst, dev):
        s = self.slot()
        d = self.make(src, dst, dev, s, s)
        d.start()
        self.sent.append((d, None))
        return d

    def go_if(self, cond, src, dst, dev, s, r):
        d = self.make(src, dst, dev, s, r)

        @pl.when(cond)
        def _():
            d.start()

        self.sent.append((d, cond))
        return d

    def drain(self):
        for d, cond in self.sent:
            if cond is None:
                d.wait_send()
            else:

                @pl.when(cond)
                def _(d=d):
                    d.wait_send()


class Line:
    def __init__(self, moves, view):
        self.m, self.view = moves, view
        self.slots = {o: moves.slot() for o in (1, 2, 3)}
        self.far = moves.slot()

    def start(self, src=None):
        m, pc, slots = self.m, self.m.pc, self.slots
        here = self.view(pc.z)
        src = here if src is None else src
        self.got = {
            1: m.go_if(pc.z != 3, src, here, pc.dev(dz=1), slots[1], slots[1]),
            2: m.make(src, here, pc.dev(dz=2), slots[2], slots[2]),
            3: m.go_if(pc.z != 0, src, here, pc.dev(dz=3), slots[3], slots[3]),
        }
        self.got[2].start()
        m.sent.append((self.got[2], None))

    def relay(self):
        m, pc = self.m, self.m.pc
        low, high = self.view(0), self.view(3)
        self.got[2].wait_recv()
        m.go_if(pc.z == 2, low, low, pc.dev(dz=1), self.far, self.slots[3])
        m.go_if(pc.z == 1, high, high, pc.dev(dz=3), self.far, self.slots[1])

    def finish(self):
        self.got[1].wait_recv()
        self.got[3].wait_recv()


class GatherZ(Moves):
    def __init__(self, pc, own, out, send, recv, loc, k):
        super().__init__(pc, send, recv, k)
        self.own, self.out, self.loc = own, out, loc

    def keep(self):
        pc = self.pc
        here = self.out(pc.z, pc.p, pc.q, pc.c)
        self.local = pltpu.make_async_copy(self.own, here, self.loc.at[self.k])
        self.local.start()
        return here

    def s0(self):
        pc = self.pc
        self.keep()
        self.line = Line(self, lambda z: self.out(z, pc.p, pc.q, pc.c))
        self.line.start(self.own)

    def s1(self):
        self.line.relay()

    def s2(self):
        pc = self.pc
        self.local.wait()
        self.line.finish()
        v = self.out(slice(None), pc.p, pc.q, pc.c)
        self.ps, self.qs = self.go(v, v, pc.dev(dp=1)), self.go(v, v, pc.dev(dq=1))

    def s3(self):
        pc = self.pc
        self.ps.wait_recv()
        v = self.out(pl.ds(0, 2), 1 - pc.p, pc.q, pc.c)
        self.rs = [self.go(v, v, pc.dev(dq=1))]
        self.qs.wait_recv()
        v = self.out(pl.ds(2, 2), pc.p, 1 - pc.q, pc.c)
        self.rs += [self.go(v, v, pc.dev(dp=1))]

    def s4(self):
        for d in self.rs:
            d.wait_recv()
        v = self.out(slice(None), slice(None), slice(None), self.pc.c)
        self.cs = self.go(v, v, self.pc.dev(dc=1))

    def s5(self):
        self.cs.wait_recv()


class GatherP(GatherZ):
    def s0(self):
        pc = self.pc
        here = self.keep()
        h = self.own.shape[0] // 2
        self.a, self.b = pl.ds(0, h), pl.ds(h, h)
        self.xs = [self.go(self.own.at[self.a], here.at[self.a], pc.dev(dp=1)), self.go(self.own.at[self.b], here.at[self.b], pc.dev(dq=1))]

    def s1(self):
        pc = self.pc
        self.local.wait()
        for d in self.xs:
            d.wait_recv()
        self.lines = [
            Line(self, lambda z: self.out(z, slice(None), pc.q, pc.c).at[:, self.a]),
            Line(self, lambda z: self.out(z, pc.p, slice(None), pc.c).at[:, self.b]),
        ]
        for line in self.lines:
            line.start()

    def s2(self):
        for line in self.lines:
            line.relay()

    def s3(self):
        pc = self.pc
        for line in self.lines:
            line.finish()
        va = self.out(slice(None), slice(None), pc.q, pc.c).at[:, :, self.a]
        vb = self.out(slice(None), pc.p, slice(None), pc.c).at[:, :, self.b]
        self.rs = [self.go(va, va, pc.dev(dq=1)), self.go(vb, vb, pc.dev(dp=1))]


def add_to(ref, *others):
    total = ref[...].astype(jnp.float32)
    for other in others:
        total += other[...].astype(jnp.float32)
    ref[...] = total.astype(ref.dtype)


class LineSum:
    def __init__(self, moves, block, came, joined):
        self.m, self.block, self.came, self.joined = moves, block, came, joined
        self.slots = {o: moves.slot() for o in (1, 2, 3)}
        self.far = moves.slot()
        self.outer = (moves.pc.z == 0) | (moves.pc.z == 3)

    def start(self):
        m, pc, slots = self.m, self.m.pc, self.slots
        first, last = pc.z == 0, pc.z == 3
        m.go_if(first, self.block(3), self.joined, pc.dev(dz=1), self.far, self.far)
        m.go_if(last, self.block(0), self.joined, pc.dev(dz=3), self.far, self.far)
        self.two = self.block((pc.z + 2) % 4)
        self.got = {
            1: m.go_if(pc.z != 3, self.block((pc.z + 1) % 4), self.came.at[0], pc.dev(dz=1), slots[1], slots[1]),
            2: m.go_if(self.outer, self.two, self.came.at[1], pc.dev(dz=2), slots[2], slots[2]),
            3: m.go_if(pc.z != 0, self.block((pc.z + 3) % 4), self.came.at[2], pc.dev(dz=3), slots[3], slots[3]),
        }

    def relay(self):
        m, pc = self.m, self.m.pc
        inner = (pc.z == 1) | (pc.z == 2)
        d = m.make(self.two, self.joined, pc.dev(dz=1), self.far, self.far)

        @pl.when(inner)
        def _():
            d.wait_recv()
            add_to(self.two, self.joined)

        m.go_if(inner, self.two, self.came.at[1], pc.dev(dz=2), self.slots[2], self.slots[2])

    def finish(self, use):
        pc = self.m.pc
        own = self.block(pc.z)
        self.got[2].wait_recv()

        @pl.when(pc.z == 0)
        def _():
            self.got[3].wait_recv()
            use(own, self.came.at[1], self.came.at[2])

        @pl.when(pc.z == 3)
        def _():
            self.got[1].wait_recv()
            use(own, self.came.at[0], self.came.at[1])

        @pl.when((pc.z == 1) | (pc.z == 2))
        def _():
            self.got[1].wait_recv()
            self.got[3].wait_recv()
            use(own, self.came.at[0], self.came.at[1], self.came.at[2])


class Sum(Moves):
    def __init__(self, pc, grad, put, r1, bufs, send, recv, k, credit=None, waits=False, gives=False):
        super().__init__(pc, send, recv, k)
        self.grad, self.put, self.r1, self.bufs = grad, put, r1, bufs
        self.credit, self.waits, self.gives = credit, waits, gives

    def others(self):
        pc = self.pc
        out = [(0, 0, pc.dev(dc=1)), (1, 1, pc.dev(dq=1)), (2, 2, pc.dev(dp=1))]
        return out + [(2 + 4 - o, 2 + o, pc.dev(dz=o)) for o in (1, 2, 3)]

    def s0(self):
        pc = self.pc
        if self.waits:
            for _, mine, _ in self.others():
                pl.semaphore_wait(self.credit.at[mine], 1)
        s = self.slot()
        self.d1 = self.make(self.grad(1 - pc.c), self.r1, pc.dev(dc=1), s, s)
        self.d1.start()

    def with_sibling(self):
        self.d1.wait()
        own = self.grad(self.pc.c)

        def body(i, _):
            at = i // 4, (i // 2) % 2, i % 2
            add_to(self.r1.at[at], own.at[at])
            return 0

        lax.fori_loop(0, 16, body, 0)

    def s6(self):
        self.drain()
        if self.gives:
            for theirs, _, dev in self.others():
                pl.semaphore_signal(self.credit.at[theirs], inc=1, device_id=(dev,), device_id_type=MESH)


class SumZ(Sum):
    @staticmethod
    def buffers(n, block):
        return [(n, 2, 2) + block, (n, 2, 2) + block, (n, 4) + block, (n, 3) + block, (n,) + block]

    def s1(self):
        pc = self.pc
        self.with_sibling()
        self.a, self.b, self.r3, self.r4, self.rx = self.bufs
        self.d2 = [
            self.go(self.r1.at[pl.ds(0, 2), :, 1 - pc.q], self.a, pc.dev(dq=1)),
            self.go(self.r1.at[pl.ds(2, 2), 1 - pc.p], self.b, pc.dev(dp=1)),
        ]

    def s2(self):
        pc = self.pc
        for d in self.d2:
            d.wait_recv()

        def body(i, _):
            h, e = i // 2, i % 2
            add_to(self.a.at[h, e], self.r1.at[h, e, pc.q])
            add_to(self.b.at[h, e], self.r1.at[2 + h, pc.p, e])
            return 0

        lax.fori_loop(0, 4, body, 0)
        self.d3 = [
            self.go(self.a.at[:, 1 - pc.p], self.r3.at[pl.ds(0, 2)], pc.dev(dp=1)),
            self.go(self.b.at[:, 1 - pc.q], self.r3.at[pl.ds(2, 2)], pc.dev(dq=1)),
        ]

    def s3(self):
        pc = self.pc
        for d in self.d3:
            d.wait_recv()

        def body(h, _):
            add_to(self.r3.at[h], self.a.at[h, pc.p])
            add_to(self.r3.at[2 + h], self.b.at[h, pc.q])
            return 0

        lax.fori_loop(0, 2, body, 0)
        self.line = LineSum(self, lambda z: self.r3.at[z], self.r4, self.rx)
        self.line.start()

    def s4(self):
        self.line.relay()

    def s5(self):
        here, end = self.put()

        def use(own, *came):
            total = own[...].astype(jnp.float32)
            for c in came:
                total += c[...].astype(jnp.float32)
            here[...] = total

        self.line.finish(use)
        if end is not None:
            end()


class SumP(Sum):
    @staticmethod
    def buffers(n, block):
        half = (block[0] // 2, block[1])
        pair = [(n, 4, 2) + half, (n, 3, 2) + half, (n, 2) + half, (n,) + half]
        return pair + pair

    def s1(self):
        pc = self.pc
        self.with_sibling()
        h = self.r1.shape[3] // 2
        self.half = pl.ds(0, h), pl.ds(h, h)
        self.sides = self.bufs[:4], self.bufs[4:]
        self.d2 = [
            self.go(self.r1.at[:, :, 1 - pc.q, self.half[0]], self.sides[0][0], pc.dev(dq=1)),
            self.go(self.r1.at[:, 1 - pc.p, :, self.half[1]], self.sides[1][0], pc.dev(dp=1)),
        ]

    def s2(self):
        pc = self.pc
        for d in self.d2:
            d.wait_recv()
        a, b = self.sides[0][0], self.sides[1][0]

        def body(i, _):
            z, e = i // 2, i % 2
            add_to(a.at[z, e], self.r1.at[z, e, pc.q, self.half[0]])
            add_to(b.at[z, e], self.r1.at[z, pc.p, e, self.half[1]])
            return 0

        lax.fori_loop(0, 8, body, 0)
        self.lines = [LineSum(self, lambda z, s=s: s[0].at[z], s[1], s[2]) for s in self.sides]
        for line in self.lines:
            line.start()

    def s3(self):
        for line in self.lines:
            line.relay()

    def s4(self):
        pc = self.pc
        for line in self.lines:
            line.finish(add_to)
        a, b = self.sides[0][0], self.sides[1][0]
        self.d3 = [
            self.go(a.at[pc.z, 1 - pc.p], self.sides[0][3], pc.dev(dp=1)),
            self.go(b.at[pc.z, 1 - pc.q], self.sides[1][3], pc.dev(dq=1)),
        ]

    def s5(self):
        pc = self.pc
        for d in self.d3:
            d.wait_recv()
        here, end = self.put()
        for s, mine, at in zip(self.sides, (pc.p, pc.q), self.half):
            here[at, :] = s[0][pc.z, mine].astype(jnp.float32) + s[3][...].astype(jnp.float32)
        end()


BF = jnp.bfloat16
F32 = jnp.float32
NN = (((1,), (0,)), ((), ()))
NT = (((1,), (1,)), ((), ()))
TN = (((0,), (0,)), ((), ()))
SCALE = 0.125 * 1.4426950408889634
FWD_NAMES = ("q", "k", "v", "o", "cq", "ck", "cv", "co", "di", "do")


def named(r, prefix):
    return [getattr(r, prefix + m) for m in FWD_NAMES]


def dot(left, right, form):
    return lax.dot_general(left, right, form, preferred_element_type=F32)


def tiles(total, step, body):
    if total == step:
        body(0)
    else:
        def one(i, _):
            body(pl.multiple_of(i * step, step))
            return 0

        lax.fori_loop(0, total // step, one, 0)


def product(left, right, form, put, step=512):
    wide = right.shape[0] if form is NT else right.shape[1]

    def one(off):
        part = right[pl.ds(off, step), :] if form is NT else right[:, pl.ds(off, step)]
        put(off, dot(left(), part, form))

    tiles(wide, step, one)


def store(ref):
    def put(off, value):
        ref[:, pl.ds(off, value.shape[1])] = value.astype(ref.dtype)

    return put


def norm_rows(src, dst, gains, i, step=64):
    def one(r):
        rows = pl.ds(r, step)
        value = src[rows, :].astype(F32)
        center = value - jnp.mean(value, axis=-1, keepdims=True)
        spread = jnp.mean(center * center, axis=-1, keepdims=True)
        unit = center * lax.rsqrt(spread + 1e-06)
        dst[rows, :] = (unit * gains[i : i + 1, :] + gains[i + 1 : i + 2, :]).astype(dst.dtype)

    tiles(src.shape[0], step, one)


def norm_back_rows(src, grad, base, dst, low, gains, i, sums, step=64):
    def one(r):
        rows = pl.ds(r, step)
        value = src[rows, :].astype(F32)
        center = value - jnp.mean(value, axis=-1, keepdims=True)
        spread = jnp.mean(center * center, axis=-1, keepdims=True)
        inverse = lax.rsqrt(spread + 1e-06)
        unit = center * inverse
        came = grad[rows, :]
        inner = came * gains[i : i + 1, :]
        back = (
            inner
            - jnp.mean(inner, axis=-1, keepdims=True)
            - unit * jnp.mean(inner * unit, axis=-1, keepdims=True)
        ) * inverse
        total = base[rows, :].astype(F32) + back
        dst[rows, :] = total
        if low is not None:
            low[rows, :] = total.astype(BF)
        sums[i] += jnp.sum((came * unit).reshape(step // 8, 8, -1), axis=0)
        sums[i + 1] += jnp.sum(came.reshape(step // 8, 8, -1), axis=0)

    tiles(src.shape[0], step, one)


def image_edges(ids, lens, rows_dev):
    me = lax.axis_index("band")
    first = rows_dev * me - rows_dev // 2

    def start_of(i):
        before = jnp.sum(jnp.where(ids[...] < i, 1.0, 0.0), axis=1, keepdims=True)
        return (before - first.astype(F32)) * float(ROW_TOK)

    def length_of(i):
        here = lax.broadcasted_iota(jnp.int32, lens.shape, 1) == i
        return jnp.sum(jnp.where(here, lens[...].astype(F32), 0.0), axis=1, keepdims=True)

    return start_of(me), start_of(me + 1), length_of(me), length_of(me + 1)


def make_masks(ids, lens, bias, cross_bias, rows_dev, text):
    low, high, own_len, next_len = image_edges(ids, lens, rows_dev)
    queries = bias.shape[1]
    halo = bias.shape[0] - queries
    step = 128

    def position(shape, axis, start):
        return (lax.broadcasted_iota(jnp.int32, shape, axis) + start).astype(F32)

    def one(r):
        shape = (step, queries)
        key, query = position(shape, 0, r), position(shape, 1, halo)
        least = jnp.where(query >= high, high, low)
        bias[pl.ds(r, step), :] = jnp.where((key <= query) & (key >= least), 0.0, -1e30)

    tiles(bias.shape[0], step, one)

    def two(r):
        shape = (step, queries)
        key, query = position(shape, 0, r), position(shape, 1, halo)
        later = query >= high
        least = jnp.where(later, float(text), 0.0)
        most = jnp.where(later, text + next_len, own_len)
        cross_bias[pl.ds(r, step), :] = jnp.where((key >= least) & (key < most), 0.0, -1e30)

    tiles(cross_bias.shape[0], step, two)


def mine_of(h, shape, axis):
    place = lax.broadcasted_iota(jnp.int32, shape, axis)
    return place < HEAD if h == 0 else place >= HEAD


def attend_pairs(q, k, v, bias, mix, lse, first, last, spans):
    def one(i, _):
        off = pl.multiple_of(i * 128, 128)
        lanes = pl.ds(off, 128)
        for q0, qn, kw in spans:
            qp, kp, vp = q[q0 : q0 + qn, lanes], k[:kw, lanes], v[:kw, lanes]
            for h in range(2):
                qm = jnp.where(mine_of(h, qp.shape, 1), qp, jnp.zeros_like(qp))
                vm = jnp.where(mine_of(h, vp.shape, 1), vp, jnp.ones_like(vp))
                s = dot(kp, qm, NT) * SCALE + bias[:kw, q0 : q0 + qn]
                peak = jnp.max(s, axis=0, keepdims=True)
                p = jnp.exp2(s - peak).astype(BF)
                got = dot(vm, p, TN)
                total = got[HEAD * (1 - h) : HEAD * (1 - h) + 1]
                own = got[HEAD * h : HEAD * (h + 1)] * (1.0 / total)
                rows = pl.ds(pl.multiple_of(off + HEAD * h, HEAD), HEAD)
                mix[rows, q0 : q0 + qn] = own.astype(BF)
                lse[i, h : h + 1, q0 : q0 + qn] = peak + jnp.log2(total)
        return 0

    lax.fori_loop(first, last, one, 0)


def attend_back_pairs(q, k, v, bias, mix, grad_mix, lse, dq, acc, put, first, last, spans):
    dk, dv = acc.at[0], acc.at[1]

    def one(i, _):
        off = pl.multiple_of(i * 128, 128)
        lanes = pl.ds(off, 128)
        acc[...] = jnp.zeros_like(acc)
        for q0, qn, kw in spans:
            cols = slice(q0, q0 + qn)
            qp, kp, vp = q[cols, lanes], k[:kw, lanes], v[:kw, lanes]
            go, mi = grad_mix[lanes, cols], mix[lanes, cols]
            dqt = jnp.zeros((128, qn), F32)
            for h in range(2):
                qm = jnp.where(mine_of(h, qp.shape, 1), qp, jnp.zeros_like(qp))
                km = jnp.where(mine_of(h, kp.shape, 1), kp, jnp.zeros_like(kp))
                gm = jnp.where(mine_of(h, go.shape, 0), go, jnp.zeros_like(go))
                inner = jnp.sum(gm.astype(F32) * mi.astype(F32), axis=0, keepdims=True)
                s = dot(kp, qm, NT) * SCALE + bias[:kw, cols]
                p = jnp.exp2(s - lse[i, h : h + 1, cols])
                ds = (p * (dot(vp, gm, NN) - inner)).astype(BF)
                dv[:kw, :] += dot(p.astype(BF), gm, NT)
                dk[:kw, :] += dot(ds, qm, NN)
                dqt += dot(km, ds, TN)
            dq[cols, lanes] = jnp.transpose(dqt * 0.125).astype(BF)
        put(lanes, dk, dv)
        return 0

    lax.fori_loop(first, last, one, 0)


class Copies:
    def __init__(self, sem):
        self.sem, self.used = sem, 0

    def start(self, src, dst):
        d = pltpu.make_async_copy(src, dst, self.sem.at[self.used])
        self.used += 1
        assert self.used <= self.sem.shape[0]
        d.start()
        return d


class Weights:
    def __init__(self, copies, slots, entries):
        self.copies, self.slots, self.entries = copies, slots, entries
        self.begun, self.used, self.live = 0, 0, {}

    def pump(self, done):
        while (
            self.begun < len(self.entries)
            and self.begun < self.used + self.slots.shape[0]
            and self.entries[self.begun][1] <= done
        ):
            src = self.entries[self.begun][0]
            self.live[self.begun] = self.copies.start(src, self.slots.at[self.begun % self.slots.shape[0]])
            self.begun += 1

    def take(self):
        e = self.used
        assert e < self.begun
        self.live[e].wait()
        return self.slots.at[e % self.slots.shape[0]]

    def free(self):
        self.used += 1


def ring_neighbors(count):
    me = lax.axis_index("band")
    return (me + 1) % count, (me + count - 1) % count


def enter(pc, count):
    sem = pltpu.get_barrier_semaphore()
    who = pc.partners() + list(ring_neighbors(count))
    for d in who:
        pl.semaphore_signal(sem, inc=1, device_id=(d,), device_id_type=MESH)
    pl.semaphore_wait(sem, len(who))


def layer_kernel(count, names, slots, early_us, late_us, *refs):
    r = types.SimpleNamespace(**dict(zip(names, refs)))
    pc = Place(count)
    Z, Pn, Qn = pc.Z, pc.P, pc.Q
    tok = r.tokens.shape[0]
    halo = tok // 2
    text = r.prompt.shape[0]
    copies = Copies(r.lsem)
    load = copies.start
    half = HEADS // 2
    q, k, v = r.gdo.at[pl.ds(0, tok)], r.gdo.at[pl.ds(tok, tok + halo)], r.gdo.at[pl.ds(2 * tok + halo, tok + halo)]
    first = 3 * tok + 2 * halo
    cq, cin = r.gdo.at[pl.ds(first, tok)], r.gdo.at[pl.ds(first + tok, tok)]
    pk, pv = r.gdo.at[pl.ds(first + 2 * tok, 2 * text)], r.gdo.at[pl.ds(first + 2 * tok + 2 * text, 2 * text)]
    pool = r.grads.reshape(r.grads.shape[0] * 1024, 1024)
    tokh, ainh = pool.at[pl.ds(0, tok + halo)], pool.at[pl.ds(tok + halo, tok + halo)]
    gx, tmp = r.ga.at[pl.ds(0, tok)], r.ga.at[pl.ds(tok, tok)]
    dkv = r.ga.at[pl.ds(2 * tok, 2 * tok)].reshape(2, tok, 1024)
    hid = r.bias.at[pl.ds(0, tok)]
    enter(pc, count)

    def remote(src, dst, i, dev):
        d = pltpu.make_async_remote_copy(
            src_ref=src, dst_ref=dst, send_sem=r.xsend.at[i], recv_sem=r.xrecv.at[i],
            device_id=(dev,), device_id_type=MESH)
        d.start()
        return d

    after, before = ring_neighbors(count)
    edge = [
        remote(r.tokens.at[pl.ds(tok - halo, halo)], tokh.at[pl.ds(0, halo)], 0, after),
        remote(r.prompt, r.pr.at[pl.ds(text, text)], 1, before),
    ]
    loads = types.SimpleNamespace(
        tok=copies.start(r.tokens, tokh.at[pl.ds(halo, tok)]),
        pr=copies.start(r.prompt, r.pr.at[pl.ds(0, text)]),
        gout=copies.start(r.gout, r.go),
    )

    shards = named(r, "s_") + [r.s_gains]
    wholes = named(r, "w_") + [r.gg]
    rows = shards[0].shape[0]
    order = [(10, 0, shards[10].shape[0], 0, 128)] + [(a, 0, rows, 0, 1024) for a in range(8)]
    order += [(9, rows * i, rows, 0, 1024) for i in range(shards[9].shape[0] // rows)]
    order += [(8, 0, rows, 1024 * j, 1024) for j in range(shards[8].shape[1] // 1024)]
    parts = shards[9].shape[0] // rows
    at = {n: 1 + a for a, n in enumerate(FWD_NAMES[:8])}
    at["do"], at["di"] = 8 + parts, 9 + parts
    gs = []
    for g, (a, r0, rn, c0, cn) in enumerate(order):
        own = shards[a].at[pl.ds(r0, rn), pl.ds(c0, cn)]
        view = wholes[a] if a == 10 else wholes[a].reshape((Z, Pn, Qn, 2) + shards[a].shape)

        def out(z, p, q, c, view=view, r0=r0, rn=rn, c0=c0, cn=cn):
            return view.at[z, p, q, c, pl.ds(r0, rn), pl.ds(c0, cn)]

        gs.append((GatherP if g % 2 else GatherZ)(pc, own, out, r.send, r.recv, r.loc, g))
    n = len(gs)

    def gather_tick(t):
        for stage in range(6):
            g = t - stage
            if 0 <= g < n:
                getattr(gs[g], f"s{stage}")()

    ff = [(r.w_do.at[pl.ds(1024 * j, 1024)], at["do"]) for j in range(parts)]
    entries = [(w, 1 + a) for a, w in enumerate(wholes[:8])] + ff
    entries += [(r.w_di.at[:, pl.ds(1024 * j, 1024)], at["di"] + j) for j in range(parts)]
    after_all = n - 1
    entries += [(r.w_di.at[:, pl.ds(1024 * j, 1024)], after_all) for j in range(parts)] + ff
    entries += [(wholes[a], after_all) for a in (7, 4, 3, 5, 6, 0, 1, 2)]
    weights = Weights(copies, r.ring, entries)
    latest = [-1]
    saves, kept = [], []

    def save(dst, src):
        kept.append(copies.start(src, dst))

    spans = [(0, tok // 2, tok), (tok // 2, tok // 2, tok + halo)]
    cross_spans = [(0, tok, 2 * text)]

    def t_masks():
        make_masks(r.ids, r.lens, r.bias, r.cbias, tok // ROW_TOK, text)

    def t_norm():
        width = 1024 // count
        per = 128 // width
        for g in range(8):
            total = jnp.zeros((8, 128), F32)
            for d in range(g * per, (g + 1) * per):
                c, qq, pp, zz = d % 2, (d // 2) % Qn, (d // (2 * Qn)) % Pn, d // (2 * Qn * Pn)
                total += r.gg[zz, pp, qq, c].astype(F32)
            r.gf[:, 128 * g : 128 * (g + 1)] = total
        loads.tok.wait()
        edge[0].wait_recv()
        norm_rows(tokh, ainh, r.gf, 0)
        save(r.o_ain, ainh.at[pl.ds(halo, tok)])

    def t_project(dst, src, lo, out):
        def go():
            w = weights.take()
            product(lambda: src[lo:, :], w, NN, store(dst))
            weights.free()
            save(out, dst)
        return go

    def t_self(a, b):
        def go():
            attend_pairs(q, k, v, r.bias, r.mix, r.lse, a, b, spans)
            if b == HEADS // 2:
                save(r.o_mix, r.mix)
        return go

    def t_out_self():
        w = weights.take()

        def put(off, value):
            cols = pl.ds(off, value.shape[1])
            r.res1[:, cols] = tokh[halo:, cols].astype(F32) + value

        product(lambda: r.mix[...], w, TN, put)
        weights.free()
        norm_rows(r.res1, cin, r.gf, 2)
        save(r.o_cin, cin)

    def t_prompt():
        loads.pr.wait()
        edge[1].wait_recv()

    def t_cross(a, b):
        def go():
            if a == 0:
                flush()
            attend_pairs(cq, pk, pv, r.cbias, r.mix, r.clse, a, b, cross_spans)
        return go

    def t_cross_out():
        w = weights.take()

        def put(off, value):
            cols = pl.ds(off, value.shape[1])
            r.res2[:, cols] = r.res1[:, cols] + value

        product(lambda: r.mix[...], w, TN, put)
        weights.free()
        norm_rows(r.res2, r.dx, r.gf, 4)

    def t_grad_act(j):
        def go():
            if j == 0:
                loads.gout.wait()
            w = weights.take()
            product(lambda: r.go[...], w, NT, store(r.ga.at[pl.ds(j * tok, tok)]))
            weights.free()
        return go

    def t_hidden(j):
        def go():
            w = weights.take()
            for c in range(2):
                cols = slice(512 * c, 512 * (c + 1))
                hid[...] = dot(r.dx[...], w[:, cols], NN)

                def one(a, cols=cols):
                    here, there = pl.ds(a, 32), pl.ds(j * tok + a, 32)
                    value = hid[here, :]
                    share = 0.5 + 0.5 * lax.erf(value * 0.7071067811865476)
                    slope = share + value * (jnp.exp(value * value * -0.5) * 0.3989422804014327)
                    r.act[there, cols] = (value * share).astype(BF)
                    r.gh[there, cols] = (r.ga[there, cols] * slope).astype(BF)

                tiles(tok, 32, one)
            weights.free()
        return go

    a2, g2 = r.act, r.gh
    L = types.SimpleNamespace(pr=loads.pr)
    blk = r.r1.shape[4]
    chunks = []
    nring = 9 + 2 * parts
    zbufs = [getattr(r, "z%d" % i) for i in range(5)]
    pbufs = [getattr(r, "p%d" % i) for i in range(8)]
    sum_slots = r.grads

    def chunk(grad, put, wide=1024):
        g = len(chunks)
        chunks.append(None)
        slot = g % slots

        def part(ref, s):
            return ref.at[(s,) + (slice(None),) * (len(ref.shape) - 2) + (pl.ds(0, wide),)]

        kind, bufs = (SumP, pbufs) if g % 2 else (SumZ, zbufs)
        r1 = part(r.r1, slot)
        chunks[g] = kind(pc, grad, put, r1, [part(x, slot // 2) for x in bufs], r.send2, r.recv2, g, r.credit, g >= slots, g + slots < nring)
        return g

    def block_view(ref, rows):
        return ref.reshape(Z, Pn, Qn, 2, rows, 1024)

    turns, staged = [0], {}

    def putter(first, c0=0, wide=1024):
        def begin():
            spot = turns[0] % r.stage.shape[0]
            turns[0] += 1
            if spot in staged:
                staged.pop(spot).wait()
            here = r.stage.at[spot, :, pl.ds(0, wide)]

            def end():
                staged[spot] = load(here, r.o_all.at[pl.ds(tok + text + first, blk), pl.ds(c0, wide)])

            return here, end

        return begin

    ready, active, summed = [], [], set()
    holder = [[] for _ in range(sum_slots.shape[0])]
    turn = [0]

    extra = []

    def item_of(g):
        return extra[0] if g == nring else chunks[g]

    def sum_tick():
        for item in sorted(active, key=lambda x: x[0] % 6):
            stage, g = item
            getattr(item_of(g), f"s{stage}")()
            if stage == 1:
                summed.add(g)
            item[0] += 1
        active[:] = [x for x in active if x[0] <= 6]
        if ready:
            g = ready.pop(0)
            item_of(g).s0()
            active.append([1, g])

    clock = [0]

    def tick():
        if clock[0] < n + 5:
            gather_tick(clock[0])
            latest[0] = clock[0] - 5
            clock[0] += 1
            weights.pump(latest[0])
        sum_tick()

    def until(gs):
        while not all(g in summed for g in gs):
            tick()

    def grad_chunk(first, form, left, right, cut=1):
        s = turn[0] % len(holder)
        turn[0] += 1
        until(holder[s])
        ref = sum_slots.at[s]
        view = block_view(ref, blk)
        wide = 1024 // cut
        holder[s] = []
        for i in range(cut):
            cols = pl.ds(wide * i, wide)
            product(left, right.at[:, cols], form, store(ref.at[:, cols]))
            g = chunk(lambda c, cols=cols: view.at[:, :, :, c, :, cols], putter(first, wide * i, wide), wide)
            holder[s].append(g)
            ready.append(g)

    X = {}
    r.sums[...] = jnp.zeros_like(r.sums)

    def t_din(j):
        def go():
            if j == 0:
                flush()
            grad_chunk(blk * (8 + j), TN, lambda: r.dx[...], g2.at[pl.ds(j * tok, tok)])
        return go

    dense = []

    def t_dout(j):
        def go():
            if j == 0:
                flush()
            here = r.gdo.at[pl.ds(1024 * j, 1024)]
            product(lambda: a2[pl.ds(j * tok, tok), :], r.go, TN, store(here))
            if j == parts - 1:
                view = block_view(r.gdo, blk * parts)
                for i in range(parts):
                    rows = pl.ds(blk * i, blk)
                    g = chunk(lambda c, rows=rows: view.at[:, :, :, c, rows], putter(blk * (8 + parts + i)))
                    dense.append(g)
                    ready.append(g)
        return go

    def area(first, n):
        whole = a2 if first < parts * tok else g2
        return whole.at[pl.ds(first % (parts * tok), n)]

    top = parts * tok
    bcq, bpk, bpv, dq = area(0, tok), area(tok, 2 * text), area(tok + 2 * text, 2 * text), area(2 * tok, tok)
    bcin, b2 = area(3 * tok, tok), area(top, tok)
    bq, bk, bv, sq = area(0, tok), area(top + tok, tok + halo), area(top + 2 * tok + halo, tok + halo), area(tok, tok)
    b1, ain = area(2 * tok, tok), area(3 * tok, tok)
    klow, vlow = area(2 * tok, tok), area(top, tok)

    def flush():
        while kept:
            kept.pop().wait()

    def t_gdx(j):
        def go():
            w = weights.take()
            mine = pl.ds(j * tok, tok)

            def put(off, value):
                cols = pl.ds(off, value.shape[1])
                if j == 0:
                    tmp[:, cols] = value
                else:
                    tmp[:, cols] += value

            product(lambda: g2[mine, :], w, NT, put)
            weights.free()
            weights.pump(latest[0])
        return go

    def t_out(j):
        def go():
            w = weights.take()
            mine = pl.ds(j * tok, tok)

            def put(off, value):
                cols = pl.ds(off, value.shape[1])
                total = (r.res2 if j == 0 else gx)[:, cols] + value
                if j < parts - 1:
                    gx[:, cols] = total
                else:
                    r.dx[:, cols] = total.astype(BF)

            product(lambda: a2[mine, :], w, NN, put)
            weights.free()
            weights.pump(latest[0])
            if j == parts - 1:
                X["o"] = copies.start(r.dx, r.o_out)
        return go

    def t_norm2():
        L.cq = load(r.o_cq, bcq)
        L.pk = load(r.o_pk, bpk)
        L.pv = load(r.o_pv, bpv)
        L.cin = load(r.o_cin, bcin)
        norm_back_rows(r.res2, tmp, r.go, gx, b2, r.gf, 4, r.sums)

    def t_gco():
        grad_chunk(blk * 7, NN, lambda: r.mix[...], b2)

    def t_gcm():
        w = weights.take()
        product(lambda: w[...], b2, NT, store(r.gmt), tok // 2)
        weights.free()
        weights.pump(latest[0])

    def cross_put(lanes, dk, dv):
        for i, (d, s) in enumerate(((dk, 0.125), (dv, 1.0))):
            r.pkv[i, :, lanes] = d[:text, :] * s
            r.psend[i, :, lanes] = (d[text:, :] * s).astype(BF)

    def b_cross(a, b):
        def go():
            if a == 0:
                for d in (L.cq, L.pk, L.pv):
                    d.wait()
            attend_back_pairs(bcq, bpk, bpv, r.cbias, r.mix, r.gmt, r.clse, dq, r.kv.at[:, pl.ds(0, 2 * text)], cross_put, a, b, cross_spans)
            if b == half:
                X["p"] = remote(r.psend, r.precv, 2, after)
                L.mix = load(r.o_mix, r.mix)
        return go

    def t_gcq():
        L.cin.wait()
        grad_chunk(blk * 4, TN, lambda: bcin[...], dq)

    def t_norm1():
        w = weights.take()
        product(lambda: dq[...], w, NT, store(tmp))
        weights.free()
        weights.pump(latest[0])
        norm_back_rows(r.res1, tmp, gx, gx, b1, r.gf, 2, r.sums)
        L.q, L.k, L.v = load(r.o_q, bq), load(r.o_k, bk), load(r.o_v, bv)

    def t_go():
        L.mix.wait()
        grad_chunk(blk * 3, NN, lambda: r.mix[...], b1)

    def t_gm():
        w = weights.take()
        product(lambda: w[...], b1, NT, store(r.gmt), tok // 2)
        weights.free()
        weights.pump(latest[0])

    hsend = r.gdo.at[pl.ds(0, 2 * halo)].reshape(2, halo, 1024)

    def self_put(lanes, dk, dv):
        for i, (d, s) in enumerate(((dk, 0.125), (dv, 1.0))):
            hsend[i, :, lanes] = (d[:halo, :] * s).astype(BF)
            dkv[i, :, lanes] = d[halo:, :] * s

    def b_self(a, b):
        def go():
            if a == 0:
                until(dense)
                for d in (L.q, L.k, L.v):
                    d.wait()
            attend_back_pairs(bq, bk, bv, r.bias, r.mix, r.gmt, r.lse, sq, r.kv, self_put, a, b, spans)
            if b == half:
                X["h"] = remote(hsend, r.hrecv, 3, before)
                L.ain = load(r.o_ain, ain)
                X.pop("o").wait()
                L.tokens = load(r.tokens, r.dx)
        return go

    gp = r.res2.at[pl.ds(0, text)]

    def b_prompt():
        X["p"].wait_recv()
        for i in range(2):
            r.plow[i] = (r.pkv[i] + r.precv[i].astype(F32)).astype(BF)

    def t_gp(i):
        def go():
            if i == 0:
                b_prompt()
            low = r.plow.at[i]
            grad_chunk(blk * (5 + i), TN, lambda: r.pr[:text, :], low)
            w = weights.take()

            def put(off, value):
                cols = pl.ds(off, value.shape[1])
                if i == 0:
                    gp[:, cols] = value
                else:
                    gp[:, cols] += value

            product(lambda: low[...], w, NT, put)
            weights.free()
            weights.pump(latest[0])
            if i == 1:
                saves.append(copies.start(gp, r.o_all.at[pl.ds(tok, text)]))
        return go

    def t_gq():
        L.ain.wait()
        grad_chunk(blk * 0, TN, lambda: ain[...], sq)

    def lower(i):
        low = (klow, vlow)[i]
        low[pl.ds(0, halo), :] = dkv[i, :halo, :].astype(BF)
        low[pl.ds(halo, halo), :] = (dkv[i, halo:, :] + r.hrecv[i].astype(F32)).astype(BF)

    def t_low_v():
        lower(1)

    def t_gkv(i):
        def go():
            low = (klow, vlow)[i]
            if i == 0:
                X["h"].wait_recv()
                lower(0)
            grad_chunk(blk * (1 + i), TN, lambda: ain[...], low, 1 + i)
        return go

    def t_gain(i):
        def go():
            w = weights.take()

            def put(off, value):
                cols = pl.ds(off, value.shape[1])
                if i == 0:
                    tmp[:, cols] = value
                else:
                    tmp[:, cols] += value

            product(lambda: (sq, klow, vlow)[i][...], w, NT, put)
            weights.free()
            weights.pump(latest[0])
        return go

    def t_norm0():
        L.tokens.wait()
        norm_back_rows(r.dx, tmp, gx, gx, None, r.gf, 0, r.sums)
        saves.append(copies.start(gx, r.o_all.at[pl.ds(0, tok)]))

    def t_vecs():
        width = 1024 // count
        per = 128 // width
        for g in range(8):
            lanes = slice(128 * g, 128 * (g + 1))
            tile = jnp.concatenate(
                [jnp.sum(r.sums[i, :, lanes], axis=0, keepdims=True) for i in range(6)] + [jnp.zeros((2, 128), F32)], axis=0)
            for d in range(g * per, (g + 1) * per):
                c, qq, pp, zz = d % 2, (d // 2) % Qn, (d // (2 * Qn)) % Pn, d // (2 * Qn * Pn)
                r.vg[zz, pp, qq, c] = tile

        bufs = [getattr(r, "v%d" % i) for i in range(6)]
        extra.append(SumZ(pc, lambda c: r.vg.at[:, :, :, c], lambda: (r.g_vec, None), bufs[0], bufs[1:], r.send2, r.recv2, nring))
        ready.append(nring)

    fore = [(-1, 2, t_masks), (0, 6, t_norm), (at["q"], 2.5, t_project(q, ainh, halo, r.o_q)),
            (at["k"], 4, t_project(k, ainh, 0, r.o_k)), (at["v"], 4, t_project(v, ainh, 0, r.o_v))]
    fore += [(at["v"], 3.5, t_self(a, a + 2)) for a in range(0, half, 2)]
    fore += [(at["o"], 3, t_out_self), (at["cq"], 1.5, t_project(cq, cin, 0, r.o_cq)), (-1, 0, t_prompt),
             (at["ck"], 1, t_project(pk, r.pr, 0, r.o_pk)), (at["cv"], 1, t_project(pv, r.pr, 0, r.o_pv)),
             (at["cv"], 4, t_cross(0, 4)), (at["cv"], 4, t_cross(4, 8)), (at["co"], 4, t_cross_out)]
    fore += [(at["do"], 1.5, t_grad_act(j)) for j in range(parts)]
    for j in range(parts):
        fore += [(at["di"] + j, 3.5, t_hidden(j)), (at["di"] + j, 1.5, t_din(j))]
    back = [(1.5, t_dout(j)) for j in range(parts)]
    back += [(1.5, t_gdx(j)) for j in range(parts)] + [(1.5, t_out(j)) for j in range(parts)]
    back += [(3, t_norm2), (1.5, t_gco), (1.5, t_gcm), (2, t_masks), (4, b_cross(0, 4)), (4, b_cross(4, 8))]
    back += [(1.5, t_gcq), (4, t_norm1), (1.5, t_go), (1.5, t_gm)]
    back += [(5, b_self(a, a + 2)) for a in range(0, half, 2)]
    back += [(1, t_gp(0)), (1, t_gp(1)), (1.5, t_gq), (2, t_gkv(0)), (0.3, t_low_v)]
    back += [(1.5, t_gain(i)) for i in range(3)] + [(3, t_norm0), (0.3, t_vecs), (2, t_gkv(1))]
    while clock[0] < n + 5:
        tick()
        spent = 0
        while fore and fore[0][0] <= max(latest[0], -1) and spent < early_us:
            _, cost, go = fore.pop(0)
            go()
            spent += cost
            weights.pump(latest[0])
    for _, _, go in fore:
        go()
        weights.pump(latest[0])
        tick()
    spent = 0
    for cost, go in back:
        go()
        weights.pump(latest[0])
        spent += cost
        if spent >= late_us and (ready or active):
            tick()
            spent = 0
    while ready or active:
        tick()
    flush()
    for d in staged.values():
        d.wait()
    for g in gs:
        g.drain()
    for d in edge + list(X.values()):
        d.wait_send()
    for d in saves:
        d.wait()


def layer(args, gains, ids, lens, count):
    tokens, prompt, gout, mats = args
    tok, text = tokens.shape[0], prompt.shape[0]
    halo = tok // 2
    dims = dims_of(count)
    blk = mats[0].shape[0]
    parts = mats[9].shape[0] // blk
    moved = 9 + 2 * parts
    slots = 6
    block = (blk, 1024)
    small = dict(s_gains=gains, tokens=tokens, prompt=prompt, gout=gout, ids=ids, lens=lens)
    names = ["s_" + m for m in FWD_NAMES] + list(small)
    outs = {"w_" + m: (w.shape[0] * count, w.shape[1], BF) for m, w in zip(FWD_NAMES, mats)}
    outs |= dict(
        o_ain=(tok, 1024, BF), o_q=(tok, 1024, BF), o_k=(tok + halo, 1024, BF), o_v=(tok + halo, 1024, BF), o_mix=(1024, tok, BF),
        o_cin=(tok, 1024, BF), o_cq=(tok, 1024, BF), o_pk=(2 * text, 1024, BF), o_pv=(2 * text, 1024, BF),
        o_out=(tok, 1024, BF), o_all=(tok + text + (8 + 2 * parts) * blk, 1024, F32))
    vouts = dict(g_vec=(8, 128, F32))
    scratch = {"z%d" % i: s + (BF,) for i, s in enumerate(SumZ.buffers(slots // 2, block))}
    scratch |= {"p%d" % i: s + (BF,) for i, s in enumerate(SumP.buffers(slots // 2, block))}
    scratch |= {"v%d" % i: s + (F32,) for i, s in enumerate([dims[:3] + (8, 128)] + [s[1:] for s in SumZ.buffers(1, (8, 128))])}
    scratch |= dict(
        r1=(slots,) + dims[:3] + block + (BF,), stage=(4,) + block + (F32,), grads=(2, 1024, 1024, BF), gdo=(1024 * parts, 1024, BF),
        act=(parts * tok, 1024, BF), gh=(parts * tok, 1024, BF), ga=(parts * tok, 1024, F32), ring=(2, 1024, 1024, BF),
        res1=(tok, 1024, F32), res2=(tok, 1024, F32), dx=(tok, 1024, BF), go=(tok, 1024, BF), pr=(2 * text, 1024, BF),
        mix=(1024, tok, BF), gmt=(1024, tok, BF), bias=(tok + halo, tok, F32), cbias=(2 * text, tok, F32), kv=(2, tok + halo, 128, F32),
        gf=(8, 1024, F32), gg=dims + (8, 128, BF), lse=(HEADS // 2, 2, tok, F32), clse=(HEADS // 2, 2, tok, F32),
        hrecv=(2, halo, 1024, BF), psend=(2, text, 1024, BF), precv=(2, text, 1024, BF), pkv=(2, text, 1024, F32),
        plow=(2, text, 1024, BF), sums=(6, 8, 1024, F32), vg=dims + (8, 128, F32))
    sems = dict(
        send=(moved, 16), recv=(moved, 16), send2=(moved + 1, 16), recv2=(moved + 1, 16), loc=(moved,), xsend=(4,), xrecv=(4,), lsem=(96,))
    every = names + list(outs) + list(vouts) + list(scratch) + list(sems) + ["credit"]
    got = pl.pallas_call(
        functools.partial(layer_kernel, count, every, slots, 5, 6),
        out_shape=[jax.ShapeDtypeStruct(s[:-1], s[-1]) for s in (outs | vouts).values()],
        in_specs=[pl.BlockSpec(memory_space=pl.ANY)] * 14 + [pl.BlockSpec(memory_space=pltpu.VMEM)] * 2,
        out_specs=[pl.BlockSpec(memory_space=pl.ANY)] * len(outs) + [pl.BlockSpec(memory_space=pltpu.VMEM)] * len(vouts),
        scratch_shapes=[pltpu.VMEM(s[:-1], s[-1]) for s in scratch.values()]
        + [pltpu.SemaphoreType.DMA(s) for s in sems.values()] + [pltpu.SemaphoreType.REGULAR((6,))],
        compiler_params=pltpu.CompilerParams(collective_id=0, has_side_effects=True, vmem_limit_bytes=63 << 20),
        name="layer",
    )(*mats, *small.values())
    return got[-3:]


def on_device(
    tokens_in,
    prompt_states,
    image_ids,
    text_lengths,
    attn_gain,
    attn_shift,
    self_query,
    self_key,
    self_value,
    self_out,
    cross_gain,
    cross_shift,
    cross_query,
    cross_key,
    cross_value,
    cross_out,
    dense_gain,
    dense_shift,
    dense_in,
    dense_out,
    out_grad,
):
    mats = (self_query, self_key, self_value, self_out, cross_query, cross_key, cross_value, cross_out, dense_in, dense_out)
    count = lax.axis_size("band")
    blk = mats[0].shape[0]
    if dims_of(count) != (4, 2, 2, 2) or blk % 32:
        return on_device_wide(
            tokens_in,
            prompt_states,
            image_ids,
            text_lengths,
            attn_gain,
            attn_shift,
            self_query,
            self_key,
            self_value,
            self_out,
            cross_gain,
            cross_shift,
            cross_query,
            cross_key,
            cross_value,
            cross_out,
            dense_gain,
            dense_shift,
            dense_in,
            dense_out,
            out_grad,
        )
    width = attn_gain.shape[0]
    per = 128 // width
    place = lax.axis_index("band") % per
    packed = jnp.stack((attn_gain, attn_shift, cross_gain, cross_shift, dense_gain, dense_shift))
    packed = jnp.pad(jnp.tile(packed, (1, per)), ((0, 2), (0, 0)))
    packed = jnp.where(jnp.arange(128, dtype=jnp.int32)[None] // width == place, packed, jnp.zeros_like(packed))
    ids, lens = image_ids[None], text_lengths[None]
    data = (tokens_in, prompt_states[0], out_grad, mats)
    block_out, every, vecs = layer(data, packed, ids, lens, count)
    vecs = lax.dynamic_slice(vecs, (0, place * width), (8, width))
    tok, text = tokens_in.shape[0], prompt_states.shape[1]
    parts = mats[9].shape[0] // blk
    own = every[tok + text :]
    g = [own[blk * i : blk * (i + 1)] for i in range(8)]
    wide = own[8 * blk : (8 + parts) * blk].reshape(parts, blk, -1).transpose(1, 0, 2).reshape(blk, -1)
    return (
        block_out, every[:tok], every[None, tok : tok + text],
        vecs[0], vecs[1], *g[:4],
        vecs[2], vecs[3], *g[4:],
        vecs[4], vecs[5], wide, own[(8 + parts) * blk :],
    )


def solution(mesh):
    return jax.shard_map(
        on_device,
        mesh=mesh,
        in_specs=(
            P("band", None),
            P("band", None, None),
            P(),
            P(),
            P("band"),
            P("band"),
            P("band", None),
            P("band", None),
            P("band", None),
            P("band", None),
            P("band"),
            P("band"),
            P("band", None),
            P("band", None),
            P("band", None),
            P("band", None),
            P("band"),
            P("band"),
            P("band", None),
            P("band", None),
            P("band", None),
        ),
        out_specs=(
            P("band", None),
            P("band", None),
            P("band", None, None),
            P("band"),
            P("band"),
            P("band", None),
            P("band", None),
            P("band", None),
            P("band", None),
            P("band"),
            P("band"),
            P("band", None),
            P("band", None),
            P("band", None),
            P("band", None),
            P("band"),
            P("band"),
            P("band", None),
            P("band", None),
        ),
        check_vma=False,
    )
```

```python
import functools
import types

import jax
import jax.numpy as jnp
from jax import lax
from jax.experimental import pallas as pl
from jax.experimental.pallas import tpu as pltpu
from jax.sharding import PartitionSpec as P

HEADS = 16
HEAD = 64
ROW_TOK = 32
MESH = pl.DeviceIdType.MESH


def dims_of(count):
    side = 1
    while 2 * (2 * side) ** 2 * 2 <= count:
        side *= 2
    return (count // (2 * side * side), side, side, 2)

class Place:
    def __init__(self, count):
        self.Z, self.P, self.Q, self.C = dims_of(count)
        me = lax.axis_index("band")
        self.c = me % 2
        self.q = (me // 2) % self.Q
        self.p = (me // (2 * self.Q)) % self.P
        self.z = me // (2 * self.Q * self.P)
    def dev(self, dz=0, dp=0, dq=0, dc=0):
        z = (self.z + dz) % self.Z
        p = (self.p + dp) % self.P
        q = (self.q + dq) % self.Q
        c = (self.c + dc) % 2
        return ((z * self.P + p) * self.Q + q) * 2 + c
    def partners(self):
        return ([self.dev(dz=o) for o in range(1, self.Z)] + [self.dev(dp=o) for o in range(1, self.P)]
                + [self.dev(dq=o) for o in range(1, self.Q)] + [self.dev(dc=1)])

def barrier(place):
    sem = pltpu.get_barrier_semaphore()
    who = place.partners()
    for d in who:
        pl.semaphore_signal(sem, inc=1, device_id=(d,), device_id_type=MESH)
    pl.semaphore_wait(sem, len(who))

class Gather:
    def __init__(self, pc, own, out, send, recv, loc, k):
        self.pc, self.own, self.out, self.send, self.recv, self.loc, self.k = pc, own, out, send, recv, loc, k
        Z, Pn, Qn = pc.Z, pc.P, pc.Q
        n = 0
        self.slots = {}
        for o in range(1, Z): self.slots["z", o] = n; n += 1
        for h in range(2):
            for o in range(1, Pn): self.slots["p", h, o] = n; n += 1
            for o in range(1, Qn): self.slots["q", h, o] = n; n += 1
        for o in range(1, Pn):
            for r in range(1, Qn):
                self.slots["pq", o, r] = n; n += 1
                self.slots["qp", o, r] = n; n += 1
        for a in range(Pn):
            for b in range(Qn):
                self.slots["c", a, b] = n; n += 1
        self.count = n
    @staticmethod
    def nslots(Z, Pn, Qn):
        return (Z - 1) + 2 * (Pn - 1 + Qn - 1) + 2 * (Pn - 1) * (Qn - 1) + Pn * Qn
    def copy(self, key, src, dst, dev):
        s = self.slots[key]
        return pltpu.make_async_remote_copy(src_ref=src, dst_ref=dst, send_sem=self.send.at[self.k, s], recv_sem=self.recv.at[self.k, s],
                                            device_id=(dev,), device_id_type=MESH)
    def half(self, h):
        return pl.ds(h * (self.pc.Z // 2), self.pc.Z // 2)
    def s0(self):
        pc = self.pc
        self.local = pltpu.make_async_copy(self.own, self.out(pc.z, pc.p, pc.q, pc.c), self.loc.at[self.k])
        self.local.start()
        self.zs = [self.copy(("z", o), self.own, self.out(pc.z, pc.p, pc.q, pc.c), pc.dev(dz=o)) for o in range(1, pc.Z)]
        for d in self.zs: d.start()
    def s1(self):
        pc = self.pc
        self.local.wait()
        for d in self.zs: d.wait_recv()
        self.ps = {}
        for h in range(2):
            v = self.out(self.half(h), pc.p, pc.q, pc.c)
            for o in range(1, pc.P): self.ps["p", h, o] = self.copy(("p", h, o), v, v, pc.dev(dp=o))
            for o in range(1, pc.Q): self.ps["q", h, o] = self.copy(("q", h, o), v, v, pc.dev(dq=o))
        for o in range(1, pc.P): self.ps["p", 0, o].start()
        for o in range(1, pc.Q): self.ps["q", 1, o].start()
        for o in range(1, pc.P): self.ps["p", 1, o].start()
        for o in range(1, pc.Q): self.ps["q", 0, o].start()
        self.cs = []
        v = self.out(slice(None), pc.p, pc.q, pc.c)
        d = self.copy(("c", 0, 0), v, v, pc.dev(dc=1)); d.start(); self.cs.append(d)
    def s2(self):
        pc = self.pc
        self.rs = []
        for o in range(1, pc.P): self.ps["p", 0, o].wait_recv()
        for o in range(1, pc.P):
            v = self.out(self.half(0), (pc.p - o) % pc.P, pc.q, pc.c)
            for r in range(1, pc.Q):
                d = self.copy(("pq", o, r), v, v, pc.dev(dq=r)); d.start(); self.rs.append(d)
        for r in range(1, pc.Q): self.ps["q", 1, r].wait_recv()
        for r in range(1, pc.Q):
            v = self.out(self.half(1), pc.p, (pc.q - r) % pc.Q, pc.c)
            for o in range(1, pc.P):
                d = self.copy(("qp", o, r), v, v, pc.dev(dp=o)); d.start(); self.rs.append(d)
        for o in range(1, pc.P): self.ps["p", 1, o].wait_recv()
        for o in range(1, pc.P):
            v = self.out(slice(None), (pc.p - o) % pc.P, pc.q, pc.c)
            d = self.copy(("c", o, 0), v, v, pc.dev(dc=1)); d.start(); self.cs.append(d)
        for r in range(1, pc.Q): self.ps["q", 0, r].wait_recv()
        for r in range(1, pc.Q):
            v = self.out(slice(None), pc.p, (pc.q - r) % pc.Q, pc.c)
            d = self.copy(("c", 0, r), v, v, pc.dev(dc=1)); d.start(); self.cs.append(d)
    def s3(self):
        pc = self.pc
        for d in self.rs: d.wait_recv()
        for o in range(1, pc.P):
            for r in range(1, pc.Q):
                v = self.out(slice(None), (pc.p - o) % pc.P, (pc.q - r) % pc.Q, pc.c)
                d = self.copy(("c", o, r), v, v, pc.dev(dc=1)); d.start(); self.cs.append(d)
    def s4(self):
        for d in self.cs: d.wait_recv()
    def drain(self):
        for d in self.zs: d.wait_send()
        for d in self.ps.values(): d.wait_send()
        for d in self.rs: d.wait_send()
        for d in self.cs: d.wait_send()

def chunks_of(shapes, n):
    out = []
    for a, (r, c) in enumerate(shapes):
        base_r = min(s[0] for s in shapes if s[1] >= 1024) if c >= 1024 else r
        if c >= 1024:
            for i in range(0, r, base_r):
                for j in range(0, c, 1024):
                    out.append((a, i, base_r, j, 1024))
        else:
            out.append((a, 0, r, 0, c))
    return out

def ag_kernel(count, nW, chunks, *refs):
    ins, outs = refs[:nW], refs[nW:2 * nW]
    send, recv, loc = refs[2 * nW:]
    pc = Place(count)
    barrier(pc)
    gs = []
    for k, (a, r0, rn, c0, cn) in enumerate(chunks):
        own = ins[a].at[pl.ds(r0, rn), pl.ds(c0, cn)]
        def out(z, p, q, c, a=a, r0=r0, rn=rn, c0=c0, cn=cn):
            return outs[a].at[z, p, q, c, pl.ds(r0, rn), pl.ds(c0, cn)]
        gs.append(Gather(pc, own, out, send, recv, loc, k))
    n = len(gs)
    for t in range(n + 4):
        for stage in range(5):
            k = t - stage
            if 0 <= k < n:
                getattr(gs[k], f"s{stage}")()
    for g in gs: g.drain()

def gather_all(shards, count, cid=0):
    dims = dims_of(count)
    nW = len(shards)
    chunks = chunks_of([s.shape for s in shards], count)
    ns = Gather.nslots(*dims[:3])
    outs = pl.pallas_call(
        functools.partial(ag_kernel, count, nW, chunks),
        out_shape=[jax.ShapeDtypeStruct(dims + s.shape, s.dtype) for s in shards],
        in_specs=[pl.BlockSpec(memory_space=pl.ANY)] * nW,
        out_specs=[pl.BlockSpec(memory_space=pl.ANY)] * nW,
        scratch_shapes=[pltpu.SemaphoreType.DMA((len(chunks), ns)), pltpu.SemaphoreType.DMA((len(chunks), ns)), pltpu.SemaphoreType.DMA((len(chunks),))],
        compiler_params=pltpu.CompilerParams(collective_id=cid, has_side_effects=True),
        name="gather",
    )(*shards)
    return [o.reshape((count * s.shape[0],) + s.shape[1:]) for o, s in zip(outs, shards)]


class Scatter:
    def __init__(self, pc, grad, put, bufs, send, recv, loc, k, kb):
        self.pc, self.grad, self.put, self.send, self.recv, self.loc, self.k, self.kb = pc, grad, put, send, recv, loc, k, kb
        self.own = bufs[0] if bufs[0] is None else bufs[0].at[kb]
        self.r1, self.r2a, self.r2b, self.r3a, self.r3b, self.r4 = [b.at[kb] for b in bufs[1:]]
        Z, Pn, Qn = pc.Z, pc.P, pc.Q
        n = 0
        self.slots = {"c": 0}; n = 1
        for o in range(1, Qn): self.slots["2a", o] = n; n += 1
        for o in range(1, Pn): self.slots["2b", o] = n; n += 1
        for o in range(1, Pn): self.slots["3a", o] = n; n += 1
        for o in range(1, Qn): self.slots["3b", o] = n; n += 1
        for o in range(1, Z): self.slots["4", o] = n; n += 1
    @staticmethod
    def nslots(Z, Pn, Qn):
        return 1 + 2 * (Pn - 1 + Qn - 1) + Z - 1
    @staticmethod
    def buffers(n, dims, block, dtype):
        Z, Pn, Qn = dims[:3]; H = Z // 2
        return [(n, Z, Pn, Qn) + block, (n, Z, Pn, Qn) + block, (n, Qn - 1, H, Pn) + block, (n, Pn - 1, H, Qn) + block,
                (n, Pn - 1, H) + block, (n, Qn - 1, H) + block, (n, Z - 1) + block]
    def copy(self, key, src, dst, dev):
        s = self.slots[key]
        return pltpu.make_async_remote_copy(src_ref=src, dst_ref=dst, send_sem=self.send.at[self.k, s], recv_sem=self.recv.at[self.k, s],
                                            device_id=(dev,), device_id_type=MESH)
    def s0(self):
        pc = self.pc
        self.d1 = self.copy("c", self.grad(1 - pc.c), self.r1, pc.dev(dc=1)); self.d1.start()
        self.l = pltpu.make_async_copy(self.grad(pc.c), self.own, self.loc.at[self.k]); self.l.start()
    def arrive(self):
        self.l.wait(); self.d1.wait_recv()
    def s1(self):
        pc = self.pc; Z, Pn, Qn = pc.Z, pc.P, pc.Q; H = Z // 2
        self.arrive()
        def body(i, _):
            z, p, q = i // (Pn * Qn), (i // Qn) % Pn, i % Qn
            self.r1[z, p, q] = (self.r1[z, p, q].astype(jnp.float32) + self.own[z, p, q].astype(jnp.float32)).astype(self.r1.dtype)
            return 0
        lax.fori_loop(0, Z * Pn * Qn, body, 0)
        self.d2 = []
        for o in range(1, Qn):
            d = self.copy(("2a", o), self.r1.at[pl.ds(0, H), :, (pc.q + o) % Qn], self.r2a.at[o - 1], pc.dev(dq=o)); d.start(); self.d2.append(d)
        for o in range(1, Pn):
            d = self.copy(("2b", o), self.r1.at[pl.ds(H, H), (pc.p + o) % Pn], self.r2b.at[o - 1], pc.dev(dp=o)); d.start(); self.d2.append(d)
    def s2(self):
        pc = self.pc; Z, Pn, Qn = pc.Z, pc.P, pc.Q; H = Z // 2
        for d in self.d2: d.wait_recv()
        def body(i, _):
            h, p = i // Pn, i % Pn
            t = self.r1[h, p, pc.q].astype(jnp.float32)
            for o in range(Qn - 1): t += self.r2a[o, h, p].astype(jnp.float32)
            self.r2a[0, h, p] = t.astype(self.r1.dtype)
            return 0
        lax.fori_loop(0, H * Pn, body, 0)
        def body(i, _):
            h, q = i // Qn, i % Qn
            t = self.r1[H + h, pc.p, q].astype(jnp.float32)
            for o in range(Pn - 1): t += self.r2b[o, h, q].astype(jnp.float32)
            self.r2b[0, h, q] = t.astype(self.r1.dtype)
            return 0
        lax.fori_loop(0, H * Qn, body, 0)
        self.d3 = []
        for o in range(1, Pn):
            d = self.copy(("3a", o), self.r2a.at[0, :, (pc.p + o) % Pn], self.r3a.at[o - 1], pc.dev(dp=o)); d.start(); self.d3.append(d)
        for o in range(1, Qn):
            d = self.copy(("3b", o), self.r2b.at[0, :, (pc.q + o) % Qn], self.r3b.at[o - 1], pc.dev(dq=o)); d.start(); self.d3.append(d)
    def s3(self):
        pc = self.pc; Z, Pn, Qn = pc.Z, pc.P, pc.Q; H = Z // 2
        for d in self.d3: d.wait_recv()
        def body(h, _):
            t = self.r2a[0, h, pc.p].astype(jnp.float32)
            for o in range(Pn - 1): t += self.r3a[o, h].astype(jnp.float32)
            self.r3a[0, h] = t.astype(self.r1.dtype)
            t = self.r2b[0, h, pc.q].astype(jnp.float32)
            for o in range(Qn - 1): t += self.r3b[o, h].astype(jnp.float32)
            self.r3b[0, h] = t.astype(self.r1.dtype)
            return 0
        lax.fori_loop(0, H, body, 0)
        self.d4 = []
        for o in range(1, Z):
            zt = (pc.z + o) % Z
            @pl.when(zt < H)
            def _():
                self.copy(("4", o), self.r3a.at[0, zt], self.r4.at[o - 1], pc.dev(dz=o)).start()
            @pl.when(zt >= H)
            def _():
                self.copy(("4", o), self.r3b.at[0, zt - H], self.r4.at[o - 1], pc.dev(dz=o)).start()
            self.d4.append(self.copy(("4", o), self.r3a.at[0, 0], self.r4.at[o - 1], pc.dev(dz=o)))
    def s4(self):
        pc = self.pc; Z, Pn, Qn = pc.Z, pc.P, pc.Q; H = Z // 2
        for d in self.d4: d.wait_recv()
        def fin(first):
            t = first.astype(jnp.float32)
            for o in range(Z - 1): t += self.r4[o].astype(jnp.float32)
            self.put(t)
        @pl.when(pc.z < H)
        def _(): fin(self.r3a[0, pc.z])
        @pl.when(pc.z >= H)
        def _(): fin(self.r3b[0, pc.z - H])
    def drain(self):
        self.d1.wait_send()
        for d in self.d2 + self.d3 + self.d4: d.wait_send()

def rs_kernel(count, nW, chunks, *refs):
    ins, outs = refs[:nW], refs[nW : 2 * nW]
    big, small = refs[2 * nW : 2 * nW + 7], refs[2 * nW + 7 : 2 * nW + 14]
    send, recv, loc = refs[2 * nW + 14 :]
    pc = Place(count)
    barrier(pc)
    ss = []
    wide = chunks[0][4]
    for k, (a, r0, rn, c0, cn) in enumerate(chunks):
        def grad(c, a=a, r0=r0, rn=rn, c0=c0, cn=cn):
            return ins[a].at[:, :, :, c, pl.ds(r0, rn), pl.ds(c0, cn)]
        def put(t, a=a, r0=r0, rn=rn, c0=c0, cn=cn):
            outs[a][pl.ds(r0, rn), pl.ds(c0, cn)] = t
        if cn == wide:
            ss.append(Scatter(pc, grad, put, big, send, recv, loc, k, k))
        else:
            ss.append(Scatter(pc, grad, put, small, send, recv, loc, k, 0))
    n = len(ss)
    for t in range(n + 4):
        for stage in range(5):
            k = t - stage
            if 0 <= k < n:
                getattr(ss[k], f"s{stage}")()
    for s in ss: s.drain()

def scatter_all(grads, shard_shapes, count, cid=1):
    dims = dims_of(count)
    nW = len(grads)
    chunks = chunks_of(shard_shapes, count)
    ns = Scatter.nslots(*dims[:3])
    block = chunks[0][2], chunks[0][4]
    bufs = [pltpu.VMEM(s, jnp.bfloat16) for s in Scatter.buffers(len(chunks) - 1, dims, block, None)]
    bufs += [pltpu.VMEM(s, jnp.float32) for s in Scatter.buffers(1, dims, shard_shapes[-1], None)]
    sems = [pltpu.SemaphoreType.DMA((len(chunks), ns)), pltpu.SemaphoreType.DMA((len(chunks), ns)), pltpu.SemaphoreType.DMA((len(chunks),))]
    return pl.pallas_call(
        functools.partial(rs_kernel, count, nW, chunks),
        out_shape=[jax.ShapeDtypeStruct(s, jnp.float32) for s in shard_shapes],
        in_specs=[pl.BlockSpec(memory_space=pl.ANY)] * nW,
        out_specs=[pl.BlockSpec(memory_space=pltpu.VMEM)] * nW,
        scratch_shapes=bufs + sems,
        compiler_params=pltpu.CompilerParams(collective_id=cid, has_side_effects=True, vmem_limit_bytes=60 << 20),
        name="scatter",
    )(*[g.reshape(dims + tuple(s)) for g, s in zip(grads, shard_shapes)])


def from_behind(block, axis, distance):
    devices = range(lax.axis_size(axis))
    route = [(i - distance, i) for i in devices if i - distance in devices]
    return lax.ppermute(block, axis, route)


def as_sent(shard):
    return jax.tree.map(lambda a: a.astype(jnp.bfloat16) if a.dtype == jnp.float32 else a, shard)


def layer_norm(value, gain, shift):
    center = value - jnp.mean(value, axis=-1, keepdims=True)
    spread = jnp.mean(center * center, axis=-1, keepdims=True)
    return center * lax.rsqrt(spread + 1e-06) * gain + shift


def norm_back(value, gain, shift, incoming):
    _, pullback = jax.vjp(layer_norm, value, gain, shift)
    return pullback(incoming)


def gelu_exact(value):
    return jax.nn.gelu(value, approximate=False)


def matmul(left, right):
    return jnp.dot(left, right, preferred_element_type=jnp.float32)


def matmul_nt(left, right):
    return lax.dot_general(
        left, right, (((1,), (1,)), ((), ())), preferred_element_type=jnp.float32
    )


def matmul_tn(left, right):
    return lax.dot_general(
        left, right, (((0,), (0,)), ((), ())), preferred_element_type=jnp.float32
    )


def by_groups(tensor):
    return tensor.reshape(tensor.shape[0], HEADS // 4, 4, HEAD).transpose(1, 0, 2, 3)


def from_groups(tensor):
    return tensor.transpose(1, 0, 2, 3).reshape(tensor.shape[1], HEADS * HEAD)


def masked_scores(block_q, block_k, allowed):
    scores = (
        jnp.einsum("qhe,khe->hqk", block_q, block_k, preferred_element_type=jnp.float32) * 0.125
    )
    return jnp.where(allowed[None], scores, -1e30)


def attend_fwd(query, keys, values, allowed):

    def one_group(parts):
        block_q, block_k, block_v = parts
        scores = masked_scores(block_q, block_k, allowed)
        peak = jnp.max(scores, axis=-1, keepdims=True)
        expo = jnp.exp(scores - peak)
        total = jnp.sum(expo, axis=-1, keepdims=True)
        probs = (expo / total).astype(jnp.bfloat16)
        mixed = jnp.einsum(
            "hqk,khe->qhe", probs, block_v, preferred_element_type=jnp.float32
        ).astype(jnp.bfloat16)
        return (mixed, peak[..., 0] + jnp.log(total[..., 0]))

    mixed, lse = lax.map(one_group, (by_groups(query), by_groups(keys), by_groups(values)))
    return (from_groups(mixed), lse)


def attend_back(query, keys, values, allowed, lse, grad_mix):

    def one_group(parts):
        block_q, block_k, block_v, block_d, block_l = parts
        scores = masked_scores(block_q, block_k, allowed)
        probs = jnp.exp(scores - block_l[..., None])
        grad_prob = jnp.einsum("qhe,khe->hqk", block_d, block_v, preferred_element_type=jnp.float32)
        inner = jnp.sum(probs * grad_prob, axis=-1, keepdims=True)
        grad_scores = (probs * (grad_prob - inner)).astype(jnp.bfloat16)
        grad_q = (
            jnp.einsum("hqk,khe->qhe", grad_scores, block_k, preferred_element_type=jnp.float32)
            * 0.125
        )
        grad_k = (
            jnp.einsum("hqk,qhe->khe", grad_scores, block_q, preferred_element_type=jnp.float32)
            * 0.125
        )
        grad_v = jnp.einsum(
            "hqk,qhe->khe", probs.astype(jnp.bfloat16), block_d, preferred_element_type=jnp.float32
        )
        return (grad_q, grad_k, grad_v)

    grad_q, grad_k, grad_v = lax.map(
        one_group, (by_groups(query), by_groups(keys), by_groups(values), by_groups(grad_mix), lse)
    )
    return (from_groups(grad_q), from_groups(grad_k), from_groups(grad_v))


def on_device_wide(
    tokens_in,
    prompt_states,
    image_ids,
    text_lengths,
    attn_gain,
    attn_shift,
    self_query,
    self_key,
    self_value,
    self_out,
    cross_gain,
    cross_shift,
    cross_query,
    cross_key,
    cross_value,
    cross_out,
    dense_gain,
    dense_shift,
    dense_in,
    dense_out,
    out_grad,
):
    shards = (
        attn_gain,
        attn_shift,
        self_query,
        self_key,
        self_value,
        self_out,
        cross_gain,
        cross_shift,
        cross_query,
        cross_key,
        cross_value,
        cross_out,
        dense_gain,
        dense_shift,
        dense_in,
        dense_out,
    )
    count = lax.axis_size("band")
    gains = (shards[0], shards[1], shards[6], shards[7], shards[12], shards[13])
    packed = jnp.pad(jnp.stack(gains), ((0, 2), (0, 128 - shards[0].shape[0])))
    mats = tuple(shards[i] for i in (2, 3, 4, 5, 8, 9, 10, 11, 14, 15))
    *full, many = gather_all(list(mats) + [packed], count)
    many = many.reshape(count, 8, 128)[:, :6, : shards[0].shape[0]].transpose(1, 0, 2).reshape(6, -1)
    whole = (many[0], many[1], *full[:4], many[2], many[3], *full[4:8], many[4], many[5], *full[8:])
    (
        gain_attn,
        bias_attn,
        full_query,
        full_key,
        full_value,
        full_out,
        gain_cross,
        bias_cross,
        full_cross_query,
        full_cross_key,
        full_cross_value,
        full_cross_out,
        gain_dense,
        bias_dense,
        full_dense_in,
        full_dense_out,
    ) = whole
    device = lax.axis_index("band")
    tok_dev = tokens_in.shape[0]
    rows_dev = tok_dev // ROW_TOK
    text = prompt_states.shape[1]
    padded_ids = jnp.concatenate([jnp.full((rows_dev,), -1, jnp.int32), image_ids])
    window_ids = lax.dynamic_slice_in_dim(padded_ids, device * rows_dev, 2 * rows_dev)
    key_ids = jnp.repeat(window_ids, ROW_TOK, total_repeat_length=2 * tok_dev)
    query_ids = key_ids[tok_dev:]
    key_place = jnp.arange(2 * tok_dev, dtype=jnp.int32)
    query_place = tok_dev + jnp.arange(tok_dev, dtype=jnp.int32)
    self_allowed = (key_ids[None, :] == query_ids[:, None]) & (
        key_place[None, :] <= query_place[:, None]
    )
    padded_len = jnp.concatenate([text_lengths, jnp.zeros((1,), jnp.int32)])
    near_len = lax.dynamic_slice_in_dim(padded_len, device, 2)
    slot_owner = device + jnp.arange(2, dtype=jnp.int32)
    owner_key = jnp.repeat(slot_owner, text, total_repeat_length=2 * text)
    length_key = jnp.repeat(near_len, text, total_repeat_length=2 * text)
    place_key = jnp.tile(jnp.arange(text, dtype=jnp.int32), 2)
    live_owner = owner_key < count
    cross_allowed = (
        (query_ids[:, None] == owner_key[None, :])
        & (place_key < length_key)[None, :]
        & live_owner[None, :]
    )
    tokens = tokens_in.astype(jnp.float32)
    attn_in = layer_norm(
        tokens, gain_attn.astype(jnp.float32), bias_attn.astype(jnp.float32)
    ).astype(jnp.bfloat16)
    query = matmul(attn_in, full_query).astype(jnp.bfloat16)
    key = matmul(attn_in, full_key).astype(jnp.bfloat16)
    value = matmul(attn_in, full_value).astype(jnp.bfloat16)
    before = from_behind((key, value), "band", 1)
    keys_all = jnp.concatenate([before[0], key], 0)
    values_all = jnp.concatenate([before[1], value], 0)
    self_mix, self_lse = attend_fwd(query, keys_all, values_all, self_allowed)
    resid_one = tokens + matmul(self_mix, full_out)
    cross_in = layer_norm(
        resid_one, gain_cross.astype(jnp.float32), bias_cross.astype(jnp.float32)
    ).astype(jnp.bfloat16)
    cross_q = matmul(cross_in, full_cross_query).astype(jnp.bfloat16)
    own_states = prompt_states[0]
    own_pair = (
        matmul(own_states, full_cross_key).astype(jnp.bfloat16),
        matmul(own_states, full_cross_value).astype(jnp.bfloat16),
    )
    next_pair = from_behind((own_pair[0], own_pair[1]), "band", -1)
    prompt_key = jnp.concatenate([own_pair[0], next_pair[0]], 0)
    prompt_value = jnp.concatenate([own_pair[1], next_pair[1]], 0)
    cross_mix, cross_lse = attend_fwd(cross_q, prompt_key, prompt_value, cross_allowed)
    resid_two = resid_one + matmul(cross_mix, full_cross_out)
    dense_x = layer_norm(
        resid_two, gain_dense.astype(jnp.float32), bias_dense.astype(jnp.float32)
    ).astype(jnp.bfloat16)
    hidden = matmul(dense_x, full_dense_in)
    act = gelu_exact(hidden).astype(jnp.bfloat16)
    block_out = (resid_two + matmul(act, full_dense_out)).astype(jnp.bfloat16)
    grad_out = out_grad.astype(jnp.float32)
    grad_dense_out = matmul_tn(act, out_grad)
    grad_act = matmul_nt(out_grad, full_dense_out)
    _, gelu_pull = jax.vjp(gelu_exact, hidden)
    grad_hidden = gelu_pull(grad_act)[0].astype(jnp.bfloat16)
    grad_dense_in = matmul_tn(dense_x, grad_hidden)
    grad_dense_x = matmul_nt(grad_hidden, full_dense_in)
    grad_resid, grad_dense_gain, grad_dense_shift = norm_back(
        resid_two, gain_dense.astype(jnp.float32), bias_dense.astype(jnp.float32), grad_dense_x
    )
    grad_resid_two = grad_out + grad_resid
    dense_local = (grad_dense_gain, grad_dense_shift, grad_dense_in, grad_dense_out)
    branch_two = grad_resid_two.astype(jnp.bfloat16)
    grad_cross_out = matmul_tn(cross_mix, branch_two)
    grad_cross_mix = matmul_nt(branch_two, full_cross_out).astype(jnp.bfloat16)
    grad_cq, grad_pk, grad_pv = attend_back(
        cross_q, prompt_key, prompt_value, cross_allowed, cross_lse, grad_cross_mix
    )
    back_pair = from_behind((as_sent(grad_pk[text:]), as_sent(grad_pv[text:])), "band", 1)
    grad_pk_low = (grad_pk[:text] + back_pair[0]).astype(jnp.bfloat16)
    grad_pv_low = (grad_pv[:text] + back_pair[1]).astype(jnp.bfloat16)
    grad_cross_key = matmul_tn(own_states, grad_pk_low)
    grad_cross_value = matmul_tn(own_states, grad_pv_low)
    grad_prompt = (
        matmul_nt(grad_pk_low, full_cross_key) + matmul_nt(grad_pv_low, full_cross_value)
    )[None]
    grad_cq_low = grad_cq.astype(jnp.bfloat16)
    grad_cross_query = matmul_tn(cross_in, grad_cq_low)
    grad_cross_in = matmul_nt(grad_cq_low, full_cross_query)
    grad_resid, grad_cross_gain, grad_cross_shift = norm_back(
        resid_one, gain_cross.astype(jnp.float32), bias_cross.astype(jnp.float32), grad_cross_in
    )
    grad_resid_one = grad_resid_two + grad_resid
    cross_local = (
        grad_cross_gain,
        grad_cross_shift,
        grad_cross_query,
        grad_cross_key,
        grad_cross_value,
        grad_cross_out,
    )
    branch_one = grad_resid_one.astype(jnp.bfloat16)
    grad_self_out = matmul_tn(self_mix, branch_one)
    grad_self_mix = matmul_nt(branch_one, full_out).astype(jnp.bfloat16)
    grad_q, grad_keys_all, grad_values_all = attend_back(
        query, keys_all, values_all, self_allowed, self_lse, grad_self_mix
    )
    back_kv = from_behind(
        (as_sent(grad_keys_all[:tok_dev]), as_sent(grad_values_all[:tok_dev])), "band", -1
    )
    grad_k = grad_keys_all[tok_dev:] + back_kv[0]
    grad_v = grad_values_all[tok_dev:] + back_kv[1]
    grad_q_low = grad_q.astype(jnp.bfloat16)
    grad_k_low = grad_k.astype(jnp.bfloat16)
    grad_v_low = grad_v.astype(jnp.bfloat16)
    grad_self_query = matmul_tn(attn_in, grad_q_low)
    grad_self_key = matmul_tn(attn_in, grad_k_low)
    grad_self_value = matmul_tn(attn_in, grad_v_low)
    grad_attn_in = (
        matmul_nt(grad_q_low, full_query)
        + matmul_nt(grad_k_low, full_key)
        + matmul_nt(grad_v_low, full_value)
    )
    grad_resid, grad_attn_gain, grad_attn_shift = norm_back(
        tokens, gain_attn.astype(jnp.float32), bias_attn.astype(jnp.float32), grad_attn_in
    )
    grad_tokens = grad_resid_one + grad_resid
    self_local = (
        grad_attn_gain,
        grad_attn_shift,
        grad_self_query,
        grad_self_key,
        grad_self_value,
        grad_self_out,
    )
    locals_ = self_local + cross_local + dense_local
    vecs = jnp.stack([locals_[i] for i in (0, 1, 6, 7, 12, 13)])
    width = vecs.shape[1] // count
    vecs = vecs.reshape(6, count, width).transpose(1, 0, 2)
    vecs = jnp.pad(vecs, ((0, 0), (0, 2), (0, 128 - width))).reshape(count * 8, 128)
    order = (2, 3, 4, 5, 8, 9, 10, 11, 14, 15)
    mats = [locals_[i].astype(jnp.bfloat16) for i in order]
    *sums, small = scatter_all(mats + [vecs], [(m.shape[0] // count, m.shape[1]) for m in mats] + [(8, 128)], count)
    summed = [None] * 16
    for i, s in zip(order, sums):
        summed[i] = s
    for j, i in enumerate((0, 1, 6, 7, 12, 13)):
        summed[i] = small[j, :width]
    summed = tuple(summed)
    return (block_out, grad_tokens, grad_prompt) + summed


class Moves:
    def __init__(self, pc, send, recv, k):
        self.pc, self.send, self.recv, self.k, self.n, self.sent = pc, send, recv, k, 0, []

    def slot(self):
        self.n += 1
        return self.n - 1

    def make(self, src, dst, dev, s, r):
        return pltpu.make_async_remote_copy(
            src_ref=src, dst_ref=dst, send_sem=self.send.at[self.k, s], recv_sem=self.recv.at[self.k, r],
            device_id=(dev,), device_id_type=MESH)

    def go(self, src, dst, dev):
        s = self.slot()
        d = self.make(src, dst, dev, s, s)
        d.start()
        self.sent.append((d, None))
        return d

    def go_if(self, cond, src, dst, dev, s, r):
        d = self.make(src, dst, dev, s, r)

        @pl.when(cond)
        def _():
            d.start()

        self.sent.append((d, cond))
        return d

    def drain(self):
        for d, cond in self.sent:
            if cond is None:
                d.wait_send()
            else:

                @pl.when(cond)
                def _(d=d):
                    d.wait_send()


class Line:
    def __init__(self, moves, view):
        self.m, self.view = moves, view
        self.slots = {o: moves.slot() for o in (1, 2, 3)}
        self.far = moves.slot()

    def start(self, src=None):
        m, pc, slots = self.m, self.m.pc, self.slots
        here = self.view(pc.z)
        src = here if src is None else src
        self.got = {
            1: m.go_if(pc.z != 3, src, here, pc.dev(dz=1), slots[1], slots[1]),
            2: m.make(src, here, pc.dev(dz=2), slots[2], slots[2]),
            3: m.go_if(pc.z != 0, src, here, pc.dev(dz=3), slots[3], slots[3]),
        }
        self.got[2].start()
        m.sent.append((self.got[2], None))

    def relay(self):
        m, pc = self.m, self.m.pc
        low, high = self.view(0), self.view(3)
        self.got[2].wait_recv()
        m.go_if(pc.z == 2, low, low, pc.dev(dz=1), self.far, self.slots[3])
        m.go_if(pc.z == 1, high, high, pc.dev(dz=3), self.far, self.slots[1])

    def finish(self):
        self.got[1].wait_recv()
        self.got[3].wait_recv()


class GatherZ(Moves):
    def __init__(self, pc, own, out, send, recv, loc, k):
        super().__init__(pc, send, recv, k)
        self.own, self.out, self.loc = own, out, loc

    def keep(self):
        pc = self.pc
        here = self.out(pc.z, pc.p, pc.q, pc.c)
        self.local = pltpu.make_async_copy(self.own, here, self.loc.at[self.k])
        self.local.start()
        return here

    def s0(self):
        pc = self.pc
        self.keep()
        self.line = Line(self, lambda z: self.out(z, pc.p, pc.q, pc.c))
        self.line.start(self.own)

    def s1(self):
        self.line.relay()

    def s2(self):
        pc = self.pc
        self.local.wait()
        self.line.finish()
        v = self.out(slice(None), pc.p, pc.q, pc.c)
        self.ps, self.qs = self.go(v, v, pc.dev(dp=1)), self.go(v, v, pc.dev(dq=1))

    def s3(self):
        pc = self.pc
        self.ps.wait_recv()
        v = self.out(pl.ds(0, 2), 1 - pc.p, pc.q, pc.c)
        self.rs = [self.go(v, v, pc.dev(dq=1))]
        self.qs.wait_recv()
        v = self.out(pl.ds(2, 2), pc.p, 1 - pc.q, pc.c)
        self.rs += [self.go(v, v, pc.dev(dp=1))]

    def s4(self):
        for d in self.rs:
            d.wait_recv()
        v = self.out(slice(None), slice(None), slice(None), self.pc.c)
        self.cs = self.go(v, v, self.pc.dev(dc=1))

    def s5(self):
        self.cs.wait_recv()


class GatherP(GatherZ):
    def s0(self):
        pc = self.pc
        here = self.keep()
        h = self.own.shape[0] // 2
        self.a, self.b = pl.ds(0, h), pl.ds(h, h)
        self.xs = [self.go(self.own.at[self.a], here.at[self.a], pc.dev(dp=1)), self.go(self.own.at[self.b], here.at[self.b], pc.dev(dq=1))]

    def s1(self):
        pc = self.pc
        self.local.wait()
        for d in self.xs:
            d.wait_recv()
        self.lines = [
            Line(self, lambda z: self.out(z, slice(None), pc.q, pc.c).at[:, self.a]),
            Line(self, lambda z: self.out(z, pc.p, slice(None), pc.c).at[:, self.b]),
        ]
        for line in self.lines:
            line.start()

    def s2(self):
        for line in self.lines:
            line.relay()

    def s3(self):
        pc = self.pc
        for line in self.lines:
            line.finish()
        va = self.out(slice(None), slice(None), pc.q, pc.c).at[:, :, self.a]
        vb = self.out(slice(None), pc.p, slice(None), pc.c).at[:, :, self.b]
        self.rs = [self.go(va, va, pc.dev(dq=1)), self.go(vb, vb, pc.dev(dp=1))]


def add_to(ref, *others):
    total = ref[...].astype(jnp.float32)
    for other in others:
        total += other[...].astype(jnp.float32)
    ref[...] = total.astype(ref.dtype)


class LineSum:
    def __init__(self, moves, block, came, joined):
        self.m, self.block, self.came, self.joined = moves, block, came, joined
        self.slots = {o: moves.slot() for o in (1, 2, 3)}
        self.far = moves.slot()
        self.outer = (moves.pc.z == 0) | (moves.pc.z == 3)

    def start(self):
        m, pc, slots = self.m, self.m.pc, self.slots
        first, last = pc.z == 0, pc.z == 3
        m.go_if(first, self.block(3), self.joined, pc.dev(dz=1), self.far, self.far)
        m.go_if(last, self.block(0), self.joined, pc.dev(dz=3), self.far, self.far)
        self.two = self.block((pc.z + 2) % 4)
        self.got = {
            1: m.go_if(pc.z != 3, self.block((pc.z + 1) % 4), self.came.at[0], pc.dev(dz=1), slots[1], slots[1]),
            2: m.go_if(self.outer, self.two, self.came.at[1], pc.dev(dz=2), slots[2], slots[2]),
            3: m.go_if(pc.z != 0, self.block((pc.z + 3) % 4), self.came.at[2], pc.dev(dz=3), slots[3], slots[3]),
        }

    def relay(self):
        m, pc = self.m, self.m.pc
        inner = (pc.z == 1) | (pc.z == 2)
        d = m.make(self.two, self.joined, pc.dev(dz=1), self.far, self.far)

        @pl.when(inner)
        def _():
            d.wait_recv()
            add_to(self.two, self.joined)

        m.go_if(inner, self.two, self.came.at[1], pc.dev(dz=2), self.slots[2], self.slots[2])

    def finish(self, use):
        pc = self.m.pc
        own = self.block(pc.z)
        self.got[2].wait_recv()

        @pl.when(pc.z == 0)
        def _():
            self.got[3].wait_recv()
            use(own, self.came.at[1], self.came.at[2])

        @pl.when(pc.z == 3)
        def _():
            self.got[1].wait_recv()
            use(own, self.came.at[0], self.came.at[1])

        @pl.when((pc.z == 1) | (pc.z == 2))
        def _():
            self.got[1].wait_recv()
            self.got[3].wait_recv()
            use(own, self.came.at[0], self.came.at[1], self.came.at[2])


class Sum(Moves):
    def __init__(self, pc, grad, put, r1, bufs, send, recv, k, credit=None, waits=False, gives=False):
        super().__init__(pc, send, recv, k)
        self.grad, self.put, self.r1, self.bufs = grad, put, r1, bufs
        self.credit, self.waits, self.gives = credit, waits, gives

    def others(self):
        pc = self.pc
        out = [(0, 0, pc.dev(dc=1)), (1, 1, pc.dev(dq=1)), (2, 2, pc.dev(dp=1))]
        return out + [(2 + 4 - o, 2 + o, pc.dev(dz=o)) for o in (1, 2, 3)]

    def s0(self):
        pc = self.pc
        if self.waits:
            for _, mine, _ in self.others():
                pl.semaphore_wait(self.credit.at[mine], 1)
        s = self.slot()
        self.d1 = self.make(self.grad(1 - pc.c), self.r1, pc.dev(dc=1), s, s)
        self.d1.start()

    def with_sibling(self):
        self.d1.wait()
        own = self.grad(self.pc.c)

        def body(i, _):
            at = i // 4, (i // 2) % 2, i % 2
            add_to(self.r1.at[at], own.at[at])
            return 0

        lax.fori_loop(0, 16, body, 0)

    def s6(self):
        self.drain()
        if self.gives:
            for theirs, _, dev in self.others():
                pl.semaphore_signal(self.credit.at[theirs], inc=1, device_id=(dev,), device_id_type=MESH)


class SumZ(Sum):
    @staticmethod
    def buffers(n, block):
        return [(n, 2, 2) + block, (n, 2, 2) + block, (n, 4) + block, (n, 3) + block, (n,) + block]

    def s1(self):
        pc = self.pc
        self.with_sibling()
        self.a, self.b, self.r3, self.r4, self.rx = self.bufs
        self.d2 = [
            self.go(self.r1.at[pl.ds(0, 2), :, 1 - pc.q], self.a, pc.dev(dq=1)),
            self.go(self.r1.at[pl.ds(2, 2), 1 - pc.p], self.b, pc.dev(dp=1)),
        ]

    def s2(self):
        pc = self.pc
        for d in self.d2:
            d.wait_recv()

        def body(i, _):
            h, e = i // 2, i % 2
            add_to(self.a.at[h, e], self.r1.at[h, e, pc.q])
            add_to(self.b.at[h, e], self.r1.at[2 + h, pc.p, e])
            return 0

        lax.fori_loop(0, 4, body, 0)
        self.d3 = [
            self.go(self.a.at[:, 1 - pc.p], self.r3.at[pl.ds(0, 2)], pc.dev(dp=1)),
            self.go(self.b.at[:, 1 - pc.q], self.r3.at[pl.ds(2, 2)], pc.dev(dq=1)),
        ]

    def s3(self):
        pc = self.pc
        for d in self.d3:
            d.wait_recv()

        def body(h, _):
            add_to(self.r3.at[h], self.a.at[h, pc.p])
            add_to(self.r3.at[2 + h], self.b.at[h, pc.q])
            return 0

        lax.fori_loop(0, 2, body, 0)
        self.line = LineSum(self, lambda z: self.r3.at[z], self.r4, self.rx)
        self.line.start()

    def s4(self):
        self.line.relay()

    def s5(self):
        here, end = self.put()

        def use(own, *came):
            total = own[...].astype(jnp.float32)
            for c in came:
                total += c[...].astype(jnp.float32)
            here[...] = total

        self.line.finish(use)
        if end is not None:
            end()


class SumP(Sum):
    @staticmethod
    def buffers(n, block):
        half = (block[0] // 2, block[1])
        pair = [(n, 4, 2) + half, (n, 3, 2) + half, (n, 2) + half, (n,) + half]
        return pair + pair

    def s1(self):
        pc = self.pc
        self.with_sibling()
        h = self.r1.shape[3] // 2
        self.half = pl.ds(0, h), pl.ds(h, h)
        self.sides = self.bufs[:4], self.bufs[4:]
        self.d2 = [
            self.go(self.r1.at[:, :, 1 - pc.q, self.half[0]], self.sides[0][0], pc.dev(dq=1)),
            self.go(self.r1.at[:, 1 - pc.p, :, self.half[1]], self.sides[1][0], pc.dev(dp=1)),
        ]

    def s2(self):
        pc = self.pc
        for d in self.d2:
            d.wait_recv()
        a, b = self.sides[0][0], self.sides[1][0]

        def body(i, _):
            z, e = i // 2, i % 2
            add_to(a.at[z, e], self.r1.at[z, e, pc.q, self.half[0]])
            add_to(b.at[z, e], self.r1.at[z, pc.p, e, self.half[1]])
            return 0

        lax.fori_loop(0, 8, body, 0)
        self.lines = [LineSum(self, lambda z, s=s: s[0].at[z], s[1], s[2]) for s in self.sides]
        for line in self.lines:
            line.start()

    def s3(self):
        for line in self.lines:
            line.relay()

    def s4(self):
        pc = self.pc
        for line in self.lines:
            line.finish(add_to)
        a, b = self.sides[0][0], self.sides[1][0]
        self.d3 = [
            self.go(a.at[pc.z, 1 - pc.p], self.sides[0][3], pc.dev(dp=1)),
            self.go(b.at[pc.z, 1 - pc.q], self.sides[1][3], pc.dev(dq=1)),
        ]

    def s5(self):
        pc = self.pc
        for d in self.d3:
            d.wait_recv()
        here, end = self.put()
        for s, mine, at in zip(self.sides, (pc.p, pc.q), self.half):
            here[at, :] = s[0][pc.z, mine].astype(jnp.float32) + s[3][...].astype(jnp.float32)
        end()


BF = jnp.bfloat16
F32 = jnp.float32
NN = (((1,), (0,)), ((), ()))
NT = (((1,), (1,)), ((), ()))
TN = (((0,), (0,)), ((), ()))
SCALE = 0.125 * 1.4426950408889634
FWD_NAMES = ("q", "k", "v", "o", "cq", "ck", "cv", "co", "di", "do")


def named(r, prefix):
    return [getattr(r, prefix + m) for m in FWD_NAMES]


def dot(left, right, form):
    return lax.dot_general(left, right, form, preferred_element_type=F32)


def tiles(total, step, body):
    if total == step:
        body(0)
    else:
        def one(i, _):
            body(pl.multiple_of(i * step, step))
            return 0

        lax.fori_loop(0, total // step, one, 0)


def product(left, right, form, put, step=512):
    wide = right.shape[0] if form is NT else right.shape[1]

    def one(off):
        part = right[pl.ds(off, step), :] if form is NT else right[:, pl.ds(off, step)]
        put(off, dot(left(), part, form))

    tiles(wide, step, one)


def store(ref):
    def put(off, value):
        ref[:, pl.ds(off, value.shape[1])] = value.astype(ref.dtype)

    return put


def norm_rows(src, dst, gains, i, step=64):
    def one(r):
        rows = pl.ds(r, step)
        value = src[rows, :].astype(F32)
        center = value - jnp.mean(value, axis=-1, keepdims=True)
        spread = jnp.mean(center * center, axis=-1, keepdims=True)
        unit = center * lax.rsqrt(spread + 1e-06)
        dst[rows, :] = (unit * gains[i : i + 1, :] + gains[i + 1 : i + 2, :]).astype(dst.dtype)

    tiles(src.shape[0], step, one)


def norm_back_rows(src, grad, base, dst, low, gains, i, sums, step=64):
    def one(r):
        rows = pl.ds(r, step)
        value = src[rows, :].astype(F32)
        center = value - jnp.mean(value, axis=-1, keepdims=True)
        spread = jnp.mean(center * center, axis=-1, keepdims=True)
        inverse = lax.rsqrt(spread + 1e-06)
        unit = center * inverse
        came = grad[rows, :]
        inner = came * gains[i : i + 1, :]
        back = (
            inner
            - jnp.mean(inner, axis=-1, keepdims=True)
            - unit * jnp.mean(inner * unit, axis=-1, keepdims=True)
        ) * inverse
        total = base[rows, :].astype(F32) + back
        dst[rows, :] = total
        if low is not None:
            low[rows, :] = total.astype(BF)
        sums[i] += jnp.sum((came * unit).reshape(step // 8, 8, -1), axis=0)
        sums[i + 1] += jnp.sum(came.reshape(step // 8, 8, -1), axis=0)

    tiles(src.shape[0], step, one)


def image_edges(ids, lens, rows_dev):
    me = lax.axis_index("band")
    first = rows_dev * me - rows_dev // 2

    def start_of(i):
        before = jnp.sum(jnp.where(ids[...] < i, 1.0, 0.0), axis=1, keepdims=True)
        return (before - first.astype(F32)) * float(ROW_TOK)

    def length_of(i):
        here = lax.broadcasted_iota(jnp.int32, lens.shape, 1) == i
        return jnp.sum(jnp.where(here, lens[...].astype(F32), 0.0), axis=1, keepdims=True)

    return start_of(me), start_of(me + 1), length_of(me), length_of(me + 1)


def make_masks(ids, lens, bias, cross_bias, rows_dev, text):
    low, high, own_len, next_len = image_edges(ids, lens, rows_dev)
    queries = bias.shape[1]
    halo = bias.shape[0] - queries
    step = 128

    def position(shape, axis, start):
        return (lax.broadcasted_iota(jnp.int32, shape, axis) + start).astype(F32)

    def one(r):
        shape = (step, queries)
        key, query = position(shape, 0, r), position(shape, 1, halo)
        least = jnp.where(query >= high, high, low)
        bias[pl.ds(r, step), :] = jnp.where((key <= query) & (key >= least), 0.0, -1e30)

    tiles(bias.shape[0], step, one)

    def two(r):
        shape = (step, queries)
        key, query = position(shape, 0, r), position(shape, 1, halo)
        later = query >= high
        least = jnp.where(later, float(text), 0.0)
        most = jnp.where(later, text + next_len, own_len)
        cross_bias[pl.ds(r, step), :] = jnp.where((key >= least) & (key < most), 0.0, -1e30)

    tiles(cross_bias.shape[0], step, two)


def mine_of(h, shape, axis):
    place = lax.broadcasted_iota(jnp.int32, shape, axis)
    return place < HEAD if h == 0 else place >= HEAD


def attend_pairs(q, k, v, bias, mix, lse, first, last, spans):
    def one(i, _):
        off = pl.multiple_of(i * 128, 128)
        lanes = pl.ds(off, 128)
        chains = [(span, h) for span in spans for h in range(2)]

        def scores(chain):
            (q0, qn, kw), h = chain
            qp = q[q0 : q0 + qn, lanes]
            return dot(k[:kw, lanes], jnp.where(mine_of(h, qp.shape, 1), qp, jnp.zeros_like(qp)), NT)

        coming = scores(chains[0])
        for e, ((q0, qn, kw), h) in enumerate(chains):
            s = coming * SCALE + bias[:kw, q0 : q0 + qn]
            if e + 1 < len(chains):
                coming = scores(chains[e + 1])
            vp = v[:kw, lanes]
            vm = jnp.where(mine_of(h, vp.shape, 1), vp, jnp.ones_like(vp))
            peak = jnp.max(s, axis=0, keepdims=True)
            p = jnp.exp2(s - peak).astype(BF)
            got = dot(vm, p, TN)
            total = got[HEAD * (1 - h) : HEAD * (1 - h) + 1]
            own = got[HEAD * h : HEAD * (h + 1)] * (1.0 / total)
            rows = pl.ds(pl.multiple_of(off + HEAD * h, HEAD), HEAD)
            mix[rows, q0 : q0 + qn] = own.astype(BF)
            lse[i, h : h + 1, q0 : q0 + qn] = peak + jnp.log2(total)
        return 0

    lax.fori_loop(first, last, one, 0)


def attend_back_pairs(q, k, v, bias, mix, grad_mix, lse, dq, acc, put, first, last, spans):
    dk, dv = acc.at[0], acc.at[1]

    def one(i, _):
        off = pl.multiple_of(i * 128, 128)
        lanes = pl.ds(off, 128)
        acc[...] = jnp.zeros_like(acc)
        chains = [(span, h) for span in spans for h in range(2)]

        def begin(chain):
            (q0, qn, kw), h = chain
            cols = slice(q0, q0 + qn)
            qp, go = q[cols, lanes], grad_mix[lanes, cols]
            qm = jnp.where(mine_of(h, qp.shape, 1), qp, jnp.zeros_like(qp))
            gm = jnp.where(mine_of(h, go.shape, 0), go, jnp.zeros_like(go))
            return qm, gm, dot(k[:kw, lanes], qm, NT), dot(v[:kw, lanes], gm, NN)

        coming = begin(chains[0])
        for e, ((q0, qn, kw), h) in enumerate(chains):
            cols = slice(q0, q0 + qn)
            qm, gm, s, dp = coming
            if e + 1 < len(chains):
                coming = begin(chains[e + 1])
            kp = k[:kw, lanes]
            km = jnp.where(mine_of(h, kp.shape, 1), kp, jnp.zeros_like(kp))
            inner = jnp.sum(gm.astype(F32) * mix[lanes, cols].astype(F32), axis=0, keepdims=True)
            p = jnp.exp2(s * SCALE + bias[:kw, cols] - lse[i, h : h + 1, cols])
            ds = (p * (dp - inner)).astype(BF)
            dv[:kw, :] += dot(p.astype(BF), gm, NT)
            dk[:kw, :] += dot(ds, qm, NN)
            part = dot(km, ds, TN)
            dqt = part if h == 0 else dqt + part
            if h == 1:
                dq[cols, lanes] = jnp.transpose(dqt * 0.125).astype(BF)
        put(lanes, dk, dv)
        return 0

    lax.fori_loop(first, last, one, 0)


class Copies:
    def __init__(self, sem):
        self.sem, self.used = sem, 0

    def start(self, src, dst):
        d = pltpu.make_async_copy(src, dst, self.sem.at[self.used])
        self.used += 1
        assert self.used <= self.sem.shape[0]
        d.start()
        return d


class Weights:
    def __init__(self, copies, slots, entries):
        self.copies, self.slots, self.entries = copies, slots, entries
        self.begun, self.used, self.live = 0, 0, {}

    def pump(self, done):
        while (
            self.begun < len(self.entries)
            and self.begun < self.used + self.slots.shape[0]
            and self.entries[self.begun][1] <= done
        ):
            src = self.entries[self.begun][0]
            self.live[self.begun] = self.copies.start(src, self.slots.at[self.begun % self.slots.shape[0]])
            self.begun += 1

    def take(self):
        e = self.used
        assert e < self.begun
        self.live[e].wait()
        return self.slots.at[e % self.slots.shape[0]]

    def free(self):
        self.used += 1


def ring_neighbors(count):
    me = lax.axis_index("band")
    return (me + 1) % count, (me + count - 1) % count


def enter(pc, count):
    sem = pltpu.get_barrier_semaphore()
    who = pc.partners() + list(ring_neighbors(count))
    for d in who:
        pl.semaphore_signal(sem, inc=1, device_id=(d,), device_id_type=MESH)
    pl.semaphore_wait(sem, len(who))


def layer_kernel(count, names, slots, early_us, late_us, *refs):
    r = types.SimpleNamespace(**dict(zip(names, refs)))
    pc = Place(count)
    Z, Pn, Qn = pc.Z, pc.P, pc.Q
    tok = r.tokens.shape[0]
    halo = tok // 2
    text = r.prompt.shape[0]
    copies = Copies(r.lsem)
    load = copies.start
    half = HEADS // 2
    q, k, v = r.gdo.at[pl.ds(0, tok)], r.gdo.at[pl.ds(tok, tok + halo)], r.gdo.at[pl.ds(2 * tok + halo, tok + halo)]
    first = 3 * tok + 2 * halo
    cq, cin = r.gdo.at[pl.ds(first, tok)], r.gdo.at[pl.ds(first + tok, tok)]
    pk, pv = r.gdo.at[pl.ds(first + 2 * tok, 2 * text)], r.gdo.at[pl.ds(first + 2 * tok + 2 * text, 2 * text)]
    pool = r.grads.reshape(r.grads.shape[0] * 1024, 1024)
    tokh, ainh = pool.at[pl.ds(0, tok + halo)], pool.at[pl.ds(tok + halo, tok + halo)]
    gx, tmp = r.ga.at[pl.ds(0, tok)], r.ga.at[pl.ds(tok, tok)]
    dkv = r.ga.at[pl.ds(2 * tok, 2 * tok)].reshape(2, tok, 1024)
    hid = r.bias.at[pl.ds(0, tok)]
    enter(pc, count)

    def remote(src, dst, i, dev):
        d = pltpu.make_async_remote_copy(
            src_ref=src, dst_ref=dst, send_sem=r.xsend.at[i], recv_sem=r.xrecv.at[i],
            device_id=(dev,), device_id_type=MESH)
        d.start()
        return d

    after, before = ring_neighbors(count)
    edge = [
        remote(r.tokens.at[pl.ds(tok - halo, halo)], tokh.at[pl.ds(0, halo)], 0, after),
        remote(r.prompt, r.pr.at[pl.ds(text, text)], 1, before),
    ]
    loads = types.SimpleNamespace(
        tok=copies.start(r.tokens, tokh.at[pl.ds(halo, tok)]),
        pr=copies.start(r.prompt, r.pr.at[pl.ds(0, text)]),
        gout=copies.start(r.gout, r.go),
    )

    shards = named(r, "s_") + [r.s_gains]
    wholes = named(r, "w_") + [r.gg]
    rows = shards[0].shape[0]
    order = [(10, 0, shards[10].shape[0], 0, 128)] + [(a, 0, rows, 0, 1024) for a in range(8)]
    order += [(9, rows * i, rows, 0, 1024) for i in range(shards[9].shape[0] // rows)]
    order += [(8, 0, rows, 1024 * j, 1024) for j in range(shards[8].shape[1] // 1024)]
    parts = shards[9].shape[0] // rows
    at = {n: 1 + a for a, n in enumerate(FWD_NAMES[:8])}
    at["do"], at["di"] = 8 + parts, 9 + parts
    gs = []
    for g, (a, r0, rn, c0, cn) in enumerate(order):
        own = shards[a].at[pl.ds(r0, rn), pl.ds(c0, cn)]
        view = wholes[a] if a == 10 else wholes[a].reshape((Z, Pn, Qn, 2) + shards[a].shape)

        def out(z, p, q, c, view=view, r0=r0, rn=rn, c0=c0, cn=cn):
            return view.at[z, p, q, c, pl.ds(r0, rn), pl.ds(c0, cn)]

        gs.append((GatherP if g % 2 else GatherZ)(pc, own, out, r.send, r.recv, r.loc, g))
    n = len(gs)

    def gather_tick(t):
        for stage in range(6):
            g = t - stage
            if 0 <= g < n:
                getattr(gs[g], f"s{stage}")()

    ff = [(r.w_do.at[pl.ds(1024 * j, 1024)], at["do"]) for j in range(parts)]
    entries = [(w, 1 + a) for a, w in enumerate(wholes[:8])] + ff
    entries += [(r.w_di.at[:, pl.ds(1024 * j, 1024)], at["di"] + j) for j in range(parts)]
    after_all = n - 1
    entries += [(r.w_di.at[:, pl.ds(1024 * j, 1024)], after_all) for j in range(parts)] + ff
    entries += [(wholes[a], after_all) for a in (7, 4, 3, 5, 6, 0, 1, 2)]
    weights = Weights(copies, r.ring, entries)
    latest = [-1]
    saves, kept = [], []

    def save(dst, src):
        kept.append(copies.start(src, dst))

    spans = [(0, tok // 2, tok), (tok // 2, tok // 2, tok + halo)]
    cross_spans = [(0, tok, 2 * text)]

    def t_masks():
        make_masks(r.ids, r.lens, r.bias, r.cbias, tok // ROW_TOK, text)

    def t_norm():
        width = 1024 // count
        per = 128 // width
        for g in range(8):
            total = jnp.zeros((8, 128), F32)
            for d in range(g * per, (g + 1) * per):
                c, qq, pp, zz = d % 2, (d // 2) % Qn, (d // (2 * Qn)) % Pn, d // (2 * Qn * Pn)
                total += r.gg[zz, pp, qq, c].astype(F32)
            r.gf[:, 128 * g : 128 * (g + 1)] = total
        loads.tok.wait()
        edge[0].wait_recv()
        norm_rows(tokh, ainh, r.gf, 0)
        save(r.o_ain, ainh.at[pl.ds(halo, tok)])

    def t_project(dst, src, lo, out):
        def go():
            w = weights.take()
            product(lambda: src[lo:, :], w, NN, store(dst))
            weights.free()
            save(out, dst)
        return go

    def t_self(a, b):
        def go():
            attend_pairs(q, k, v, r.bias, r.mix, r.lse, a, b, spans)
            if b == HEADS // 2:
                save(r.o_mix, r.mix)
        return go

    def t_out_self():
        w = weights.take()

        def put(off, value):
            cols = pl.ds(off, value.shape[1])
            r.res1[:, cols] = tokh[halo:, cols].astype(F32) + value

        product(lambda: r.mix[...], w, TN, put)
        weights.free()
        norm_rows(r.res1, cin, r.gf, 2)
        save(r.o_cin, cin)

    def t_prompt():
        loads.pr.wait()
        edge[1].wait_recv()

    def t_cross(a, b):
        def go():
            if a == 0:
                flush()
            attend_pairs(cq, pk, pv, r.cbias, r.mix, r.clse, a, b, cross_spans)
        return go

    def t_cross_out():
        w = weights.take()

        def put(off, value):
            cols = pl.ds(off, value.shape[1])
            r.res2[:, cols] = r.res1[:, cols] + value

        product(lambda: r.mix[...], w, TN, put)
        weights.free()
        norm_rows(r.res2, r.dx, r.gf, 4)

    def t_grad_act(j):
        def go():
            if j == 0:
                loads.gout.wait()
            w = weights.take()
            product(lambda: r.go[...], w, NT, store(r.ga.at[pl.ds(j * tok, tok)]))
            weights.free()
        return go

    def t_hidden(j):
        def go():
            w = weights.take()
            def side(off):
                cols = pl.ds(off, 512)
                hid[...] = dot(r.dx[...], w[:, cols], NN)

                def one(a):
                    here, there = pl.ds(a, 32), pl.ds(j * tok + a, 32)
                    value = hid[here, :]
                    share = 0.5 + 0.5 * lax.erf(value * 0.7071067811865476)
                    slope = share + value * (jnp.exp(value * value * -0.5) * 0.3989422804014327)
                    r.act[there, cols] = (value * share).astype(BF)
                    r.gh[there, cols] = (r.ga[there, cols] * slope).astype(BF)

                tiles(tok, 32, one)

            tiles(1024, 512, side)
            weights.free()
        return go

    a2, g2 = r.act, r.gh
    L = types.SimpleNamespace(pr=loads.pr)
    blk = r.r1.shape[4]
    chunks = []
    cuts = (1, 2)
    nring = 6 + 2 * parts + sum(cuts)
    zbufs = [getattr(r, "z%d" % i) for i in range(5)]
    pbufs = [getattr(r, "p%d" % i) for i in range(8)]
    sum_slots = r.grads

    def chunk(grad, put, wide=1024):
        g = len(chunks)
        chunks.append(None)
        slot = g % slots

        def part(ref, s):
            return ref.at[(s,) + (slice(None),) * (len(ref.shape) - 2) + (pl.ds(0, wide),)]

        kind, bufs = (SumP, pbufs) if g % 2 else (SumZ, zbufs)
        r1 = part(r.r1, slot)
        chunks[g] = kind(pc, grad, put, r1, [part(x, slot // 2) for x in bufs], r.send2, r.recv2, g, r.credit, g >= slots, g + slots < nring)
        return g

    def block_view(ref, rows):
        return ref.reshape(Z, Pn, Qn, 2, rows, 1024)

    turns, staged = [0], {}

    def putter(out, first, c0=0, wide=1024):
        def begin():
            spot = turns[0] % r.stage.shape[0]
            turns[0] += 1
            if spot in staged:
                staged.pop(spot).wait()
            here = r.stage.at[spot, :, pl.ds(0, wide)]

            def end():
                staged[spot] = load(here, out.at[pl.ds(first, blk), pl.ds(c0, wide)])

            return here, end

        return begin

    ready, active, summed = [], [], set()
    holder = [[] for _ in range(sum_slots.shape[0])]
    turn = [0]

    extra = []

    def item_of(g):
        return extra[0] if g == nring else chunks[g]

    def sum_tick():
        for item in sorted(active, key=lambda x: x[0] % 6):
            stage, g = item
            getattr(item_of(g), f"s{stage}")()
            if stage == 1:
                summed.add(g)
            item[0] += 1
        active[:] = [x for x in active if x[0] <= 6]
        if ready:
            g = ready.pop(0)
            item_of(g).s0()
            active.append([1, g])

    clock = [0]

    def tick():
        if clock[0] < n + 5:
            gather_tick(clock[0])
            latest[0] = clock[0] - 5
            clock[0] += 1
            weights.pump(latest[0])
        sum_tick()

    def until(gs):
        while not all(g in summed for g in gs):
            tick()

    def grad_chunk(first, form, left, right, cut=1, out=None, c0=0):
        s = turn[0] % len(holder)
        turn[0] += 1
        until(holder[s])
        ref = sum_slots.at[s]
        view = block_view(ref, blk)
        wide = 1024 // cut
        holder[s] = []
        for i in range(cut):
            cols = pl.ds(wide * i, wide)
            product(left, right.at[:, cols], form, store(ref.at[:, cols]))
            g = chunk(lambda c, cols=cols: view.at[:, :, :, c, :, cols], putter(r.o_eight if out is None else out, first, c0 + wide * i, wide), wide)
            holder[s].append(g)
            ready.append(g)

    X = {}
    r.sums[...] = jnp.zeros_like(r.sums)

    def t_din(j):
        def go():
            if j == 0:
                flush()
            grad_chunk(0, TN, lambda: r.dx[...], g2.at[pl.ds(j * tok, tok)], 1, r.o_di, 1024 * j)
        return go

    dense = []

    def t_dout(j):
        def go():
            if j == 0:
                flush()
            here = r.gdo.at[pl.ds(1024 * j, 1024)]
            product(lambda: a2[pl.ds(j * tok, tok), :], r.go, TN, store(here))
            if j == parts - 1:
                view = block_view(r.gdo, blk * parts)
                for i in range(parts):
                    rows = pl.ds(blk * i, blk)
                    g = chunk(lambda c, rows=rows: view.at[:, :, :, c, rows], putter(r.o_do, blk * i))
                    dense.append(g)
                    ready.append(g)
        return go

    def area(first, n):
        whole = a2 if first < parts * tok else g2
        return whole.at[pl.ds(first % (parts * tok), n)]

    top = parts * tok
    bcq, bpk, bpv, dq = area(0, tok), area(tok, 2 * text), area(tok + 2 * text, 2 * text), area(2 * tok, tok)
    bcin, b2 = area(3 * tok, tok), area(top, tok)
    bq, bk, bv, sq = area(0, tok), area(top + tok, tok + halo), area(top + 2 * tok + halo, tok + halo), area(tok, tok)
    b1, ain = area(2 * tok, tok), area(3 * tok, tok)
    klow, vlow = area(2 * tok, tok), area(top, tok)

    def flush():
        while kept:
            kept.pop().wait()

    def t_gdx(j):
        def go():
            w = weights.take()
            mine = pl.ds(j * tok, tok)

            def put(off, value):
                cols = pl.ds(off, value.shape[1])
                if j == 0:
                    tmp[:, cols] = value
                else:
                    tmp[:, cols] += value

            product(lambda: g2[mine, :], w, NT, put)
            weights.free()
            weights.pump(latest[0])
        return go

    def t_out(j):
        def go():
            w = weights.take()
            mine = pl.ds(j * tok, tok)

            def put(off, value):
                cols = pl.ds(off, value.shape[1])
                total = (r.res2 if j == 0 else gx)[:, cols] + value
                if j < parts - 1:
                    gx[:, cols] = total
                else:
                    r.dx[:, cols] = total.astype(BF)

            product(lambda: a2[mine, :], w, NN, put)
            weights.free()
            weights.pump(latest[0])
            if j == parts - 1:
                X["o"] = copies.start(r.dx, r.o_out)
        return go

    def t_norm2():
        L.cq = load(r.o_cq, bcq)
        L.pk = load(r.o_pk, bpk)
        L.pv = load(r.o_pv, bpv)
        L.cin = load(r.o_cin, bcin)
        norm_back_rows(r.res2, tmp, r.go, gx, b2, r.gf, 4, r.sums)

    def t_gco():
        grad_chunk(blk * 7, NN, lambda: r.mix[...], b2)

    def t_gcm():
        w = weights.take()
        product(lambda: w[...], b2, NT, store(r.gmt), tok // 2)
        weights.free()
        weights.pump(latest[0])

    def cross_put(lanes, dk, dv):
        for i, (d, s) in enumerate(((dk, 0.125), (dv, 1.0))):
            r.pkv[i, :, lanes] = d[:text, :] * s
            r.psend[i, :, lanes] = (d[text:, :] * s).astype(BF)

    def b_cross(a, b):
        def go():
            if a == 0:
                for d in (L.cq, L.pk, L.pv):
                    d.wait()
            attend_back_pairs(bcq, bpk, bpv, r.cbias, r.mix, r.gmt, r.clse, dq, r.kv.at[:, pl.ds(0, 2 * text)], cross_put, a, b, cross_spans)
            if b == half:
                X["p"] = remote(r.psend, r.precv, 2, after)
                L.mix = load(r.o_mix, r.mix)
        return go

    def t_gcq():
        L.cin.wait()
        grad_chunk(blk * 4, TN, lambda: bcin[...], dq)

    def t_norm1():
        w = weights.take()
        product(lambda: dq[...], w, NT, store(tmp))
        weights.free()
        weights.pump(latest[0])
        norm_back_rows(r.res1, tmp, gx, gx, b1, r.gf, 2, r.sums)
        L.q, L.k, L.v = load(r.o_q, bq), load(r.o_k, bk), load(r.o_v, bv)

    def t_go():
        L.mix.wait()
        grad_chunk(blk * 3, NN, lambda: r.mix[...], b1)

    def t_gm():
        w = weights.take()
        product(lambda: w[...], b1, NT, store(r.gmt), tok // 2)
        weights.free()
        weights.pump(latest[0])

    hsend = r.gdo.at[pl.ds(0, 2 * halo)].reshape(2, halo, 1024)

    def self_put(lanes, dk, dv):
        for i, (d, s) in enumerate(((dk, 0.125), (dv, 1.0))):
            hsend[i, :, lanes] = (d[:halo, :] * s).astype(BF)
            dkv[i, :, lanes] = d[halo:, :] * s

    def b_self(a, b):
        def go():
            if a == 0:
                until(dense)
                for d in (L.q, L.k, L.v):
                    d.wait()
            attend_back_pairs(bq, bk, bv, r.bias, r.mix, r.gmt, r.lse, sq, r.kv, self_put, a, b, spans)
            if b == half:
                X["h"] = remote(hsend, r.hrecv, 3, before)
                L.ain = load(r.o_ain, ain)
                X.pop("o").wait()
                L.tokens = load(r.tokens, r.dx)
        return go

    gp = r.res2.at[pl.ds(0, text)]

    def b_prompt():
        X["p"].wait_recv()
        for i in range(2):
            r.plow[i] = (r.pkv[i] + r.precv[i].astype(F32)).astype(BF)

    def t_gp(i):
        def go():
            if i == 0:
                b_prompt()
            low = r.plow.at[i]
            grad_chunk(blk * (5 + i), TN, lambda: r.pr[:text, :], low)
            w = weights.take()

            def put(off, value):
                cols = pl.ds(off, value.shape[1])
                if i == 0:
                    gp[:, cols] = value
                else:
                    gp[:, cols] += value

            product(lambda: low[...], w, NT, put)
            weights.free()
            weights.pump(latest[0])
            if i == 1:
                saves.append(copies.start(gp, r.o_gp))
        return go

    def t_gq():
        L.ain.wait()
        grad_chunk(blk * 0, TN, lambda: ain[...], sq)

    def lower(i):
        low = (klow, vlow)[i]
        low[pl.ds(0, halo), :] = dkv[i, :halo, :].astype(BF)
        low[pl.ds(halo, halo), :] = (dkv[i, halo:, :] + r.hrecv[i].astype(F32)).astype(BF)

    def t_low_v():
        lower(1)

    def t_gkv(i):
        def go():
            low = (klow, vlow)[i]
            if i == 0:
                X["h"].wait_recv()
                lower(0)
            grad_chunk(blk * (1 + i), TN, lambda: ain[...], low, cuts[i])
        return go

    def t_gain(i):
        def go():
            w = weights.take()

            def put(off, value):
                cols = pl.ds(off, value.shape[1])
                if i == 0:
                    tmp[:, cols] = value
                else:
                    tmp[:, cols] += value

            product(lambda: (sq, klow, vlow)[i][...], w, NT, put)
            weights.free()
            weights.pump(latest[0])
        return go

    def t_norm0():
        L.tokens.wait()
        norm_back_rows(r.dx, tmp, gx, gx, None, r.gf, 0, r.sums)
        saves.append(copies.start(gx, r.o_gt))

    def t_vecs():
        width = 1024 // count
        per = 128 // width
        for g in range(8):
            lanes = slice(128 * g, 128 * (g + 1))
            tile = jnp.concatenate(
                [jnp.sum(r.sums[i, :, lanes], axis=0, keepdims=True) for i in range(6)] + [jnp.zeros((2, 128), F32)], axis=0)
            for d in range(g * per, (g + 1) * per):
                c, qq, pp, zz = d % 2, (d // 2) % Qn, (d // (2 * Qn)) % Pn, d // (2 * Qn * Pn)
                r.vg[zz, pp, qq, c] = tile

        bufs = [getattr(r, "v%d" % i) for i in range(6)]
        extra.append(SumZ(pc, lambda c: r.vg.at[:, :, :, c], lambda: (r.g_vec, None), bufs[0], bufs[1:], r.send2, r.recv2, nring))
        ready.append(nring)

    fore = [(-1, 2, t_masks), (0, 6, t_norm), (at["q"], 2.5, t_project(q, ainh, halo, r.o_q)),
            (at["k"], 4, t_project(k, ainh, 0, r.o_k)), (at["v"], 4, t_project(v, ainh, 0, r.o_v))]
    fore += [(at["v"], 3.5, t_self(a, a + 2)) for a in range(0, half, 2)]
    fore += [(at["o"], 3, t_out_self), (at["cq"], 1.5, t_project(cq, cin, 0, r.o_cq)), (-1, 0, t_prompt),
             (at["ck"], 1, t_project(pk, r.pr, 0, r.o_pk)), (at["cv"], 1, t_project(pv, r.pr, 0, r.o_pv)),
             (at["cv"], 4, t_cross(0, 4)), (at["cv"], 4, t_cross(4, 8)), (at["co"], 4, t_cross_out)]
    fore += [(at["do"], 1.5, t_grad_act(j)) for j in range(parts)]
    for j in range(parts):
        fore += [(at["di"] + j, 3.5, t_hidden(j)), (at["di"] + j, 1.5, t_din(j))]
    back = [(1.5, t_dout(j)) for j in range(parts)]
    back += [(1.5, t_gdx(j)) for j in range(parts)] + [(1.5, t_out(j)) for j in range(parts)]
    back += [(3, t_norm2), (1.5, t_gco), (1.5, t_gcm), (2, t_masks), (4, b_cross(0, 4)), (4, b_cross(4, 8))]
    back += [(1.5, t_gcq), (4, t_norm1), (1.5, t_go), (1.5, t_gm)]
    back += [(5, b_self(a, a + 2)) for a in range(0, half, 2)]
    back += [(1, t_gp(0)), (1, t_gp(1)), (1.5, t_gq), (2, t_gkv(0)), (0.3, t_low_v)]
    back += [(1.5, t_gain(i)) for i in range(3)] + [(3, t_norm0), (0.3, t_vecs), (2, t_gkv(1))]
    while clock[0] < n + 5:
        tick()
        spent = 0
        while fore and fore[0][0] <= max(latest[0], -1) and spent < early_us:
            _, cost, go = fore.pop(0)
            go()
            spent += cost
            weights.pump(latest[0])
    for _, _, go in fore:
        go()
        weights.pump(latest[0])
        tick()
    spent = 0
    for cost, go in back:
        go()
        weights.pump(latest[0])
        spent += cost
        if spent >= late_us and (ready or active):
            tick()
            spent = 0
    while ready or active:
        tick()
    flush()
    for d in staged.values():
        d.wait()
    for g in gs:
        g.drain()
    for d in edge + list(X.values()):
        d.wait_send()
    for d in saves:
        d.wait()


def layer(args, gains, ids, lens, count):
    tokens, prompt, gout, mats = args
    tok, text = tokens.shape[0], prompt.shape[0]
    halo = tok // 2
    dims = dims_of(count)
    blk = mats[0].shape[0]
    parts = mats[9].shape[0] // blk
    moved = 9 + 2 * parts
    slots = 6
    block = (blk, 1024)
    small = dict(s_gains=gains, tokens=tokens, prompt=prompt, gout=gout, ids=ids, lens=lens)
    names = ["s_" + m for m in FWD_NAMES] + list(small)
    outs = {"w_" + m: (w.shape[0] * count, w.shape[1], BF) for m, w in zip(FWD_NAMES, mats)}
    outs |= dict(
        o_ain=(tok, 1024, BF), o_q=(tok, 1024, BF), o_k=(tok + halo, 1024, BF), o_v=(tok + halo, 1024, BF), o_mix=(1024, tok, BF),
        o_cin=(tok, 1024, BF), o_cq=(tok, 1024, BF), o_pk=(2 * text, 1024, BF), o_pv=(2 * text, 1024, BF),
        o_out=(tok, 1024, BF), o_gt=(tok, 1024, F32), o_gp=(text, 1024, F32), o_eight=(8 * blk, 1024, F32), o_di=mats[8].shape + (F32,),
        o_do=mats[9].shape + (F32,))
    vouts = dict(g_vec=(8, 128, F32))
    scratch = {"z%d" % i: s + (BF,) for i, s in enumerate(SumZ.buffers(slots // 2, block))}
    scratch |= {"p%d" % i: s + (BF,) for i, s in enumerate(SumP.buffers(slots // 2, block))}
    scratch |= {"v%d" % i: s + (F32,) for i, s in enumerate([dims[:3] + (8, 128)] + [s[1:] for s in SumZ.buffers(1, (8, 128))])}
    scratch |= dict(
        r1=(slots,) + dims[:3] + block + (BF,), stage=(4,) + block + (F32,), grads=(2, 1024, 1024, BF), gdo=(1024 * parts, 1024, BF),
        act=(parts * tok, 1024, BF), gh=(parts * tok, 1024, BF), ga=(parts * tok, 1024, F32), ring=(2, 1024, 1024, BF),
        res1=(tok, 1024, F32), res2=(tok, 1024, F32), dx=(tok, 1024, BF), go=(tok, 1024, BF), pr=(2 * text, 1024, BF),
        mix=(1024, tok, BF), gmt=(1024, tok, BF), bias=(tok + halo, tok, F32), cbias=(2 * text, tok, F32), kv=(2, tok + halo, 128, F32),
        gf=(8, 1024, F32), gg=dims + (8, 128, BF), lse=(HEADS // 2, 2, tok, F32), clse=(HEADS // 2, 2, tok, F32),
        hrecv=(2, halo, 1024, BF), psend=(2, text, 1024, BF), precv=(2, text, 1024, BF), pkv=(2, text, 1024, F32),
        plow=(2, text, 1024, BF), sums=(6, 8, 1024, F32), vg=dims + (8, 128, F32))
    sems = dict(
        send=(moved, 16), recv=(moved, 16), send2=(moved + 6, 16), recv2=(moved + 6, 16), loc=(moved,), xsend=(4,), xrecv=(4,), lsem=(112,))
    every = names + list(outs) + list(vouts) + list(scratch) + list(sems) + ["credit"]
    got = pl.pallas_call(
        functools.partial(layer_kernel, count, every, slots, 6, 7),
        out_shape=[jax.ShapeDtypeStruct(s[:-1], s[-1]) for s in (outs | vouts).values()],
        in_specs=[pl.BlockSpec(memory_space=pl.ANY)] * 14 + [pl.BlockSpec(memory_space=pltpu.VMEM)] * 2,
        out_specs=[pl.BlockSpec(memory_space=pl.ANY)] * len(outs) + [pl.BlockSpec(memory_space=pltpu.VMEM)] * len(vouts),
        scratch_shapes=[pltpu.VMEM(s[:-1], s[-1]) for s in scratch.values()]
        + [pltpu.SemaphoreType.DMA(s) for s in sems.values()] + [pltpu.SemaphoreType.REGULAR((6,))],
        compiler_params=pltpu.CompilerParams(collective_id=0, has_side_effects=True, vmem_limit_bytes=63 << 20),
        name="layer",
    )(*mats, *small.values())
    return got[-7:]


def on_device(
    tokens_in,
    prompt_states,
    image_ids,
    text_lengths,
    attn_gain,
    attn_shift,
    self_query,
    self_key,
    self_value,
    self_out,
    cross_gain,
    cross_shift,
    cross_query,
    cross_key,
    cross_value,
    cross_out,
    dense_gain,
    dense_shift,
    dense_in,
    dense_out,
    out_grad,
):
    mats = (self_query, self_key, self_value, self_out, cross_query, cross_key, cross_value, cross_out, dense_in, dense_out)
    count = lax.axis_size("band")
    blk = mats[0].shape[0]
    if dims_of(count) != (4, 2, 2, 2) or blk % 32:
        return on_device_wide(
            tokens_in,
            prompt_states,
            image_ids,
            text_lengths,
            attn_gain,
            attn_shift,
            self_query,
            self_key,
            self_value,
            self_out,
            cross_gain,
            cross_shift,
            cross_query,
            cross_key,
            cross_value,
            cross_out,
            dense_gain,
            dense_shift,
            dense_in,
            dense_out,
            out_grad,
        )
    width = attn_gain.shape[0]
    per = 128 // width
    place = lax.axis_index("band") % per
    packed = jnp.stack((attn_gain, attn_shift, cross_gain, cross_shift, dense_gain, dense_shift))
    packed = jnp.pad(jnp.tile(packed, (1, per)), ((0, 2), (0, 0)))
    packed = jnp.where(jnp.arange(128, dtype=jnp.int32)[None] // width == place, packed, jnp.zeros_like(packed))
    ids, lens = image_ids[None], text_lengths[None]
    data = (tokens_in, prompt_states[0], out_grad, mats)
    block_out, grad_tokens, grad_prompt, eight, wide, tall, vecs = layer(data, packed, ids, lens, count)
    vecs = lax.dynamic_slice(vecs, (0, place * width), (8, width))
    g = [eight[blk * i : blk * (i + 1)] for i in range(8)]
    return (
        block_out, grad_tokens, grad_prompt[None],
        vecs[0], vecs[1], *g[:4],
        vecs[2], vecs[3], *g[4:],
        vecs[4], vecs[5], wide, tall,
    )


def solution(mesh):
    return jax.shard_map(
        on_device,
        mesh=mesh,
        in_specs=(
            P("band", None),
            P("band", None, None),
            P(),
            P(),
            P("band"),
            P("band"),
            P("band", None),
            P("band", None),
            P("band", None),
            P("band", None),
            P("band"),
            P("band"),
            P("band", None),
            P("band", None),
            P("band", None),
            P("band", None),
            P("band"),
            P("band"),
            P("band", None),
            P("band", None),
            P("band", None),
        ),
        out_specs=(
            P("band", None),
            P("band", None),
            P("band", None, None),
            P("band"),
            P("band"),
            P("band", None),
            P("band", None),
            P("band", None),
            P("band", None),
            P("band"),
            P("band"),
            P("band", None),
            P("band", None),
            P("band", None),
            P("band", None),
            P("band"),
            P("band"),
            P("band", None),
            P("band", None),
        ),
        check_vma=False,
    )
```
